32 devices in a mesh: rep: 8 (over z, core), fsdp: 4 (over y, x).
Axes of the slice: x: 2, y: 2, z: 4, core: 2. Of those that a mesh axis runs over, the one named last changes fastest.
Arguments:
- tokens: bfloat16 [8192, 1536], P(('rep', 'fsdp')), may hold values from -6 to 6
- segment_ids: int32 [32, 256], P(('rep', 'fsdp')), may hold values from 0 to 3, never falling along the last dimension, each value on 1 to 128 neighbouring positions
- cotangent: bfloat16 [8192, 1536], P(('rep', 'fsdp')), may hold values from -6 to 6
- norm_gain: bfloat16 [1536], P('fsdp'), may hold values from 0.5 to 1.5
- in_weight: bfloat16 [1536, 6448], P('fsdp'), may hold values from -0.15625 to 0.15625
- conv_weight: bfloat16 [4, 3328], P(None, 'fsdp'), may hold values from -3 to 3
- conv_bias: bfloat16 [3328], P('fsdp'), may hold values from -0.5 to 0.5
- step_bias: bfloat16 [48], replicated, may hold values from -6 to -2
- rate_log: bfloat16 [48], replicated, may hold values from 0 to 2.5
- skip_gain: bfloat16 [48], replicated, may hold values from 0.5 to 2
- gate_gain: bfloat16 [3072], P('fsdp'), may hold values from 0.5 to 1.5
- out_weight: bfloat16 [3072, 1536], P('fsdp'), may hold values from -0.109375 to 0.109375
Outputs:
- output: bfloat16 [8192, 1536], P(('rep', 'fsdp'))
- tokens_grad: bfloat16 [8192, 1536], P(('rep', 'fsdp'))
- grad_norm: float32 [1536], P('fsdp')
- grad_inproj: float32 [1536, 6448], P('fsdp')
- grad_kernel: float32 [4, 3328], P(None, 'fsdp')
- grad_convbias: float32 [3328], P('fsdp')
- grad_step: float32 [48], replicated
- grad_rate: float32 [48], replicated
- grad_skip: float32 [48], replicated
- grad_gate: float32 [3072], P('fsdp')
- grad_outproj: float32 [3072, 1536], P('fsdp')
The draws below stay inside these ranges and needn't reach their ends.
Inputs may be any that keep to these rules, and one draw needn't show every extreme that they name: `segment_ids`: in each row the ids never fall; each of the 4 ids covers 1 to 128 consecutive slots, and some id covers exactly 128.
All inputs are finite; a program needn't handle non-finite values.
Results may differ from the reference program's by a relative error of at most 0.0072.
Values may be sent and summed in bfloat16 or wider, within the bound.
No kernel may reach another device: no remote copies, remote signals or barrier semaphores. Data moves between devices by JAX's collectives and lax.ppermute only.
A program may use at most 256 MiB of HBM per device.

```python
import math
from functools import partial
import jax
import jax.numpy as jnp
import numpy as np
from jax import lax

D = 1536
HEADS = 48
HEADDIM = 64
DSTATE = 128
KERNEL = 4
TOK_DEV = 256
SEQS_DEV = 4
DI = 3072
CONV = 3328
PROJ = 6448
SEQ_MAX = 128
BUFFERS = 32
TOKENS = 8192


def shard_levels(rng, extent, cuts, smallest, top_value):
    gain, own = 1.0, jax.random.fold_in(rng, 6)
    for dim, shards_of in cuts:
        steps = jnp.exp(jax.random.uniform(jax.random.fold_in(own, dim), (shards_of,), jnp.float32, smallest / len(cuts), top_value / len(cuts)))
        gain = gain * jnp.repeat(steps, extent[dim] // shards_of).reshape([-1 if axis == dim else 1 for axis in range(len(extent))])
    return gain


def split_up(number_of, total, limit, lean):
    portions = [(1 << 20) // math.isqrt(rank ** lean) + 1 for rank in range(2, number_of + 1)]
    surplus, holding = total - limit - (number_of - 1), [1] * (number_of - 1)
    while surplus > 0:
        movable = [i for i in range(number_of - 1) if holding[i] < limit]
        mass, left = sum([portions[i] for i in movable]), surplus
        for i in movable:
            addition = min(limit - holding[i], max(1, left * portions[i] // mass), surplus)
            holding[i] = holding[i] + addition
            surplus = surplus - addition
    return np.array([limit] + holding)


def uneven(rng, count, total, limit, slope):
    if count == 2:
        one = jax.random.randint(rng, (), max(1, total - limit), min(limit, total - 1) + 1)
        return jnp.stack([one, total - one])
    tallies = jnp.asarray(split_up(count, total, limit, slope), jnp.int32)
    couples = (count - 1) // 2
    donor, receiver = tallies[1:1 + 2 * couples:2], tallies[2:2 + 2 * couples:2]
    margin = jnp.minimum(donor - 1, limit - receiver)
    shifted = jax.random.randint(jax.random.fold_in(rng, 1), (couples,), 0, 1 << 20) % (margin + 1)
    tallies = tallies.at[1:1 + 2 * couples:2].set(donor - shifted).at[2:2 + 2 * couples:2].set(receiver + shifted)
    return tallies[jax.random.permutation(jax.random.fold_in(rng, 2), count)]


def scatter_about(rng, extent, width, most, split=(), held_as=jnp.bfloat16):
    values = jax.random.normal(rng, extent, jnp.float32) * width
    if len(split) > 0:
        values = shard_levels(rng, extent, split, -0.22, 0.18) * values
    return jnp.clip(values, min=-most, max=most).astype(held_as)


def setup_inputs(seed: int = 0) -> dict:
    key_of = jax.random.split(jax.random.key(seed), 13)
    tokens = scatter_about(key_of[0], (TOKENS, D), 1.0, 6.0, ((0, 32),))
    segment_ids = jax.vmap(lambda own: jnp.searchsorted(jnp.cumsum(uneven(own, SEQS_DEV, TOK_DEV, SEQ_MAX, 2)), jnp.arange(TOK_DEV), side="right"))(jax.random.split(key_of[1], BUFFERS)).reshape((BUFFERS, TOK_DEV)).astype(jnp.int32)
    cotangent = scatter_about(key_of[2], (TOKENS, D), 1.0, 6.0, ((0, 32),))
    norm_gain = jnp.clip(1.0 + 0.1 * jax.random.normal(key_of[3], (D,), jnp.float32), 0.5, 1.5).astype(jnp.bfloat16)
    in_weight = scatter_about(key_of[4], (D, PROJ), D ** -0.5, 0.15625, ((0, 4),))
    conv_weight = scatter_about(key_of[5], (KERNEL, CONV), KERNEL ** -0.5, 3.0, ((1, 4),))
    conv_bias = jnp.clip(jax.random.uniform(key_of[6], (CONV,), jnp.float32, -0.5, 0.5) * shard_levels(key_of[6], (CONV,), ((0, 4),), -0.4, 0.0), -0.5, 0.5).astype(jnp.bfloat16)
    step_bias = jnp.clip(jax.random.uniform(key_of[7], (HEADS,), jnp.float32, -6.0, -2.0), -6.0, -2.0).astype(jnp.bfloat16)
    rate_log = jnp.clip(jax.random.uniform(key_of[8], (HEADS,), jnp.float32, 0.0, 2.5), 0.0, 2.5).astype(jnp.bfloat16)
    skip_gain = jnp.clip(jax.random.uniform(key_of[9], (HEADS,), jnp.float32, 0.5, 2.0), 0.5, 2.0).astype(jnp.bfloat16)
    gate_gain = jnp.clip(1.0 + 0.1 * jax.random.normal(key_of[10], (DI,), jnp.float32), 0.5, 1.5).astype(jnp.bfloat16)
    out_weight = scatter_about(key_of[11], (DI, D), DI ** -0.5, 0.109375, ((0, 4),))
    return dict(tokens=tokens, segment_ids=segment_ids, cotangent=cotangent, norm_gain=norm_gain, in_weight=in_weight, conv_weight=conv_weight, conv_bias=conv_bias, step_bias=step_bias, rate_log=rate_log, skip_gain=skip_gain, gate_gain=gate_gain, out_weight=out_weight)


HIGHEST = lax.Precision.HIGHEST
EPSILON = 1e-05

def prenorm(values, scaling):
    factor = lax.rsqrt(lax.optimization_barrier(jnp.mean(values * values, axis=-1, keepdims=True)) + EPSILON)
    return values * factor * scaling

def convolve(segments, conv_input, conv_kernel, conv_shift):
    token_count = conv_input.shape[0]
    padded = jnp.pad(conv_input, ((KERNEL - 1, 0), (0, 0)))
    padded_ids = jnp.concatenate([jnp.full((KERNEL - 1,), -1, jnp.int32), segments.astype(jnp.int32)])
    summed = jnp.zeros_like(conv_input) + conv_shift
    for offset in range(KERNEL):
        matches = (padded_ids[offset:offset + token_count] == segments).astype(conv_input.dtype)
        summed = summed + conv_kernel[offset] * padded[offset:offset + token_count] * matches[:, None]
    return jax.nn.silu(summed)

def scan_whole(segments, values_in, key_side, query_side, step_size, decay):
    token_count = values_in.shape[0]
    running = jnp.cumsum(decay, axis=0).T
    between = running[:, :, None] - running[:, None, :]
    places = jnp.arange(token_count)
    allowed = (places[:, None] >= places[None, :]) & (segments[:, None] == segments[None, :])
    decays = jnp.where(allowed[None], jnp.exp(jnp.where(allowed[None], between, 0.0)), 0.0)
    affinity = jnp.dot(query_side, key_side.T, precision=HIGHEST)
    weights = decays * affinity[None] * step_size.T[:, None, :]
    return jnp.einsum('hij,jhp->ihp', weights, values_in, precision=HIGHEST)

def mixer(segments, projected, conv_kernel, conv_shift, step_offset, rate_values, skip_weight, gate_scale):
    token_count = projected.shape[0]
    gate_part = projected[:, :DI]
    conv_input = projected[:, DI:DI + CONV]
    step_input = projected[:, DI + CONV:]
    activated = convolve(segments, conv_input, conv_kernel, conv_shift)
    values_in = activated[:, :DI].reshape(token_count, HEADS, HEADDIM)
    key_side = activated[:, DI:DI + DSTATE]
    query_side = activated[:, DI + DSTATE:]
    step_size = jax.nn.softplus(step_input + step_offset)
    decay = -jnp.exp(rate_values) * step_size
    scanned = scan_whole(segments, values_in, key_side, query_side, step_size, decay) + skip_weight[None, :, None] * values_in
    gated = scanned.reshape(token_count, DI) * jax.nn.silu(gate_part)
    factor = lax.rsqrt(lax.optimization_barrier(jnp.mean(gated * gated, axis=-1, keepdims=True)) + EPSILON)
    return gated * factor * gate_scale

def reference(tokens, segment_ids, cotangent, norm_gain, in_weight, conv_weight, conv_bias, step_bias, rate_log, skip_gain, gate_gain, out_weight):
    small = tuple((value.astype(jnp.float32) for value in (conv_weight, conv_bias, step_bias, rate_log, skip_gain, gate_gain)))
    first_gain = norm_gain.astype(jnp.float32)
    contract = (((0,), (0,)), ((), ()))

    def one_row(totals, inputs):
        row_tokens, segments, row_cotangent = inputs
        inputs32 = row_tokens.astype(jnp.float32)
        normed, norm_back = jax.vjp(prenorm, inputs32, first_gain)
        normed_low = normed.astype(jnp.bfloat16)
        projected = jnp.dot(normed_low, in_weight, preferred_element_type=jnp.float32)
        mixed, mix_back = jax.vjp(partial(mixer, segments), projected, *small)
        mixed_low = mixed.astype(jnp.bfloat16)
        result = (inputs32 + jnp.dot(mixed_low, out_weight, preferred_element_type=jnp.float32)).astype(jnp.bfloat16)
        grad_mixed = jnp.dot(row_cotangent, out_weight.T, preferred_element_type=jnp.float32)
        grads = mix_back(grad_mixed)
        grad_low = grads[0].astype(jnp.bfloat16)
        grad_normed = jnp.dot(grad_low, in_weight.T, preferred_element_type=jnp.float32)
        grad_through, grad_first = norm_back(grad_normed)
        row_grad = (row_cotangent.astype(jnp.float32) + grad_through).astype(jnp.bfloat16)
        input_terms = lax.dot_general(normed_low, grad_low, contract, preferred_element_type=jnp.float32)
        output_terms = lax.dot_general(mixed_low, row_cotangent, contract, preferred_element_type=jnp.float32)
        updated = (totals[0] + grad_first, totals[1] + input_terms, totals[2] + grads[1], totals[3] + grads[2], totals[4] + grads[3], totals[5] + grads[4], totals[6] + grads[5], totals[7] + grads[6], totals[8] + output_terms)
        return (updated, (result, row_grad))
    start = (jnp.zeros((D,), jnp.float32), jnp.zeros((D, PROJ), jnp.float32), jnp.zeros((KERNEL, CONV), jnp.float32), jnp.zeros((CONV,), jnp.float32), jnp.zeros((HEADS,), jnp.float32), jnp.zeros((HEADS,), jnp.float32), jnp.zeros((HEADS,), jnp.float32), jnp.zeros((DI,), jnp.float32), jnp.zeros((DI, D), jnp.float32))
    rows_in = (tokens.reshape(BUFFERS, TOK_DEV, D), segment_ids.astype(jnp.int32), cotangent.reshape(BUFFERS, TOK_DEV, D))
    totals, stacked = lax.scan(one_row, start, rows_in)
    output = stacked[0].reshape(TOKENS, D)
    tokens_grad = stacked[1].reshape(TOKENS, D)
    return (output, tokens_grad, totals[0], totals[1], totals[2], totals[3], totals[4], totals[5], totals[6], totals[7], totals[8])
```

```python
from functools import partial

import jax
import jax.numpy as jnp
from jax import lax
from jax.experimental import pallas as pl
from jax.experimental.pallas import tpu as pltpu
from jax.sharding import PartitionSpec as P

HEADS = 48
HEADDIM = 64
DSTATE = 128
KERNEL = 4
LANES = 128
EPSILON = 1e-05
BF = jnp.bfloat16
F32 = jnp.float32
HIGHEST = lax.Precision.HIGHEST
VMEM_LIMIT = 60 * 1024 * 1024

NN = (((1,), (0,)), ((), ()))
NT = (((1,), (1,)), ((), ()))
TN = (((0,), (0,)), ((), ()))


def mm(a, b, dims):
    return lax.dot_general(a, b, dims, preferred_element_type=F32)


def mm_full(a, b, dims):
    return lax.dot_general(a, b, dims, precision=HIGHEST, preferred_element_type=F32)


def silu_parts(v):
    gate = jax.nn.sigmoid(v)
    return v * gate, gate * (1.0 + v * (1.0 - gate))


def call(kernel, out_shape, flops, moved, **kw):
    return pl.pallas_call(
        kernel,
        out_shape=out_shape,
        cost_estimate=pl.CostEstimate(flops=flops, bytes_accessed=moved, transcendentals=0),
        compiler_params=pltpu.CompilerParams(vmem_limit_bytes=VMEM_LIMIT),
        **kw,
    )


VM = pl.BlockSpec(memory_space=pltpu.VMEM)
HBM = pl.BlockSpec(memory_space=pl.ANY)


def inproj_kernel(groups, *refs):
    tokens = refs[:groups]
    gain_ref = refs[groups]
    place_ref = refs[groups + 1]
    own_ref = refs[groups + 2]
    near = refs[groups + 3 : 2 * groups + 2]
    far = refs[2 * groups + 2 : 3 * groups + 1]
    normed_ref, proj_ref, weight_ref, sems = refs[3 * groups + 1 :]
    member, core = place_ref[0], place_ref[1]
    rows = own_ref.shape[0]
    half = rows // 2
    copies = [
        pltpu.make_async_copy(
            own_ref, weight_ref.at[pl.ds(pl.multiple_of(member * rows, 16), rows), :], sems.at[0]
        )
    ]
    for k in range(1, groups):
        base = jnp.bitwise_xor(member, k) * rows
        first = pl.multiple_of(base + core * half, 16)
        second = pl.multiple_of(base + (1 - core) * half, 16)
        copies.append(
            pltpu.make_async_copy(near[k - 1], weight_ref.at[pl.ds(first, half), :], sems.at[2 * k - 1])
        )
        copies.append(
            pltpu.make_async_copy(far[k - 1], weight_ref.at[pl.ds(second, half), :], sems.at[2 * k])
        )
    for copy in copies:
        copy.start()
    span = tokens[0].shape[0]
    gain = gain_ref[...]
    for r in range(groups):
        x = tokens[r][...].astype(F32)
        factor = lax.rsqrt(jnp.mean(x * x, axis=-1, keepdims=True) + EPSILON)
        normed_ref[r * span : (r + 1) * span, :] = (x * factor * gain).astype(BF)
    for copy in copies:
        copy.wait()
    width = 384
    total = weight_ref.shape[1] // width

    def column(n, carry):
        at = pl.multiple_of(n * width, LANES)
        for r in range(groups):
            proj_ref[r * span : (r + 1) * span, pl.ds(at, width)] = mm(
                normed_ref[r * span : (r + 1) * span, :], weight_ref[:, pl.ds(at, width)], NN
            )
        return carry

    lax.fori_loop(0, total, column, 0)


def conv_forward(x, masks, taps, shift):
    total = shift + taps[KERNEL - 1] * x
    for s in range(1, KERNEL):
        total = total + taps[KERNEL - 1 - s] * (pltpu.roll(x, s, 0) * masks[s - 1])
    return total


def conv_backward(grad, x, masks, taps):
    span = x.shape[0]
    back = taps[KERNEL - 1] * grad
    tap_grads = [None] * KERNEL
    tap_grads[KERNEL - 1] = jnp.sum(grad * x, axis=0, keepdims=True)
    for s in range(1, KERNEL):
        part = grad * masks[s - 1]
        back = back + taps[KERNEL - 1 - s] * pltpu.roll(part, span - s, 0)
        tap_grads[KERNEL - 1 - s] = jnp.sum(part * pltpu.roll(x, s, 0), axis=0, keepdims=True)
    return back, tap_grads


def wide(column, count):
    return jnp.concatenate([column] * (count // LANES), axis=1)


def segment_masks(seg_ref):
    span = seg_ref.shape[-1]
    row = seg_ref[0:1, :]
    column = jnp.broadcast_to(row, (LANES, span)).T
    token = lax.broadcasted_iota(jnp.int32, (span, LANES), 0)
    masks = []
    for s in range(1, KERNEL):
        same = (pltpu.roll(column, s, 0) == column) & (token >= s)
        masks.append(jnp.where(same, 1.0, 0.0))
    i = lax.broadcasted_iota(jnp.int32, (span, span), 0)
    j = lax.broadcasted_iota(jnp.int32, (span, span), 1)
    allowed = (i >= j) & (wide(column, span) == row)
    lower = jnp.where(i >= j, 1.0, 0.0)
    return masks, jnp.where(allowed, 1.0, 0.0), lower


def row_setup(shared_ref, seg_ref, taps_ref, head_ref, member, per, saved):
    (mask_ref, affinity_ref, step_ref, run_ref, runt_ref, extra) = saved
    masks, allowed, lower = segment_masks(seg_ref)
    for s in range(KERNEL - 1):
        mask_ref[s] = masks[s]
    outs = []
    for c in range(2):
        at = slice(c * LANES, (c + 1) * LANES)
        taps = [taps_ref[k : k + 1, at] for k in range(KERNEL)]
        total = conv_forward(shared_ref[:, at], masks, taps, taps_ref[KERNEL : KERNEL + 1, at])
        outs.append((total, silu_parts(total)))
    keys, queries = outs[0][1][0], outs[1][1][0]
    affinity_ref[...] = mm_full(queries, keys, NT) * allowed
    raw = pltpu.roll(shared_ref[:, 2 * LANES :], lax.rem(LANES - member * per, LANES), 1)
    raw = raw + head_ref[0:1, :]
    step = jnp.maximum(raw, 0.0) + jnp.log1p(jnp.exp(-jnp.abs(raw)))
    run = mm_full(lower, -head_ref[1:2, :] * step, NN)
    step_ref[...] = step
    run_ref[...] = run
    runt_ref[...] = run.T
    if extra is not None:
        allowed_ref, lower_ref, raw_ref, sum_ref, keys_ref, queries_ref = extra
        allowed_ref[...] = allowed
        lower_ref[...] = lower
        raw_ref[...] = raw
        sum_ref[:, :LANES] = outs[0][0]
        sum_ref[:, LANES:] = outs[1][0]
        keys_ref[...] = keys
        queries_ref[...] = queries


def pair_decays(pair, run_ref, runt_ref, step_ref):
    back = lax.rem(LANES - 2 * pair, LANES)
    runs = pltpu.roll(run_ref[...], back, 1)
    steps = pltpu.roll(step_ref[...], back, 1)
    span = runs.shape[0]
    lane = lax.broadcasted_iota(jnp.int32, (span, LANES), 1)
    low = lane < HEADDIM
    stepx = jnp.where(low, steps[:, 0:1], steps[:, 1:2])
    decays = []
    for e in range(2):
        row = runt_ref[pl.ds(2 * pair + e, 1), :]
        decays.append(jnp.exp(jnp.minimum(runs[:, e : e + 1] - row, 0.0)))
    return decays, stepx, steps, low, lane


def forward_kernel(
    per,
    place_ref,
    z_ref,
    v_ref,
    shared_ref,
    seg_ref,
    taps_s_ref,
    taps_v_ref,
    head_ref,
    scanned_ref,
    gated_ref,
    square_ref,
    mask_ref,
    affinity_ref,
    step_ref,
    run_ref,
    runt_ref,
    total_ref,
):
    pair = pl.program_id(1)
    saved = (mask_ref, affinity_ref, step_ref, run_ref, runt_ref, None)

    @pl.when(pair == 0)
    def _():
        row_setup(shared_ref, seg_ref, taps_s_ref, head_ref, place_ref[0], per, saved)
        total_ref[...] = jnp.zeros_like(total_ref)

    masks = [mask_ref[s] for s in range(KERNEL - 1)]
    taps = [taps_v_ref[k : k + 1, :] for k in range(KERNEL)]
    values = silu_parts(conv_forward(v_ref[...], masks, taps, taps_v_ref[KERNEL : KERNEL + 1, :]))[0]
    decays, stepx, _, low, _ = pair_decays(pair, run_ref, runt_ref, step_ref)
    affinity = affinity_ref[...]
    fed = (stepx * values).astype(BF)
    first = mm((decays[0] * affinity).astype(BF), fed, NN)
    second = mm((decays[1] * affinity).astype(BF), fed, NN)
    inner = jnp.where(low, first, second)
    scanned = inner + taps_v_ref[KERNEL + 1 : KERNEL + 2, :] * values
    z = z_ref[...]
    g = scanned * (z * jax.nn.sigmoid(z))
    scanned_ref[...] = scanned
    gated_ref[...] = (g * taps_v_ref[KERNEL + 2 : KERNEL + 3, :]).astype(BF)
    total_ref[...] = total_ref[...] + g * g

    @pl.when(pair == pl.num_programs(1) - 1)
    def _():
        row = jnp.sum(total_ref[...].T, axis=0, keepdims=True)
        square_ref[...] = jnp.broadcast_to(row, square_ref.shape)


def mixgrad_kernel(groups, *refs):
    cots = refs[:groups]
    out_w_ref, gated_ref, square_ref, dm_ref, sums_ref = refs[groups:]
    span = cots[0].shape[0]
    weight = out_w_ref[...]
    for r in range(groups):
        at = slice(r * span, (r + 1) * span)
        dm = mm(cots[r][...], weight, NT)
        dm_ref[at, :] = dm
        prod = dm * gated_ref[at, :].astype(F32)
        part = prod[:, :LANES]
        for c in range(1, prod.shape[1] // LANES):
            part = part + prod[:, c * LANES : (c + 1) * LANES]
        row = jnp.sum(part.T, axis=0, keepdims=True)
        sub = lax.broadcasted_iota(jnp.int32, (8, span), 0)
        sums_ref[8 * r : 8 * r + 8, :] = jnp.where(sub == 0, square_ref[8 * r : 8 * r + 8, :], row)


def outproj_kernel(groups, gated_ref, out_w_ref, *outs):
    span = outs[0].shape[0]
    weight = out_w_ref[...]
    for r in range(groups):
        outs[r][...] = mm(gated_ref[r * span : (r + 1) * span, :], weight, NN).astype(outs[r].dtype)


def gate_scales(parts, width):
    total = parts[0]
    for part in parts[1:]:
        total = total + part
    square, cross = total[0:1, :], total[1:2, :]
    factor = lax.rsqrt(square / width + EPSILON)
    bend = factor * factor * factor * (cross / width)
    span = total.shape[1]
    return (
        jnp.broadcast_to(factor, (LANES, span)).T,
        jnp.broadcast_to(bend, (LANES, span)).T,
    )


def gatebwd_kernel(groups, width, *refs):
    sums = refs[:groups]
    z_ref, scanned_ref, dm_ref, gain_ref, gz_ref, ds_ref, mixed_ref, gate_ref = refs[groups:]
    r = pl.program_id(0)
    factor, bend = gate_scales([s[...] for s in sums], width)

    @pl.when(r == 0)
    def _():
        gate_ref[...] = jnp.zeros_like(gate_ref)

    for c in range(z_ref.shape[1] // LANES):
        at = slice(c * LANES, (c + 1) * LANES)
        gain = gain_ref[0:1, at]
        sz, dsz = silu_parts(z_ref[:, at])
        scanned = scanned_ref[:, at]
        dm = dm_ref[:, at]
        g = scanned * sz
        scaled = g * factor
        dg = factor * (dm * gain) - g * bend
        mixed_ref[:, at] = (scaled * gain).astype(BF)
        gz_ref[:, at] = (dg * scanned * dsz).astype(BF)
        ds_ref[:, at] = dg * sz
        gate_ref[0:1, at] += jnp.sum(dm * scaled, axis=0, keepdims=True)


def backward_kernel(
    per,
    place_ref,
    ds_ref,
    v_ref,
    scanned_ref,
    shared_ref,
    seg_ref,
    taps_s_ref,
    taps_v_ref,
    head_ref,
    gv_ref,
    gs_ref,
    vsum_ref,
    ssum_ref,
    mask_ref,
    affinity_ref,
    step_ref,
    run_ref,
    runt_ref,
    allowed_ref,
    lower_ref,
    raw_ref,
    sum_ref,
    keys_ref,
    queries_ref,
    daff_ref,
    dstep_ref,
    drun_ref,
):
    row, pair = pl.program_id(0), pl.program_id(1)
    extra = (allowed_ref, lower_ref, raw_ref, sum_ref, keys_ref, queries_ref)
    saved = (mask_ref, affinity_ref, step_ref, run_ref, runt_ref, extra)

    @pl.when((row == 0) & (pair == 0))
    def _():
        vsum_ref[...] = jnp.zeros_like(vsum_ref)
        ssum_ref[...] = jnp.zeros_like(ssum_ref)

    @pl.when(pair == 0)
    def _():
        row_setup(shared_ref, seg_ref, taps_s_ref, head_ref, place_ref[0], per, saved)
        daff_ref[...] = jnp.zeros_like(daff_ref)
        dstep_ref[...] = jnp.zeros_like(dstep_ref)
        drun_ref[...] = jnp.zeros_like(drun_ref)

    masks = [mask_ref[s] for s in range(KERNEL - 1)]
    taps = [taps_v_ref[k : k + 1, :] for k in range(KERNEL)]
    skip = taps_v_ref[KERNEL + 1 : KERNEL + 2, :]
    x = v_ref[...]
    total = conv_forward(x, masks, taps, taps_v_ref[KERNEL : KERNEL + 1, :])
    values, dvalues = silu_parts(total)
    decays, stepx, steps, low, lane = pair_decays(pair, run_ref, runt_ref, step_ref)
    affinity = affinity_ref[...]
    ds = ds_ref[...]
    dsb = ds.astype(BF)
    fed = (stepx * values).astype(BF)
    daff = daff_ref[...]
    backs = []
    for e in range(2):
        backs.append(mm((decays[e] * affinity).astype(BF), dsb, TN))
        chosen = jnp.where(low if e == 0 else ~low, ds, 0.0).astype(BF)
        daff = daff + mm(chosen, fed, NT) * decays[e]
    daff_ref[...] = daff
    back = jnp.where(low, backs[0], backs[1])
    inner = scanned_ref[...] - skip * values
    direct = back * values
    moved = dsb.astype(F32) * inner - fed.astype(F32) * back
    dstep, drun = dstep_ref[...], drun_ref[...]
    for e in range(2):
        half = low if e == 0 else ~low
        spot = lane == 2 * pair + e
        dstep = dstep + jnp.where(spot, jnp.sum(jnp.where(half, direct, 0.0), axis=1, keepdims=True), 0.0)
        drun = drun + jnp.where(spot, jnp.sum(jnp.where(half, moved, 0.0), axis=1, keepdims=True), 0.0)
    dstep_ref[...] = dstep
    drun_ref[...] = drun
    dact = stepx * back + skip * ds
    dtotal = dact * dvalues
    dx, tap_grads = conv_backward(dtotal, x, masks, taps)
    gv_ref[...] = dx.astype(BF)
    rows = tap_grads + [
        jnp.sum(dtotal, axis=0, keepdims=True),
        jnp.sum(ds * values, axis=0, keepdims=True),
        jnp.zeros((2, LANES), F32),
    ]
    at = pl.ds(pl.multiple_of(pair * LANES, LANES), LANES)
    vsum_ref[:, at] = vsum_ref[:, at] + jnp.concatenate(rows, axis=0)

    @pl.when(pair == pl.num_programs(1) - 1)
    def _():
        full = daff_ref[...] * allowed_ref[...]
        keys, queries = keys_ref[...], queries_ref[...]
        dqueries = mm_full(full, keys, NN)
        dkeys = mm_full(full, queries, TN)
        for c, dside in enumerate((dkeys, dqueries)):
            lanes = slice(c * LANES, (c + 1) * LANES)
            taps_c = [taps_s_ref[k : k + 1, lanes] for k in range(KERNEL)]
            dsum = dside * silu_parts(sum_ref[:, lanes])[1]
            dside_x, taps_g = conv_backward(dsum, shared_ref[:, lanes], masks, taps_c)
            gs_ref[:, lanes] = dside_x.astype(BF)
            more = taps_g + [jnp.sum(dsum, axis=0, keepdims=True), jnp.zeros((3, LANES), F32)]
            ssum_ref[:, lanes] = ssum_ref[:, lanes] + jnp.concatenate(more, axis=0)
        ddecay = mm_full(lower_ref[...], drun_ref[...], TN)
        rate = -head_ref[1:2, :]
        step = step_ref[...]
        draw = (dstep_ref[...] + ddecay * rate) * jax.nn.sigmoid(raw_ref[...])
        draw = draw * head_ref[2:3, :]
        span = draw.shape[0]
        gs_ref[:, 2 * LANES :] = pltpu.roll(draw, place_ref[0] * per, 1).astype(BF)
        heads = [
            jnp.sum(draw, axis=0, keepdims=True),
            jnp.sum(ddecay * (rate * step), axis=0, keepdims=True) * head_ref[2:3, :],
            jnp.zeros((6, LANES), F32),
        ]
        ssum_ref[:, 2 * LANES :] = ssum_ref[:, 2 * LANES :] + jnp.concatenate(heads, axis=0)


def normgrad_kernel(groups, gz_ref, gv_ref, gs_ref, weight_ref, *outs):
    span = outs[0].shape[0]
    inner = gz_ref.shape[1]
    wz = weight_ref[:, :inner]
    wv = weight_ref[:, inner : 2 * inner]
    ws = weight_ref[:, 2 * inner :]
    for r in range(groups):
        at = slice(r * span, (r + 1) * span)
        total = mm(gz_ref[at, :], wz, NT) + mm(gv_ref[at, :], wv, NT) + mm(gs_ref[at, :], ws, NT)
        outs[r][...] = total.astype(outs[r].dtype)


def final_kernel(groups, width, *refs):
    outs = refs[:groups]
    grads = refs[groups : 2 * groups]
    sums = refs[2 * groups : 3 * groups]
    tokens_ref, cot_ref, gain_ref, output_ref, tgrad_ref, gnorm_ref = refs[3 * groups :]
    factor = gate_scales([s[...] for s in sums], width)[0]
    x = tokens_ref[...].astype(F32)
    total = outs[0][...].astype(F32)
    for part in outs[1:]:
        total = total + part[...].astype(F32)
    output_ref[...] = (x + total * factor[:, 0:1]).astype(BF)
    grad = grads[0][...].astype(F32)
    for part in grads[1:]:
        grad = grad + part[...].astype(F32)
    scale = lax.rsqrt(jnp.mean(x * x, axis=-1, keepdims=True) + EPSILON)
    gained = grad * gain_ref[...]
    bend = scale * scale * scale * jnp.mean(gained * x, axis=-1, keepdims=True)
    tgrad_ref[...] = (cot_ref[...].astype(F32) + (gained * scale - x * bend)).astype(BF)
    gnorm_ref[...] = jnp.broadcast_to(jnp.sum(grad * (x * scale), axis=0, keepdims=True), gnorm_ref.shape)


def place_kernel(groups, place_ref, zk, zs, vk, vs, sk, ss, ok, os, gin_ref, gout_ref):
    member, core = place_ref[0], place_ref[1]
    half = zk.shape[1]
    wide_ = zk.shape[2]
    edge = 2 * groups * wide_
    tail = gin_ref.shape[1] - edge
    for which, (z, v, s, o) in enumerate(((zk, vk, sk, ok), (zs, vs, ss, os))):
        part = core if which == 0 else 1 - core
        rows = pl.ds(pl.multiple_of(part * half, 16), half)
        for k in range(groups):
            col = jnp.bitwise_xor(member, k) * wide_
            gin_ref[rows, pl.ds(pl.multiple_of(col, LANES), wide_)] = z[k].astype(F32)
            gin_ref[rows, pl.ds(pl.multiple_of(groups * wide_ + col, LANES), wide_)] = v[k].astype(F32)
        gin_ref[rows, edge:] = s[:, :tail].astype(F32)
        deep = o.shape[0]
        gout_ref[pl.ds(pl.multiple_of(part * deep, 16), deep), :] = o[...].astype(F32)


def swap(value, axis, step):
    size = lax.axis_size(axis)
    return lax.ppermute(value, axis, [(i, i ^ step) for i in range(size)])


def rounded_sum(a, b):
    return (a.astype(F32) + b.astype(F32)).astype(BF)


def line_sum(value):
    size = lax.axis_size("rep")
    bits = size.bit_length() - 1
    last = bits - 2 if bits >= 3 else bits
    for b in range(1, last):
        value = rounded_sum(value, swap(value, "rep", 1 << b))
    if bits < 3:
        return value
    low = size // 4
    where = lax.axis_index("rep") // low
    inward = [(low * a + i, low * b + i) for a, b in ((0, 1), (3, 2)) for i in range(low)]
    middle = [(low * a + i, low * b + i) for a, b in ((1, 2), (2, 1)) for i in range(low)]
    outward = [(low * a + i, low * b + i) for a, b in ((1, 0), (2, 3)) for i in range(low)]
    value = rounded_sum(value, lax.ppermute(value, "rep", inward))
    value = rounded_sum(value, lax.ppermute(value, "rep", middle))
    back = lax.ppermute(value, "rep", outward)
    return jnp.where((where == 0) | (where == 3), back, value)


def all_sum(value):
    for axis in ("rep", "fsdp"):
        step = 1
        while step < lax.axis_size(axis):
            value = value + swap(value, axis, step)
            step *= 2
    return value


def pick(value, index):
    return lax.dynamic_index_in_dim(value, index, 0, keepdims=False)


def owner_terms(term, groups, member, core, after=None):
    rows = term.shape[0] // (2 * groups)
    cut = term.astype(BF).reshape(groups, 2, rows, term.shape[1])
    kept = lax.dynamic_index_in_dim(cut, core, 1, keepdims=False)
    given = lax.dynamic_index_in_dim(cut, 1 - core, 1, keepdims=False)
    total = rounded_sum(kept, swap(given, "rep", 1))
    return [pick(total, member)] + [
        swap(pick(total, member ^ k), "fsdp", k) for k in range(1, groups)
    ]


def body(
    tokens,
    segment_ids,
    cotangent,
    norm_gain,
    in_weight,
    conv_weight,
    conv_bias,
    step_bias,
    rate_log,
    skip_gain,
    gate_gain,
    out_weight,
):
    groups = lax.axis_size("fsdp")
    member = lax.axis_index("fsdp")
    core = lax.axis_index("rep") % 2
    span, model = tokens.shape
    per = HEADS // groups
    inner = per * HEADDIM
    full = inner * groups
    conv = conv_bias.shape[0] * groups
    tail = in_weight.shape[1] - 2 * full
    padded = -(-tail // 384) * 384
    width = 2 * inner + padded
    pairs = per // 2
    whole = groups * span
    place = jnp.stack([member, core]).astype(jnp.int32)

    pieces = [norm_gain, conv_weight.reshape(-1), conv_bias, segment_ids[0].astype(BF)]
    packed = jnp.concatenate(pieces).reshape(1, -1)
    small = [packed] + [swap(packed, "fsdp", k) for k in range(1, groups)]
    xs = [tokens] + [swap(tokens, "fsdp", k) for k in range(1, groups)]
    rows = in_weight.shape[0]
    shared_w = jnp.pad(in_weight[:, 2 * full :], ((0, 0), (0, padded - tail)))

    def columns_for(peer, source, shared):
        return jnp.concatenate(
            [
                lax.dynamic_slice_in_dim(source, peer * inner, inner, 1),
                lax.dynamic_slice_in_dim(source, full + peer * inner, inner, 1),
                shared,
            ],
            axis=1,
        )

    mine = columns_for(member, in_weight, shared_w)
    half_w = lax.dynamic_slice_in_dim(in_weight, core * (rows // 2), rows // 2, 0)
    half_s = lax.dynamic_slice_in_dim(shared_w, core * (rows // 2), rows // 2, 0)
    near = [swap(columns_for(member ^ k, half_w, half_s), "fsdp", k) for k in range(1, groups)]
    far = [swap(n, "rep", 1) for n in near]
    late, _ = lax.optimization_barrier((cotangent, (near[-1], xs[-1])))
    cots = [cotangent] + [swap(late, "fsdp", k) for k in range(1, groups)]

    table = jnp.concatenate(small, axis=0)
    order = jnp.arange(groups) ^ member
    table = jnp.take(table, order, axis=0).astype(F32)
    taken = rows
    gain_full = table[:, :rows].reshape(1, model)
    cols = conv // groups
    taps_full = jnp.concatenate(
        [
            jnp.swapaxes(table[:, rows : rows + KERNEL * cols].reshape(groups, KERNEL, cols), 0, 1).reshape(
                KERNEL, conv
            ),
            table[:, rows + KERNEL * cols : rows + (KERNEL + 1) * cols].reshape(1, conv),
        ],
        axis=0,
    )
    own_heads = lambda v: lax.dynamic_slice_in_dim(v.astype(F32), member * per, per, 0)
    taps_v = jnp.concatenate(
        [
            lax.dynamic_slice_in_dim(taps_full, member * inner, inner, 1),
            jnp.repeat(own_heads(skip_gain), HEADDIM).reshape(1, inner),
            gate_gain.astype(F32).reshape(1, inner),
            jnp.zeros((1, inner), F32),
        ],
        axis=0,
    )
    taps_s = jnp.concatenate([taps_full[:, full:], jnp.zeros((3, conv - full), F32)], axis=0)
    spread = lambda v: jnp.pad(v, (0, LANES - per)).reshape(1, LANES)
    heads = jnp.concatenate(
        [
            spread(own_heads(step_bias)),
            spread(jnp.exp(own_heads(rate_log))),
            spread(jnp.ones((per,), F32)),
            jnp.zeros((5, LANES), F32),
        ],
        axis=0,
    )
    segs = jnp.concatenate([jnp.broadcast_to(s[:, -span:], (8, span)) for s in small], axis=0).astype(F32)

    sems = pltpu.SemaphoreType.DMA((2 * groups,))
    smem = pl.BlockSpec(memory_space=pltpu.SMEM)
    normed, projected, weight = call(
        partial(inproj_kernel, groups),
        (
            jax.ShapeDtypeStruct((whole, model), BF),
            jax.ShapeDtypeStruct((whole, width), F32),
            jax.ShapeDtypeStruct((model, width), BF),
        ),
        2 * whole * model * width,
        4 * whole * width + 4 * model * width + 4 * whole * model,
        in_specs=[VM] * groups + [VM, smem] + [HBM] * (2 * groups - 1),
        out_specs=(VM, VM, VM),
        scratch_shapes=[sems],
    )(*xs, gain_full, place, mine, *near, *far)

    tile = lambda col: pl.BlockSpec((span, LANES), lambda r, p: (r, col + p))
    per_row = lambda cols_, col: pl.BlockSpec((span, cols_), lambda r, p: (r, col))
    fixed = lambda shape: pl.BlockSpec(shape, lambda r, p: (0, 0))
    pair_cols = pl.BlockSpec((8, LANES), lambda r, p: (0, p))
    seg_spec = pl.BlockSpec((8, span), lambda r, p: (r, 0))
    shared_spec = per_row(padded, 2 * inner // padded)
    state = [
        pltpu.VMEM((KERNEL - 1, span, LANES), F32),
        pltpu.VMEM((span, span), F32),
        pltpu.VMEM((span, LANES), F32),
        pltpu.VMEM((span, LANES), F32),
        pltpu.VMEM((LANES, span), F32),
    ]
    scan_flops = 4 * whole * span * inner
    scanned, gated, squares = call(
        partial(forward_kernel, per),
        (
            jax.ShapeDtypeStruct((whole, inner), F32),
            jax.ShapeDtypeStruct((whole, inner), BF),
            jax.ShapeDtypeStruct((8 * groups, span), F32),
        ),
        8 * scan_flops,
        16 * whole * inner,
        grid=(groups, pairs),
        in_specs=[
            smem,
            tile(0),
            tile(pairs),
            shared_spec,
            seg_spec,
            fixed((8, conv - full)),
            pair_cols,
            fixed((8, LANES)),
        ],
        out_specs=(tile(0), tile(0), seg_spec),
        scratch_shapes=state + [pltpu.VMEM((span, LANES), F32)],
    )(place, projected, projected, projected, segs, taps_s, taps_v, heads)

    proj_flops = 2 * whole * inner * model
    dm, sums = call(
        partial(mixgrad_kernel, groups),
        (jax.ShapeDtypeStruct((whole, inner), F32), jax.ShapeDtypeStruct((8 * groups, span), F32)),
        proj_flops,
        2 * whole * model + 6 * whole * inner + 2 * inner * model,
        in_specs=[VM] * (groups + 3),
        out_specs=(VM, VM),
    )(*cots, out_weight, gated, squares)
    sums_all = [sums] + [swap(sums, "fsdp", k) for k in range(1, groups)]

    outs = call(
        partial(outproj_kernel, groups),
        tuple(jax.ShapeDtypeStruct((span, model), BF if k else F32) for k in range(groups)),
        proj_flops,
        2 * whole * model + 2 * whole * inner + 2 * inner * model,
        in_specs=[VM, VM],
        out_specs=(VM,) * groups,
    )(gated, out_weight)
    outs = [outs[0]] + [swap(outs[k], "fsdp", k) for k in range(1, groups)]

    row_spec = lambda cols_, col=0: pl.BlockSpec((span, cols_), lambda r: (r, col))
    gz, ds, mixed, gate_sum = call(
        partial(gatebwd_kernel, groups, float(full)),
        (
            jax.ShapeDtypeStruct((whole, inner), BF),
            jax.ShapeDtypeStruct((whole, inner), F32),
            jax.ShapeDtypeStruct((whole, inner), BF),
            jax.ShapeDtypeStruct((8, inner), F32),
        ),
        20 * whole * inner,
        20 * whole * inner,
        grid=(groups,),
        in_specs=[
            pl.BlockSpec((8, span), (lambda k: lambda r: (jnp.bitwise_xor(r, k), 0))(k)) for k in range(groups)
        ]
        + [row_spec(inner), row_spec(inner), row_spec(inner), pl.BlockSpec((8, inner), lambda r: (0, 0))],
        out_specs=(
            row_spec(inner),
            row_spec(inner),
            row_spec(inner),
            pl.BlockSpec((8, inner), lambda r: (0, 0)),
        ),
    )(*sums_all, projected, scanned, dm, jnp.broadcast_to(gate_gain.astype(F32).reshape(1, inner), (8, inner)))

    cot_all = jnp.concatenate(cots, axis=0)
    grad_out = lax.dot_general(mixed, cot_all, TN, preferred_element_type=F32).astype(BF)
    grad_z = lax.dot_general(normed, gz, TN, preferred_element_type=F32)
    cut = grad_out.reshape(2, inner // 2, model)
    out_part = rounded_sum(pick(cut, core), swap(pick(cut, 1 - core), "rep", 1))
    out_part = line_sum(out_part)
    out_other = swap(out_part, "rep", 1)
    z_part = line_sum(jnp.stack(owner_terms(grad_z, groups, member, core)))
    z_other = swap(z_part, "rep", 1)

    gv, gs, vsum, ssum = call(
        partial(backward_kernel, per),
        (
            jax.ShapeDtypeStruct((whole, inner), BF),
            jax.ShapeDtypeStruct((whole, padded), BF),
            jax.ShapeDtypeStruct((8, inner), F32),
            jax.ShapeDtypeStruct((8, padded), F32),
        ),
        16 * scan_flops,
        16 * whole * inner,
        grid=(groups, pairs),
        in_specs=[
            smem,
            tile(0),
            tile(pairs),
            tile(0),
            shared_spec,
            seg_spec,
            fixed((8, conv - full)),
            pair_cols,
            fixed((8, LANES)),
        ],
        out_specs=(tile(0), per_row(padded, 0), fixed((8, inner)), fixed((8, padded))),
        scratch_shapes=state
        + [
            pltpu.VMEM((span, span), F32),
            pltpu.VMEM((span, span), F32),
            pltpu.VMEM((span, LANES), F32),
            pltpu.VMEM((span, 2 * LANES), F32),
            pltpu.VMEM((span, LANES), F32),
            pltpu.VMEM((span, LANES), F32),
            pltpu.VMEM((span, span), F32),
            pltpu.VMEM((span, LANES), F32),
            pltpu.VMEM((span, LANES), F32),
        ],
    )(place, ds, projected, scanned, projected, segs, taps_s, taps_v, heads)

    backs = call(
        partial(normgrad_kernel, groups),
        tuple(jax.ShapeDtypeStruct((span, model), BF if k else F32) for k in range(groups)),
        2 * whole * width * model,
        2 * whole * model + 2 * whole * width + 2 * width * model,
        in_specs=[VM] * 4,
        out_specs=(VM,) * groups,
    )(gz, gv, gs, weight)
    backs = [backs[0]] + [swap(backs[k], "fsdp", k) for k in range(1, groups)]

    grad_v = lax.dot_general(normed, gv, TN, preferred_element_type=F32)
    v_part = line_sum(jnp.stack(owner_terms(grad_v, groups, member, core)))
    v_other = swap(v_part, "rep", 1)
    grad_s = lax.dot_general(normed, gs, TN, preferred_element_type=F32)
    s_terms = owner_terms(grad_s, groups, member, core)
    s_part = s_terms[0].astype(F32)
    for term in s_terms[1:]:
        s_part = s_part + term.astype(F32)
    s_part = line_sum(s_part.astype(BF))
    s_other = swap(s_part, "rep", 1)

    whole_spec = lambda shape: pl.BlockSpec(shape, lambda i: (0,) * len(shape))
    output, tokens_grad, norm_sum = call(
        partial(final_kernel, groups, float(full)),
        (
            jax.ShapeDtypeStruct((span, model), BF),
            jax.ShapeDtypeStruct((span, model), BF),
            jax.ShapeDtypeStruct((8, model), F32),
        ),
        30 * span * model,
        24 * span * model,
        grid=(1,),
        in_specs=[whole_spec((span, model))] * (2 * groups)
        + [pl.BlockSpec((8, span), (lambda k: lambda i: (k, 0))(k)) for k in range(groups)]
        + [whole_spec((span, model))] * 2
        + [whole_spec((1, model))],
        out_specs=(whole_spec((span, model)), whole_spec((span, model)), whole_spec((8, model))),
    )(*outs, *backs, *sums_all, tokens, cotangent, gain_full)

    grad_inproj, grad_outproj = call(
        partial(place_kernel, groups),
        (
            jax.ShapeDtypeStruct(in_weight.shape, F32),
            jax.ShapeDtypeStruct(out_weight.shape, F32),
        ),
        in_weight.size,
        6 * (in_weight.size + out_weight.size),
        in_specs=[smem] + [VM] * 8,
        out_specs=(VM, VM),
    )(place, z_part, z_other, v_part, v_other, s_part, s_other, out_part, out_other)

    own_cols = lambda v: lax.dynamic_update_slice_in_dim(
        jnp.zeros((v.shape[0], full), F32), v, member * inner, 1
    )
    own_spot = lambda v: lax.dynamic_update_slice_in_dim(jnp.zeros((HEADS,), F32), v, member * per, 0)
    taps_grad = jnp.concatenate([own_cols(vsum[: KERNEL + 1]), ssum[: KERNEL + 1, : conv - full]], axis=1)
    head_grads = [
        own_spot(ssum[0, 2 * LANES : 2 * LANES + per]),
        own_spot(ssum[1, 2 * LANES : 2 * LANES + per]),
        own_spot(vsum[KERNEL + 1].reshape(per, HEADDIM).sum(axis=1)),
    ]
    flat = jnp.concatenate(
        [norm_sum[0], taps_grad.reshape(-1), own_cols(gate_sum[:1]).reshape(-1)] + head_grads
    )
    length = flat.shape[0]
    flat = jnp.pad(flat, (0, -length % 1024)).reshape(-1, LANES)
    flat = all_sum(flat).reshape(-1)
    at = 0
    grad_norm = lax.dynamic_slice_in_dim(flat, member * rows, rows, 0)
    at += model
    taps_all = flat[at : at + (KERNEL + 1) * conv].reshape(KERNEL + 1, conv)
    taps_own = lax.dynamic_slice_in_dim(taps_all, member * cols, cols, 1)
    at += (KERNEL + 1) * conv
    grad_gate = lax.dynamic_slice_in_dim(flat, at + member * inner, inner, 0)
    at += full
    return (
        output,
        tokens_grad,
        grad_norm,
        grad_inproj,
        taps_own[:KERNEL],
        taps_own[KERNEL],
        flat[at : at + HEADS],
        flat[at + HEADS : at + 2 * HEADS],
        flat[at + 2 * HEADS : at + 3 * HEADS],
        grad_gate,
        grad_outproj,
    )


def solution(mesh):
    rows = P(("rep", "fsdp"), None)
    in_specs = (
        rows,
        rows,
        rows,
        P("fsdp"),
        P("fsdp", None),
        P(None, "fsdp"),
        P("fsdp"),
        P(),
        P(),
        P(),
        P("fsdp"),
        P("fsdp", None),
    )
    out_specs = (
        rows,
        rows,
        P("fsdp"),
        P("fsdp", None),
        P(None, "fsdp"),
        P("fsdp"),
        P(),
        P(),
        P(),
        P("fsdp"),
        P("fsdp", None),
    )
    return jax.shard_map(body, mesh=mesh, in_specs=in_specs, out_specs=out_specs, check_vma=False)
```

```python
from functools import partial

import jax
import jax.numpy as jnp
from jax import lax
from jax.experimental import pallas as pl
from jax.experimental.pallas import tpu as pltpu
from jax.sharding import PartitionSpec as P


HEADS = 48
HEADDIM = 64
KERNEL = 4
LANES = 128
EPSILON = 1e-05
BF = jnp.bfloat16
F32 = jnp.float32

NN = (((1,), (0,)), ((), ()))
NT = (((1,), (1,)), ((), ()))
TN = (((0,), (0,)), ((), ()))


def mm(a, b, dims):
    return lax.dot_general(a, b, dims, preferred_element_type=F32)


def halves(x):
    top = x.astype(BF)
    return top, (x - top.astype(F32)).astype(BF)


def mm_fine(a, b, dims):
    a_top, a_low = halves(a)
    b_top, b_low = halves(b)
    return mm(a_top, b_top, dims) + (mm(a_top, b_low, dims) + mm(a_low, b_top, dims))


def mm_ones(ones, x, dims):
    top, low = halves(x)
    rest = (x - top.astype(F32) - low.astype(F32)).astype(BF)
    parts = mm(ones, jnp.concatenate([top, low, rest], axis=1), dims)
    lanes = x.shape[1]
    return parts[:, :lanes] + (parts[:, lanes : 2 * lanes] + parts[:, 2 * lanes :])


def sigmoid(v):
    return 0.5 * jnp.tanh(0.5 * v) + 0.5


def silu_parts(v):
    gate = sigmoid(v)
    return v * gate, gate * (1.0 + v * (1.0 - gate))


def call(kernel, out_shape, flops, moved, mib=None, **kw):
    grant = (mib or 4 * lax.axis_size("fsdp")) * 1024 * 1024

    def run(*operands):
        return pl.pallas_call(
            kernel,
            out_shape=out_shape,
            cost_estimate=pl.CostEstimate(flops=flops, bytes_accessed=moved, transcendentals=0),
            compiler_params=pltpu.CompilerParams(vmem_limit_bytes=grant),
            **kw,
        )(*operands)

    return run


VM = pl.BlockSpec(memory_space=pltpu.VMEM)
HBM = pl.BlockSpec(memory_space=pl.ANY)


def pack_kernel(groups, *refs):
    place_ref, weight_ref, gain_ref, taps_ref, shift_ref, seg_ref = refs[:6]
    sends = refs[6 : 5 + groups]
    small_ref, sems = refs[5 + groups :]
    member, core = place_ref[0], place_ref[1]
    half, edge, part, tail = half_sizes(sends[0].shape[0], weight_ref.shape[0], groups)
    copies = []
    for k in range(1, groups):
        peer = jnp.bitwise_xor(member, k)
        for i in range(2):
            source = pl.multiple_of(i * (edge // 2) + peer * (2 * half) + core * half, 16)
            copies.append(
                pltpu.make_async_copy(
                    weight_ref.at[pl.ds(source, half), :],
                    sends[k - 1].at[pl.ds(i * half, half), :],
                    sems.at[2 * k - 2 + i],
                )
            )
    for copy in copies:
        copy.start()
    for c, count in ((0, part), (1, tail - part)):

        @pl.when(core == c)
        def _():
            more = [
                pltpu.make_async_copy(
                    weight_ref.at[pl.ds(edge + c * part, count), :],
                    sends[k - 1].at[pl.ds(2 * half, count), :],
                    sems.at[2 * groups - 3 + k],
                )
                for k in range(1, groups)
            ]
            for copy in more:
                copy.start()
            if count < part:
                for k in range(1, groups):
                    sends[k - 1][2 * half + count :, :] = jnp.zeros((part - count, weight_ref.shape[1]), BF)
            for copy in more:
                copy.wait()

    small_ref[...] = jnp.zeros_like(small_ref)
    small_ref[0:1, : gain_ref.shape[1]] = gain_ref[...].astype(F32)
    small_ref[1 : 1 + KERNEL, : taps_ref.shape[1]] = taps_ref[...].astype(F32)
    small_ref[1 + KERNEL : 2 + KERNEL, : shift_ref.shape[1]] = shift_ref[...].astype(F32)
    small_ref[2 + KERNEL : 3 + KERNEL, : seg_ref.shape[1]] = seg_ref[...].astype(F32)
    for copy in copies:
        copy.wait()


def half_sizes(sent, columns, groups):
    full = HEADS * HEADDIM
    half = full // (2 * groups)
    return half, 2 * full, sent - 2 * half, columns - 2 * full


def inproj_kernel(groups, aligned, *refs):
    tokens = refs[:groups]
    gain_ref, place_ref, own_ref = refs[groups : groups + 3]
    given = refs[groups + 3 : -4]
    normed_ref, proj_ref, weight_ref, sems = refs[-4:]
    member, core = place_ref[0], place_ref[1]
    model = gain_ref.shape[1]
    rows = model // groups
    copies = []
    if aligned:
        half, edge, part, tail = half_sizes(given[0].shape[0], own_ref.shape[0], groups)
        for i, (source, count) in enumerate(
            ((member * 2 * half, 2 * half), (edge // 2 + member * 2 * half, 2 * half), (edge, tail))
        ):
            copies.append(
                pltpu.make_async_copy(
                    own_ref.at[pl.ds(pl.multiple_of(source, 16), count), :],
                    weight_ref.at[pl.ds(i * 2 * half, count), pl.ds(0, rows)],
                    sems.at[i],
                )
            )
        for n, piece in enumerate(given):
            k = n % (groups - 1) + 1
            whose = core if n < groups - 1 else 1 - core
            for i, count in enumerate((half, half, part)):
                target = pl.multiple_of(i * 2 * half + whose * count, 16)
                copies.append(
                    pltpu.make_async_copy(
                        piece.at[pl.ds(i * half, count), :],
                        weight_ref.at[pl.ds(target, count), pl.ds(k * rows, rows)],
                        sems.at[3 + 3 * n + i],
                    )
                )
    else:
        copies.append(pltpu.make_async_copy(own_ref, weight_ref, sems.at[0]))
    for copy in copies:
        copy.start()
    if aligned and part * 2 > tail:
        weight_ref[4 * half + tail :, 0:rows] = jnp.zeros((2 * part - tail, rows), BF)
    span = tokens[0].shape[0]
    for r in range(groups):
        blocks = [tokens[r][:, lane_block(aligned, member, k, rows)].astype(F32) for k in range(groups)]
        total = jnp.sum(blocks[0] * blocks[0], axis=-1, keepdims=True)
        for x in blocks[1:]:
            total = total + jnp.sum(x * x, axis=-1, keepdims=True)
        factor = lax.rsqrt(total / model + EPSILON)
        for k in range(groups):
            at = slice(k * rows, (k + 1) * rows)
            normed_ref[r * span : (r + 1) * span, at] = (blocks[k] * factor * gain_ref[:, at]).astype(BF)
    for copy in copies:
        copy.wait()
    width = 384
    total = weight_ref.shape[0] // width

    def column(n, carry):
        at = pl.multiple_of(n * width, LANES)
        for r in range(groups):
            proj_ref[r * span : (r + 1) * span, pl.ds(at, width)] = mm(
                normed_ref[r * span : (r + 1) * span, :], weight_ref[pl.ds(at, width), :], NT
            )
        return carry

    lax.fori_loop(0, total, column, 0)


def lane_block(aligned, member, k, rows):
    if aligned:
        return pl.ds(pl.multiple_of(jnp.bitwise_xor(member, k) * rows, LANES), rows)
    return slice(k * rows, (k + 1) * rows)


def conv_forward(x, masks, taps, shift):
    total = shift + taps[KERNEL - 1] * x
    for s in range(1, KERNEL):
        total = total + taps[KERNEL - 1 - s] * (pltpu.roll(x, s, 0) * masks[s - 1])
    return total


def conv_backward(grad, x, masks, taps):
    span = x.shape[0]
    back = taps[KERNEL - 1] * grad
    tap_grads = [None] * KERNEL
    tap_grads[KERNEL - 1] = jnp.sum(grad * x, axis=0, keepdims=True)
    for s in range(1, KERNEL):
        part = grad * masks[s - 1]
        back = back + taps[KERNEL - 1 - s] * pltpu.roll(part, span - s, 0)
        tap_grads[KERNEL - 1 - s] = jnp.sum(part * pltpu.roll(x, s, 0), axis=0, keepdims=True)
    return back, tap_grads


def wide(column, count):
    return jnp.concatenate([column] * (count // LANES), axis=1)


def segment_masks(seg_ref):
    span = seg_ref.shape[-1]
    row = seg_ref[0:1, :]
    column = jnp.broadcast_to(row, (LANES, span)).T
    token = lax.broadcasted_iota(jnp.int32, (span, LANES), 0)
    masks = []
    for s in range(1, KERNEL):
        same = (pltpu.roll(column, s, 0) == column) & (token >= s)
        masks.append(jnp.where(same, 1.0, 0.0))
    return masks, wide(column, span), row


def ordered(span):
    i = lax.broadcasted_iota(jnp.int32, (span, span), 0)
    j = lax.broadcasted_iota(jnp.int32, (span, span), 1)
    return i >= j, i <= j


def row_setup(shared_ref, seg_ref, taps_ref, head_ref, member, per, affinity_ref, kept):
    mask_ref, afft_ref, step_ref, run_ref, runt_ref, raw_ref, act_ref, sum_ref = kept
    masks, column, row = segment_masks(seg_ref)
    after, _ = ordered(row.shape[1])
    for s in range(KERNEL - 1):
        mask_ref[:, s * LANES : (s + 1) * LANES] = masks[s]
    outs = []
    for c in range(2):
        at = slice(c * LANES, (c + 1) * LANES)
        taps = [taps_ref[k : k + 1, at] for k in range(KERNEL)]
        total = conv_forward(shared_ref[:, at], masks, taps, taps_ref[KERNEL : KERNEL + 1, at])
        active = total * sigmoid(total)
        outs.append(active)
        sum_ref[:, at] = total
        act_ref[:, at] = active
    affinity = jnp.where(after & (column == row), mm_fine(outs[1], outs[0], NT), 0.0)
    affinity_ref[...] = affinity
    afft_ref[...] = affinity.T
    raw = pltpu.roll(shared_ref[:, 2 * LANES :], lax.rem(LANES - member * per, LANES), 1)
    raw = raw + head_ref[0:1, :]
    step = jnp.maximum(raw, 0.0) + jnp.log1p(jnp.exp(-jnp.abs(raw)))
    run = mm_ones(jnp.where(after, 1.0, 0.0).astype(BF), -head_ref[1:2, :] * step, NN)
    raw_ref[...] = raw
    step_ref[...] = step
    run_ref[...] = run
    runt_ref[...] = run.T


def pair_columns(pair, run_ref, runt_ref, step_ref):
    back = lax.rem(LANES - 2 * pair, LANES)
    runs = pltpu.roll(run_ref[...], back, 1)
    steps = pltpu.roll(step_ref[...], back, 1)
    lane = lax.broadcasted_iota(jnp.int32, runs.shape, 1)
    low = lane < HEADDIM
    stepx = jnp.where(low, steps[:, 0:1], steps[:, 1:2])
    columns = [runs[:, e : e + 1] for e in range(2)]
    rows = [runt_ref[pl.ds(2 * pair + e, 1), :] for e in range(2)]
    return columns, rows, stepx, low, lane


def forward_kernel(
    per,
    place_ref,
    z_ref,
    v_ref,
    shared_ref,
    seg_ref,
    taps_s_ref,
    taps_v_ref,
    head_ref,
    scanned_ref,
    total_ref,
    gated_ref,
    square_ref,
    mask_ref,
    afft_ref,
    step_ref,
    run_ref,
    runt_ref,
    raw_ref,
    act_ref,
    sum_ref,
    affinity_ref,
    square_sum_ref,
):
    pair = pl.program_id(1)

    @pl.when(pair == 0)
    def _():
        kept = (mask_ref, afft_ref, step_ref, run_ref, runt_ref, raw_ref, act_ref, sum_ref)
        row_setup(shared_ref, seg_ref, taps_s_ref, head_ref, place_ref[0], per, affinity_ref, kept)
        square_sum_ref[...] = jnp.zeros_like(square_sum_ref)

    masks = [mask_ref[:, s * LANES : (s + 1) * LANES] for s in range(KERNEL - 1)]
    taps = [taps_v_ref[k : k + 1, :] for k in range(KERNEL)]
    total = conv_forward(v_ref[...], masks, taps, taps_v_ref[KERNEL : KERNEL + 1, :])
    total_ref[...] = total
    values = total * sigmoid(total)
    columns, rows, stepx, low, _ = pair_columns(pair, run_ref, runt_ref, step_ref)
    fed = (stepx * values).astype(BF)
    skipped = taps_v_ref[KERNEL + 1 : KERNEL + 2, :] * values
    cut = fed.shape[0] // 2
    for n in range(2):
        at = slice(n * cut, (n + 1) * cut)
        seen = (n + 1) * cut
        affinity = affinity_ref[at, :seen]
        parts = []
        for e in range(2):
            decay = jnp.exp(jnp.minimum(columns[e][at] - rows[e][:, :seen], 0.0))
            parts.append(mm((decay * affinity).astype(BF), fed[:seen], NN))
        scanned = jnp.where(low[at], parts[0], parts[1]) + skipped[at]
        z = z_ref[at, :]
        g = scanned * (z * sigmoid(z))
        scanned_ref[at, :] = scanned
        gated_ref[at, :] = (g * taps_v_ref[KERNEL + 2 : KERNEL + 3, :]).astype(BF)
        square_sum_ref[at, :] = square_sum_ref[at, :] + g * g

    @pl.when(pair == pl.num_programs(1) - 1)
    def _():
        row = jnp.sum(square_sum_ref[...].T, axis=0, keepdims=True)
        square_ref[...] = jnp.broadcast_to(row, square_ref.shape)


def mixgrad_kernel(groups, *refs):
    cots = refs[:groups]
    out_w_ref, gated_ref, square_ref, dm_ref, sums_ref = refs[groups:]
    span = cots[0].shape[0]
    weight = out_w_ref[...]
    for r in range(groups):
        at = slice(r * span, (r + 1) * span)
        dm = mm(cots[r][...], weight, NT)
        dm_ref[at, :] = dm
        prod = dm * gated_ref[at, :].astype(F32)
        part = prod[:, :LANES]
        for c in range(1, prod.shape[1] // LANES):
            part = part + prod[:, c * LANES : (c + 1) * LANES]
        row = jnp.sum(part.T, axis=0, keepdims=True)
        sub = lax.broadcasted_iota(jnp.int32, (8, span), 0)
        sums_ref[8 * r : 8 * r + 8, :] = jnp.where(sub == 0, square_ref[8 * r : 8 * r + 8, :], row)


def outproj_kernel(groups, gated_ref, out_w_ref, *outs):
    span = outs[0].shape[0]
    weight = out_w_ref[...]
    for r in range(groups):
        outs[r][...] = mm(gated_ref[r * span : (r + 1) * span, :], weight, NN).astype(outs[r].dtype)


def gate_scales(parts, width):
    total = parts[0]
    for part in parts[1:]:
        total = total + part
    square, cross = total[0:1, :], total[1:2, :]
    factor = lax.rsqrt(square / width + EPSILON)
    bend = factor * factor * factor * (cross / width)
    span = total.shape[1]
    return (
        jnp.broadcast_to(factor, (LANES, span)).T,
        jnp.broadcast_to(bend, (LANES, span)).T,
    )


def gatebwd_kernel(groups, width, *refs):
    sums = refs[:groups]
    z_ref, scanned_ref, dm_ref, gain_ref, gz_ref, ds_ref, mixed_ref, gate_ref = refs[groups:]
    r = pl.program_id(0)
    factor, bend = gate_scales([s[...] for s in sums], width)

    @pl.when(r == 0)
    def _():
        gate_ref[...] = jnp.zeros_like(gate_ref)

    for c in range(z_ref.shape[1] // LANES):
        at = slice(c * LANES, (c + 1) * LANES)
        gain = gain_ref[0:1, at]
        sz, dsz = silu_parts(z_ref[:, at])
        scanned = scanned_ref[:, at]
        dm = dm_ref[:, at]
        g = scanned * sz
        scaled = g * factor
        dg = factor * (dm * gain) - g * bend
        mixed_ref[:, at] = (scaled * gain).astype(BF)
        gz_ref[:, at] = (dg * scanned * dsz).astype(BF)
        ds_ref[:, at] = dg * sz
        gate_ref[0:1, at] += jnp.sum(dm * scaled, axis=0, keepdims=True)


def backward_kernel(per, first, last, carried, *refs):
    (ds_ref, v_ref, total_in_ref, scanned_ref, mask_ref, afft_ref, step_ref, run_ref, runt_ref, taps_v_ref) = refs[:10]
    refs = refs[10:]
    if carried:
        carry, refs = refs[:3], refs[3:]
    if last:
        (shared_ref, raw_ref, act_ref, sum_ref, seg_ref, taps_s_ref, head_ref, place_ref) = refs[:8]
        gv_ref, vsum_ref, gs_ref, ssum_ref, daff_ref, dstep_ref, drun_ref = refs[8:]
    else:
        gv_ref, vsum_ref, daff_ref, dstep_ref, drun_ref = refs
    row, pair = pl.program_id(0), pl.program_id(1)
    head_pair = pair + first

    @pl.when((row == 0) & (pair == 0))
    def _():
        vsum_ref[...] = jnp.zeros_like(vsum_ref)
        if last:
            ssum_ref[...] = jnp.zeros_like(ssum_ref)

    @pl.when(pair == 0)
    def _():
        for n, target in enumerate((daff_ref, dstep_ref, drun_ref)):
            target[...] = carry[n][...] if carried else jnp.zeros_like(target)

    masks = [mask_ref[:, s * LANES : (s + 1) * LANES] for s in range(KERNEL - 1)]
    taps = [taps_v_ref[k : k + 1, :] for k in range(KERNEL)]
    skip = taps_v_ref[KERNEL + 1 : KERNEL + 2, :]
    values, dvalues = silu_parts(total_in_ref[...])
    columns, rows, stepx, low, lane = pair_columns(head_pair, run_ref, runt_ref, step_ref)
    ds = ds_ref[...]
    dsb = ds.astype(BF)
    fed = (stepx * values).astype(BF)
    zero = jnp.zeros_like(dsb)
    chosen = [jnp.where(low, dsb, zero), jnp.where(low, zero, dsb)]
    cut = fed.shape[0] // 2
    backs = []
    for n in range(2):
        at = slice(n * cut, (n + 1) * cut)
        begin = n * cut
        affinity = afft_ref[at, begin:]
        daff = daff_ref[at, begin:]
        parts = []
        for e in range(2):
            decay = jnp.exp(jnp.minimum(rows[e][:, begin:] - columns[e][at], 0.0))
            parts.append(mm((decay * affinity).astype(BF), dsb[begin:], NN))
            daff = daff + mm(fed[at], chosen[e][begin:], NT) * decay
        daff_ref[at, begin:] = daff
        backs.append(jnp.where(low[at], parts[0], parts[1]))
    back = jnp.concatenate(backs, axis=0)
    inner = scanned_ref[...] - skip * values
    direct = back * values
    moved = dsb.astype(F32) * inner - fed.astype(F32) * back
    dstep, drun = dstep_ref[...], drun_ref[...]
    for e in range(2):
        half = low if e == 0 else ~low
        spot = lane == 2 * head_pair + e
        dstep = dstep + jnp.where(spot, jnp.sum(jnp.where(half, direct, 0.0), axis=1, keepdims=True), 0.0)
        drun = drun + jnp.where(spot, jnp.sum(jnp.where(half, moved, 0.0), axis=1, keepdims=True), 0.0)
    dstep_ref[...] = dstep
    drun_ref[...] = drun
    dtotal = (stepx * back + skip * ds) * dvalues
    dx, tap_grads = conv_backward(dtotal, v_ref[...], masks, taps)
    gv_ref[...] = dx.astype(BF)
    sums = tap_grads + [
        jnp.sum(dtotal, axis=0, keepdims=True),
        jnp.sum(ds * values, axis=0, keepdims=True),
        jnp.zeros((2, LANES), F32),
    ]
    at = pl.ds(pl.multiple_of(pair * LANES, LANES), LANES)
    vsum_ref[:, at] = vsum_ref[:, at] + jnp.concatenate(sums, axis=0)
    if not last:
        return

    @pl.when(pair == pl.num_programs(1) - 1)
    def _():
        _, column, seg_row = segment_masks(seg_ref)
        _, before = ordered(seg_row.shape[1])
        allowed = before & (column == seg_row)
        full = jnp.where(allowed, daff_ref[...], 0.0)
        keys, queries = act_ref[:, :LANES], act_ref[:, LANES:]
        dkeys = mm_fine(full, queries, NN)
        dqueries = mm_fine(full, keys, TN)
        for c, dside in enumerate((dkeys, dqueries)):
            lanes = slice(c * LANES, (c + 1) * LANES)
            taps_c = [taps_s_ref[k : k + 1, lanes] for k in range(KERNEL)]
            dsum = dside * silu_parts(sum_ref[:, lanes])[1]
            dside_x, taps_g = conv_backward(dsum, shared_ref[:, lanes], masks, taps_c)
            gs_ref[:, lanes] = dside_x.astype(BF)
            more = taps_g + [jnp.sum(dsum, axis=0, keepdims=True), jnp.zeros((3, LANES), F32)]
            ssum_ref[:, lanes] = ssum_ref[:, lanes] + jnp.concatenate(more, axis=0)
        ddecay = mm_ones(jnp.where(before, 1.0, 0.0).astype(BF), drun_ref[...], NN)
        rate = -head_ref[1:2, :]
        draw = (dstep_ref[...] + ddecay * rate) * jax.nn.sigmoid(raw_ref[...])
        draw = draw * head_ref[2:3, :]
        gs_ref[:, 2 * LANES :] = pltpu.roll(draw, place_ref[0] * per, 1).astype(BF)
        heads = [
            jnp.sum(draw, axis=0, keepdims=True),
            jnp.sum(ddecay * (rate * step_ref[...]), axis=0, keepdims=True) * head_ref[2:3, :],
            jnp.zeros((6, LANES), F32),
        ]
        ssum_ref[:, 2 * LANES :] = ssum_ref[:, 2 * LANES :] + jnp.concatenate(heads, axis=0)


def normgrad_kernel(groups, gz_ref, gv1_ref, gv2_ref, gs_ref, weight_ref, *outs):
    span = outs[0].shape[0]
    model = weight_ref.shape[1]
    width = 384 if model % 384 == 0 else LANES
    for r in range(groups):
        at = slice(r * span, (r + 1) * span)
        terms = jnp.concatenate([gz_ref[at, :], gv1_ref[at, :], gv2_ref[at, :], gs_ref[at, :]], axis=1)
        for n in range(model // width):
            cols = slice(n * width, (n + 1) * width)
            outs[r][:, cols] = mm(terms, weight_ref[:, cols], NN).astype(outs[r].dtype)


def final_kernel(groups, aligned, width, *refs):
    outs = refs[:groups]
    grads = refs[groups : 2 * groups]
    sums = refs[2 * groups : 3 * groups]
    place_ref, tokens_ref, normal_ref, cot_ref, gain_ref, output_ref, tgrad_ref, gnorm_ref = refs[3 * groups :]
    member = place_ref[0]
    model = gain_ref.shape[1]
    rows = model // groups
    factor = gate_scales([s[...] for s in sums], width)[0]
    total = outs[0][...].astype(F32)
    for part in outs[1:]:
        total = total + part[...].astype(F32)
    output_ref[...] = (tokens_ref[...].astype(F32) + total * factor[:, 0:1]).astype(BF)
    xs, gained, square, cross = [], [], 0.0, 0.0
    for b in range(groups):
        at = slice(b * rows, (b + 1) * rows)
        grad = grads[0][:, at].astype(F32)
        for k in range(1, groups):
            grad = grad + grads[k][:, (b ^ k) * rows : ((b ^ k) + 1) * rows].astype(F32)
        x = normal_ref[:, lane_block(aligned, member, b, rows)].astype(F32)
        more = grad * gain_ref[:, at]
        square = square + jnp.sum(x * x, axis=-1, keepdims=True)
        cross = cross + jnp.sum(more * x, axis=-1, keepdims=True)
        xs.append((x, grad))
        gained.append(more)
    scale = lax.rsqrt(square / model + EPSILON)
    bend = scale * scale * scale * (cross / model)
    for b in range(groups):
        at = slice(b * rows, (b + 1) * rows)
        x, grad = xs[b]
        lanes = lane_block(aligned, member, b, rows)
        tgrad_ref[:, lanes] = (cot_ref[:, lanes].astype(F32) + (gained[b] * scale - x * bend)).astype(BF)
        gnorm_ref[0:1, at] = jnp.sum(grad * (x * scale), axis=0, keepdims=True)


def place_kernel(pieces, groups, *refs):
    place_ref = refs[0]
    count = len(pieces)
    sources = refs[1 : 1 + 2 * count]
    out_ref, stage_ref, sems = refs[-3:]
    member, core = place_ref[0], place_ref[1]
    copies = []
    row = 0
    later = []
    for n, (half, offset, stride, shared) in enumerate(pieces):
        for which in range(2):
            whose = core if which == 0 else 1 - core
            source = sources[2 * n + which]
            for k in range(groups):
                stage_ref[row : row + half, :] = source[k * half : (k + 1) * half, :].astype(F32)
                target = offset + jnp.bitwise_xor(member, k) * stride + whose * half
                copy = pltpu.make_async_copy(
                    stage_ref.at[pl.ds(row, half), :],
                    out_ref.at[pl.ds(pl.multiple_of(target, 8), half), :],
                    sems.at[len(copies)],
                )
                copy.start()
                copies.append(copy)
                row += half
            if shared:
                part = source.shape[0] - groups * half
                begin, tail = shared
                stage_ref[row : row + part, :] = source[groups * half :, :].astype(F32)
                later.append((whose, row, begin, part, tail, len(copies) + len(later) + which))
                row += part
    for whose, row, begin, part, tail, sem in later:
        for c, size in ((0, part), (1, tail - part)):

            @pl.when(whose == c)
            def _():
                copy = pltpu.make_async_copy(
                    stage_ref.at[pl.ds(row, size), :], out_ref.at[pl.ds(begin + c * part, size), :], sems.at[sem]
                )
                copy.start()
                copy.wait()

    for copy in copies:
        copy.wait()


def place_rows(place, groups, shape, pieces, values, onto=None):
    rows = sum(v.shape[0] for v in values)
    given = [] if onto is None else [onto]
    return call(
        partial(place_kernel, pieces, groups),
        jax.ShapeDtypeStruct(shape, F32),
        rows * shape[1],
        6 * rows * shape[1],
        in_specs=[pl.BlockSpec(memory_space=pltpu.SMEM)] + [VM] * len(values) + [HBM] * len(given),
        out_specs=HBM,
        scratch_shapes=[
            pltpu.VMEM((rows, shape[1]), F32),
            pltpu.SemaphoreType.DMA((2 * len(pieces) * (groups + 2),)),
        ],
        input_output_aliases={1 + len(values): 0} if given else {},
    )(place, *values, *given)


def swap(value, axis, step):
    size = lax.axis_size(axis)
    return lax.ppermute(value, axis, [(i, i ^ step) for i in range(size)])


def rounded_sum(a, b):
    return (a.astype(F32) + b.astype(F32)).astype(BF)


def line_sum(value):
    size = lax.axis_size("rep")
    bits = size.bit_length() - 1
    last = bits - 2 if bits >= 3 else bits
    for b in range(1, last):
        value = rounded_sum(value, swap(value, "rep", 1 << b))
    if bits < 3:
        return value
    low = size // 4
    where = lax.axis_index("rep") // low
    inward = [(low * a + i, low * b + i) for a, b in ((0, 1), (3, 2)) for i in range(low)]
    middle = [(low * a + i, low * b + i) for a, b in ((1, 2), (2, 1)) for i in range(low)]
    outward = [(low * a + i, low * b + i) for a, b in ((1, 0), (2, 3)) for i in range(low)]
    got = lax.ppermute(value, "rep", inward)
    value = rounded_sum(value, got)
    got = lax.ppermute(value, "rep", middle)
    value = rounded_sum(value, got)
    back = lax.ppermute(value, "rep", outward)
    return jnp.where((where == 0) | (where == 3), back, value)


def all_sum(value):
    for axis in ("fsdp", "rep"):
        size = lax.axis_size(axis)
        step = 1
        while step < size:
            if step * 4 <= size:
                near, far, both = (swap(value, axis, step * m) for m in (1, 2, 3))
                value = (value + near) + (far + both)
                step *= 4
            else:
                value = value + swap(value, axis, step)
                step *= 2
    return value


def pick(value, index):
    return lax.dynamic_index_in_dim(value, index, 0, keepdims=False)


def to_owners(total, groups):
    rows = total.shape[1] // groups
    blocks = [total[:, k * rows : (k + 1) * rows] for k in range(groups)]
    return [blocks[0]] + [swap(blocks[k], "fsdp", k) for k in range(1, groups)]


def core_sum(value, core):
    got = swap(pick(value, 1 - core), "rep", 1)
    return rounded_sum(pick(value, core), got)


def body(
    tokens,
    segment_ids,
    cotangent,
    norm_gain,
    in_weight,
    conv_weight,
    conv_bias,
    step_bias,
    rate_log,
    skip_gain,
    gate_gain,
    out_weight,
):
    groups = lax.axis_size("fsdp")
    member = lax.axis_index("fsdp")
    core = lax.axis_index("rep") % 2
    span, model = tokens.shape
    per = HEADS // groups
    inner = per * HEADDIM
    full = inner * groups
    conv = conv_bias.shape[0] * groups
    tail = in_weight.shape[1] - 2 * full
    padded = -(-tail // 384) * 384
    width = 2 * inner + padded
    pairs = per // 2
    whole = groups * span
    place = jnp.stack([member, core]).astype(jnp.int32)

    rows = in_weight.shape[0]
    aligned = rows % LANES == 0
    cols = conv // groups
    smem = pl.BlockSpec(memory_space=pltpu.SMEM)
    weight_t = in_weight.T

    xs = [tokens] + [swap(tokens, "fsdp", k) for k in range(1, groups)]
    small_width = -(-max(rows, cols, span) // LANES) * LANES
    packed = call(
        partial(pack_kernel, groups),
        tuple(jax.ShapeDtypeStruct((width // 2, rows), BF) for _ in range(1, groups))
        + (jax.ShapeDtypeStruct((8, small_width), F32),),
        1,
        4 * width * rows * groups,
        in_specs=[smem, HBM] + [VM] * 4,
        out_specs=(VM,) * groups,
        scratch_shapes=[pltpu.SemaphoreType.DMA((3 * groups,))],
    )(place, weight_t, norm_gain.reshape(1, -1), conv_weight, conv_bias.reshape(1, -1), segment_ids)
    near = [swap(packed[k - 1], "fsdp", k) for k in range(1, groups)]
    small = [packed[-1]] + [swap(packed[-1], "fsdp", k) for k in range(1, groups)]
    far = [swap(n, "rep", 1) for n in near]
    late, _ = lax.optimization_barrier((cotangent, (near[-1], xs[-1])))
    cots = [cotangent] + [swap(late, "fsdp", k) for k in range(1, groups)]

    gain_x = jnp.concatenate([t[0:1, :rows] for t in small], axis=1)
    order = jnp.arange(groups) ^ member
    table = jnp.take(jnp.stack(small), order, axis=0)
    taps_full = jnp.swapaxes(table[:, 1 : 2 + KERNEL, :cols], 0, 1).reshape(KERNEL + 1, conv)
    own_heads = lambda v: lax.dynamic_slice_in_dim(v.astype(F32), member * per, per, 0)
    taps_v = jnp.concatenate(
        [
            lax.dynamic_slice_in_dim(taps_full, member * inner, inner, 1),
            jnp.repeat(own_heads(skip_gain), HEADDIM).reshape(1, inner),
            gate_gain.astype(F32).reshape(1, inner),
            jnp.zeros((1, inner), F32),
        ],
        axis=0,
    )
    taps_s = jnp.concatenate([taps_full[:, full:], jnp.zeros((3, conv - full), F32)], axis=0)
    spread = lambda v: jnp.pad(v, (0, LANES - per)).reshape(1, LANES)
    heads = jnp.concatenate(
        [
            spread(own_heads(step_bias)),
            spread(jnp.exp(own_heads(rate_log))),
            spread(jnp.ones((per,), F32)),
            jnp.zeros((5, LANES), F32),
        ],
        axis=0,
    )
    segs = jnp.concatenate(
        [jnp.broadcast_to(s[2 + KERNEL : 3 + KERNEL, :span], (8, span)) for s in small], axis=0
    )

    def in_peer_order(value):
        if aligned:
            return value
        return jnp.take(value.reshape(value.shape[0], groups, rows), order, axis=1).reshape(value.shape)

    if aligned:
        sources = [weight_t] + near + far
    else:
        both = lambda n, f: jnp.where(core == 0, jnp.stack([n, f]), jnp.stack([f, n]))

        def block(n, f):
            two = both(n, f)
            z, v, t = two[:, : inner // 2], two[:, inner // 2 : inner], two[:, inner:]
            return jnp.concatenate([u.reshape(-1, rows) for u in (z, v, t)], axis=0)

        mine = jnp.concatenate(
            [
                lax.dynamic_slice_in_dim(weight_t, member * inner, inner, 0),
                lax.dynamic_slice_in_dim(weight_t, full + member * inner, inner, 0),
                jnp.pad(weight_t[2 * full :], ((0, padded - tail), (0, 0))),
            ],
            axis=0,
        )
        sources = [jnp.concatenate([mine] + [block(n, f) for n, f in zip(near, far)], axis=1)]
    sems = pltpu.SemaphoreType.DMA((6 * groups,))
    normed, projected, weight = call(
        partial(inproj_kernel, groups, aligned),
        (
            jax.ShapeDtypeStruct((whole, model), BF),
            jax.ShapeDtypeStruct((whole, width), F32),
            jax.ShapeDtypeStruct((width, model), BF),
        ),
        2 * whole * model * width,
        4 * whole * width + 4 * model * width + 4 * whole * model,
        in_specs=[VM] * groups + [VM, smem] + [HBM] * len(sources),
        out_specs=(VM, VM, VM),
        scratch_shapes=[sems],
    )(*[in_peer_order(x) for x in xs], gain_x, place, *sources)

    tile = lambda col: pl.BlockSpec((span, LANES), lambda r, p: (r, col + p))
    per_row = lambda cols_, col: pl.BlockSpec((span, cols_), lambda r, p: (r, col))
    fixed = lambda shape: pl.BlockSpec(shape, lambda r, p: (0, 0))
    pair_cols = pl.BlockSpec((8, LANES), lambda r, p: (0, p))
    seg_spec = pl.BlockSpec((8, span), lambda r, p: (r, 0))
    shared_spec = per_row(padded, 2 * inner // padded)
    scan_flops = 4 * whole * span * inner
    side = lambda w: jax.ShapeDtypeStruct((whole, w), F32)
    flipped_spec = pl.BlockSpec((LANES, span), lambda r, p: (r, 0))
    kept_shapes = (
        side((KERNEL - 1) * LANES),
        side(span),
        side(LANES),
        side(LANES),
        jax.ShapeDtypeStruct((groups * LANES, span), F32),
        side(LANES),
        side(2 * LANES),
        side(2 * LANES),
    )
    kept_specs = (
        per_row((KERNEL - 1) * LANES, 0),
        per_row(span, 0),
        per_row(LANES, 0),
        per_row(LANES, 0),
        flipped_spec,
        per_row(LANES, 0),
        per_row(2 * LANES, 0),
        per_row(2 * LANES, 0),
    )
    scanned, totals, gated, squares, *kept = call(
        partial(forward_kernel, per),
        (
            side(inner),
            side(inner),
            jax.ShapeDtypeStruct((whole, inner), BF),
            jax.ShapeDtypeStruct((8 * groups, span), F32),
        )
        + kept_shapes,
        8 * scan_flops,
        20 * whole * inner,
        mib=12,
        grid=(groups, pairs),
        in_specs=[
            smem,
            tile(0),
            tile(pairs),
            shared_spec,
            seg_spec,
            fixed((8, conv - full)),
            pair_cols,
            fixed((8, LANES)),
        ],
        out_specs=(tile(0), tile(0), tile(0), seg_spec) + kept_specs,
        scratch_shapes=[pltpu.VMEM((span, span), F32), pltpu.VMEM((span, LANES), F32)],
    )(place, projected, projected, projected, segs, taps_s, taps_v, heads)

    proj_flops = 2 * whole * inner * model
    dm, sums = call(
        partial(mixgrad_kernel, groups),
        (jax.ShapeDtypeStruct((whole, inner), F32), jax.ShapeDtypeStruct((8 * groups, span), F32)),
        proj_flops,
        2 * whole * model + 6 * whole * inner + 2 * inner * model,
        in_specs=[VM] * (groups + 3),
        out_specs=(VM, VM),
    )(*cots, out_weight, gated, squares)
    sums_all = [sums] + [swap(sums, "fsdp", k) for k in range(1, groups)]

    outs = call(
        partial(outproj_kernel, groups),
        tuple(jax.ShapeDtypeStruct((span, model), BF if k else F32) for k in range(groups)),
        proj_flops,
        2 * whole * model + 2 * whole * inner + 2 * inner * model,
        in_specs=[VM, VM],
        out_specs=(VM,) * groups,
    )(gated, out_weight)
    outs = [outs[0]] + [swap(outs[k], "fsdp", k) for k in range(1, groups)]

    row_spec = lambda cols_, col=0: pl.BlockSpec((span, cols_), lambda r: (r, col))
    gz, ds, mixed, gate_sum = call(
        partial(gatebwd_kernel, groups, float(full)),
        (
            jax.ShapeDtypeStruct((whole, inner), BF),
            jax.ShapeDtypeStruct((whole, inner), F32),
            jax.ShapeDtypeStruct((whole, inner), BF),
            jax.ShapeDtypeStruct((8, inner), F32),
        ),
        20 * whole * inner,
        20 * whole * inner,
        mib=16,
        grid=(groups,),
        in_specs=[
            pl.BlockSpec((8, span), (lambda k: lambda r: (jnp.bitwise_xor(r, k), 0))(k)) for k in range(groups)
        ]
        + [row_spec(inner), row_spec(inner), row_spec(inner), pl.BlockSpec((8, inner), lambda r: (0, 0))],
        out_specs=(
            row_spec(inner),
            row_spec(inner),
            row_spec(inner),
            pl.BlockSpec((8, inner), lambda r: (0, 0)),
        ),
    )(*sums_all, projected, scanned, dm, jnp.broadcast_to(gate_gain.astype(F32).reshape(1, inner), (8, inner)))

    cot_all = jnp.concatenate(cots, axis=0)
    grad_out = lax.dot_general(mixed, cot_all, TN, preferred_element_type=F32).astype(BF)
    grad_z = lax.dot_general(gz, normed, TN, preferred_element_type=F32).astype(BF)
    out_part = line_sum(core_sum(grad_out.reshape(2, inner // 2, model), core))
    z_sum = core_sum(grad_z.reshape(2, inner // 2, model), core)
    z_part = line_sum(jnp.concatenate(to_owners(z_sum, groups), axis=0))

    third = pairs // 3
    cuts = (0, third, 2 * third, pairs)
    split = cuts[2]
    carry_shapes = (side(span), side(LANES), side(LANES))
    carry_specs = (per_row(span, 0), per_row(LANES, 0), per_row(LANES, 0))

    def backward(n, carry):
        first, count, last = cuts[n], cuts[n + 1] - cuts[n], n == 2
        cols_ = count * LANES
        outs_ = (jax.ShapeDtypeStruct((whole, cols_), BF), jax.ShapeDtypeStruct((8, cols_), F32))
        specs_ = (tile(0), fixed((8, cols_)))
        scratch, more, more_specs = [], [], []
        if last:
            outs_ += (jax.ShapeDtypeStruct((whole, padded), BF), jax.ShapeDtypeStruct((8, padded), F32))
            specs_ += (per_row(padded, 0), fixed((8, padded)))
            scratch = [
                pltpu.VMEM((span, span), F32),
                pltpu.VMEM((span, LANES), F32),
                pltpu.VMEM((span, LANES), F32),
            ]
            more = [projected, kept[5], kept[6], kept[7], segs, taps_s, heads, place]
            more_specs = [shared_spec, kept_specs[5], kept_specs[6], kept_specs[7], seg_spec]
            more_specs += [fixed((8, conv - full)), fixed((8, LANES)), smem]
        else:
            outs_ += carry_shapes
            specs_ += carry_specs
        return call(
            partial(backward_kernel, per, first, last, len(carry) > 0),
            outs_,
            16 * scan_flops * count // pairs,
            24 * whole * cols_,
            mib=12,
            grid=(groups, count),
            in_specs=[tile(first), tile(pairs + first), tile(first), tile(first)]
            + list(kept_specs[:5])
            + [pl.BlockSpec((8, LANES), lambda r, p: (0, first + p))]
            + (list(carry_specs) if carry else [])
            + more_specs,
            out_specs=specs_,
            scratch_shapes=scratch,
        )(ds, projected, totals, scanned, *kept[:5], taps_v, *carry, *more)

    gva, vsum1, *handed = backward(0, ())
    gvb, vsum2, *handed = backward(1, handed)
    gv1 = jnp.concatenate([gva, gvb], axis=1)
    grad_v1 = lax.dot_general(gv1, normed, TN, preferred_element_type=F32).astype(BF)
    gv2, vsum3, gs, ssum = backward(2, handed)
    vsum = jnp.concatenate([vsum1, vsum2, vsum3], axis=1)

    backs = call(
        partial(normgrad_kernel, groups),
        tuple(jax.ShapeDtypeStruct((span, model), BF if k else F32) for k in range(groups)),
        2 * whole * width * model,
        2 * whole * model + 2 * whole * width + 2 * width * model,
        in_specs=[VM] * 5,
        out_specs=(VM,) * groups,
    )(gz, gv1, gv2, gs, weight)
    backs = [backs[0]] + [swap(backs[k], "fsdp", k) for k in range(1, groups)]

    v1_sum = core_sum(grad_v1.reshape(2, split * HEADDIM, model), core)
    v1_part = line_sum(jnp.concatenate(to_owners(v1_sum, groups), axis=0))
    grad_v2 = lax.dot_general(gv2, normed, TN, preferred_element_type=F32).astype(BF)
    grad_s = lax.dot_general(gs, normed, TN, preferred_element_type=F32).astype(BF)
    deep = (pairs - split) * HEADDIM
    both = jnp.concatenate([grad_v2.reshape(2, deep, model), grad_s.reshape(2, padded // 2, model)], axis=1)
    terms = to_owners(core_sum(both, core), groups)
    shared_sum = terms[0][deep:].astype(F32)
    for term in terms[1:]:
        shared_sum = shared_sum + term[deep:].astype(F32)
    s_part = line_sum(jnp.concatenate([t[:deep] for t in terms] + [shared_sum.astype(BF)], axis=0))

    whole_spec = lambda shape: pl.BlockSpec(shape, lambda i: (0,) * len(shape))
    output, tokens_grad, norm_sum = call(
        partial(final_kernel, groups, aligned, float(full)),
        (
            jax.ShapeDtypeStruct((span, model), BF),
            jax.ShapeDtypeStruct((span, model), BF),
            jax.ShapeDtypeStruct((8, model), F32),
        ),
        30 * span * model,
        24 * span * model,
        grid=(1,),
        in_specs=[whole_spec((span, model))] * (2 * groups)
        + [pl.BlockSpec((8, span), (lambda k: lambda i: (k, 0))(k)) for k in range(groups)]
        + [smem]
        + [whole_spec((span, model))] * 3
        + [whole_spec((1, model))],
        out_specs=(whole_spec((span, model)), whole_spec((span, model)), whole_spec((8, model))),
    )(*outs, *backs, *sums_all, place, tokens, in_peer_order(tokens), in_peer_order(cotangent), gain_x)
    tokens_grad = in_peer_order(tokens_grad)
    norm_sum = jnp.take(norm_sum[0].reshape(groups, rows), order, axis=0).reshape(1, model)

    def returned(part):
        return [part, swap(part, "rep", 1)]

    grad_outproj = place_rows(place, 1, out_weight.shape, ((inner // 2, 0, 0, None),), returned(out_part))
    early = returned(z_part) + returned(v1_part)
    gin = place_rows(
        place, groups, weight_t.shape, ((inner // 2, 0, inner, None), (split * HEADDIM, full, inner, None)), early
    )
    grad_inproj = place_rows(
        place,
        groups,
        weight_t.shape,
        ((deep, full + split * 2 * HEADDIM, inner, (2 * full, tail)),),
        returned(s_part),
        gin,
    ).T

    own_cols = lambda v: lax.dynamic_update_slice_in_dim(
        jnp.zeros((v.shape[0], full), F32), v, member * inner, 1
    )
    own_spot = lambda v: lax.dynamic_update_slice_in_dim(jnp.zeros((HEADS,), F32), v, member * per, 0)
    taps_grad = jnp.concatenate([own_cols(vsum[: KERNEL + 1]), ssum[: KERNEL + 1, : conv - full]], axis=1)
    head_grads = [
        own_spot(ssum[0, 2 * LANES : 2 * LANES + per]),
        own_spot(ssum[1, 2 * LANES : 2 * LANES + per]),
        own_spot(vsum[KERNEL + 1].reshape(per, HEADDIM).sum(axis=1)),
    ]
    flat = jnp.concatenate(
        [norm_sum[0], taps_grad.reshape(-1), own_cols(gate_sum[:1]).reshape(-1)] + head_grads
    )
    length = flat.shape[0]
    flat = jnp.pad(flat, (0, -length % 1024)).reshape(-1, LANES)
    flat = all_sum(flat).reshape(-1)
    at = 0
    grad_norm = lax.dynamic_slice_in_dim(flat, member * rows, rows, 0)
    at += model
    taps_all = flat[at : at + (KERNEL + 1) * conv].reshape(KERNEL + 1, conv)
    taps_own = lax.dynamic_slice_in_dim(taps_all, member * cols, cols, 1)
    at += (KERNEL + 1) * conv
    grad_gate = lax.dynamic_slice_in_dim(flat, at + member * inner, inner, 0)
    at += full
    return (
        output,
        tokens_grad,
        grad_norm,
        grad_inproj,
        taps_own[:KERNEL],
        taps_own[KERNEL],
        flat[at : at + HEADS],
        flat[at + HEADS : at + 2 * HEADS],
        flat[at + 2 * HEADS : at + 3 * HEADS],
        grad_gate,
        grad_outproj,
    )


def solution(mesh):
    rows = P(("rep", "fsdp"), None)
    in_specs = (
        rows,
        rows,
        rows,
        P("fsdp"),
        P("fsdp", None),
        P(None, "fsdp"),
        P("fsdp"),
        P(),
        P(),
        P(),
        P("fsdp"),
        P("fsdp", None),
    )
    out_specs = (
        rows,
        rows,
        P("fsdp"),
        P("fsdp", None),
        P(None, "fsdp"),
        P("fsdp"),
        P(),
        P(),
        P(),
        P("fsdp"),
        P("fsdp", None),
    )

    return jax.shard_map(body, mesh=mesh, in_specs=in_specs, out_specs=out_specs, check_vma=False)
```

```python
from functools import partial

import jax
import jax.numpy as jnp
from jax import lax
from jax.experimental import pallas as pl
from jax.experimental.pallas import tpu as pltpu
from jax.sharding import PartitionSpec as P


HEADS = 48
HEADDIM = 64
KERNEL = 4
LANES = 128
EPSILON = 1e-05
BF = jnp.bfloat16
F32 = jnp.float32

NN = (((1,), (0,)), ((), ()))
NT = (((1,), (1,)), ((), ()))
TN = (((0,), (0,)), ((), ()))


def mm(a, b, dims):
    return lax.dot_general(a, b, dims, preferred_element_type=F32)


def halves(x):
    top = x.astype(BF)
    return top, (x - top.astype(F32)).astype(BF)


def mm_fine(a, b, dims):
    a_top, a_low = halves(a)
    b_top, b_low = halves(b)
    return mm(a_top, b_top, dims) + (mm(a_top, b_low, dims) + mm(a_low, b_top, dims))


def mm_ones(ones, x, dims):
    top, low = halves(x)
    rest = (x - top.astype(F32) - low.astype(F32)).astype(BF)
    parts = mm(ones, jnp.concatenate([top, low, rest], axis=1), dims)
    lanes = x.shape[1]
    return parts[:, :lanes] + (parts[:, lanes : 2 * lanes] + parts[:, 2 * lanes :])


def sigmoid(v):
    return 0.5 * jnp.tanh(0.5 * v) + 0.5


def silu_parts(v):
    gate = sigmoid(v)
    return v * gate, gate * (1.0 + v * (1.0 - gate))


def call(kernel, out_shape, flops, moved, mib=None, **kw):
    grant = (mib or 4 * lax.axis_size("fsdp")) * 1024 * 1024

    def run(*operands):
        return pl.pallas_call(
            kernel,
            out_shape=out_shape,
            cost_estimate=pl.CostEstimate(flops=flops, bytes_accessed=moved, transcendentals=0),
            compiler_params=pltpu.CompilerParams(vmem_limit_bytes=grant),
            **kw,
        )(*operands)

    return run


VM = pl.BlockSpec(memory_space=pltpu.VMEM)
HBM = pl.BlockSpec(memory_space=pl.ANY)


def pack_kernel(groups, *refs):
    place_ref, weight_ref, gain_ref, taps_ref, shift_ref, seg_ref = refs[:6]
    sends = refs[6 : 5 + groups]
    small_ref, sems = refs[5 + groups :]
    member, quarter = place_ref[0], place_ref[2]
    inner, share, edge, part, tail = quarter_sizes(sends[0].shape[0], weight_ref.shape[0], groups)
    copies = []
    for k in range(1, groups):
        peer = jnp.bitwise_xor(member, k)
        for i in range(2):
            source = pl.multiple_of(i * (edge // 2) + peer * inner + quarter * share, 16)
            copies.append(
                pltpu.make_async_copy(
                    weight_ref.at[pl.ds(source, share), :],
                    sends[k - 1].at[pl.ds(i * share, share), :],
                    sems.at[2 * k - 2 + i],
                )
            )
    for copy in copies:
        copy.start()
    for q in range(4):
        count = max(0, min(part, tail - q * part))

        @pl.when(quarter == q)
        def _():
            more = [
                pltpu.make_async_copy(
                    weight_ref.at[pl.ds(edge + q * part, count), :],
                    sends[k - 1].at[pl.ds(2 * share, count), :],
                    sems.at[2 * groups - 3 + k],
                )
                for k in range(1, groups)
                if count > 0
            ]
            for copy in more:
                copy.start()
            if count < part:
                for k in range(1, groups):
                    sends[k - 1][2 * share + count :, :] = jnp.zeros((part - count, weight_ref.shape[1]), BF)
            for copy in more:
                copy.wait()

    small_ref[...] = jnp.zeros_like(small_ref)
    small_ref[0:1, : gain_ref.shape[1]] = gain_ref[...].astype(F32)
    small_ref[1 : 1 + KERNEL, : taps_ref.shape[1]] = taps_ref[...].astype(F32)
    small_ref[1 + KERNEL : 2 + KERNEL, : shift_ref.shape[1]] = shift_ref[...].astype(F32)
    small_ref[2 + KERNEL : 3 + KERNEL, : seg_ref.shape[1]] = seg_ref[...].astype(F32)
    for copy in copies:
        copy.wait()


def copy_kernel(source_ref, target_ref):
    target_ref[...] = source_ref[...]


def quarter_sizes(sent, columns, groups):
    full = HEADS * HEADDIM
    inner = full // groups
    return inner, inner // 4, 2 * full, sent - inner // 2, columns - 2 * full


def inproj_kernel(groups, aligned, *refs):
    tokens = refs[:groups]
    gain_ref, place_ref, own_ref = refs[groups : groups + 3]
    given = refs[groups + 3 : -7]
    normed_ref, proj_ref, weight_out_ref, token_ref, weight_ref, sems, token_sems = refs[-7:]
    member, quarter = place_ref[0], place_ref[2]
    model = gain_ref.shape[1]
    rows = model // groups
    span = tokens[0].shape[0]
    loads = [pltpu.make_async_copy(tokens[r], token_ref.at[r], token_sems.at[r]) for r in range(groups)]
    for load in loads:
        load.start()
    copies = []
    if aligned:
        sent = given[0].shape[0] // (groups - 1)
        inner, share, edge, part, tail = quarter_sizes(sent, own_ref.shape[0], groups)
        for i, (source, count) in enumerate(
            ((member * inner, inner), (edge // 2 + member * inner, inner), (edge, tail))
        ):
            copies.append(
                pltpu.make_async_copy(
                    own_ref.at[pl.ds(pl.multiple_of(source, 16), count), :],
                    weight_ref.at[pl.ds(i * inner, count), pl.ds(0, rows)],
                    sems.at[i],
                )
            )
        for n, piece in enumerate(given):
            whose = jnp.bitwise_xor(quarter, n)
            for k in range(1, groups):
                for i, count in enumerate((share, share, part)):
                    target = pl.multiple_of(i * inner + whose * count, 16)
                    copies.append(
                        pltpu.make_async_copy(
                            piece.at[pl.ds((k - 1) * sent + i * share, count), :],
                            weight_ref.at[pl.ds(target, count), pl.ds(k * rows, rows)],
                            sems.at[len(copies)],
                        )
                    )
    else:
        copies.append(pltpu.make_async_copy(own_ref, weight_ref, sems.at[0]))
    for copy in copies:
        copy.start()
    if aligned and part * 4 > tail:
        weight_ref[2 * inner + tail :, 0:rows] = jnp.zeros((4 * part - tail, rows), BF)
    for r in range(groups):
        loads[r].wait()
        blocks = [token_ref[r, :, lane_block(aligned, member, k, rows)].astype(F32) for k in range(groups)]
        total = jnp.sum(blocks[0] * blocks[0], axis=-1, keepdims=True)
        for x in blocks[1:]:
            total = total + jnp.sum(x * x, axis=-1, keepdims=True)
        factor = lax.rsqrt(total / model + EPSILON)
        for k in range(groups):
            at = slice(k * rows, (k + 1) * rows)
            normed_ref[r * span : (r + 1) * span, at] = (blocks[k] * factor * gain_ref[:, at]).astype(BF)
    for copy in copies:
        copy.wait()
    keep = pltpu.make_async_copy(weight_ref, weight_out_ref, sems.at[0])
    keep.start()
    width = 384
    total = weight_ref.shape[0] // width

    def column(n, carry):
        at = pl.multiple_of(n * width, LANES)
        for r in range(groups):
            proj_ref[r * span : (r + 1) * span, pl.ds(at, width)] = mm(
                normed_ref[r * span : (r + 1) * span, :], weight_ref[pl.ds(at, width), :], NT
            )
        return carry

    lax.fori_loop(0, total, column, 0)
    keep.wait()


def lane_block(aligned, member, k, rows):
    if aligned:
        return pl.ds(pl.multiple_of(jnp.bitwise_xor(member, k) * rows, LANES), rows)
    return slice(k * rows, (k + 1) * rows)


def conv_forward(x, masks, taps, shift):
    total = shift + taps[KERNEL - 1] * x
    for s in range(1, KERNEL):
        total = total + taps[KERNEL - 1 - s] * (pltpu.roll(x, s, 0) * masks[s - 1])
    return total


def conv_backward(grad, x, masks, taps):
    span = x.shape[0]
    back = taps[KERNEL - 1] * grad
    tap_grads = [None] * KERNEL
    tap_grads[KERNEL - 1] = jnp.sum(grad * x, axis=0, keepdims=True)
    for s in range(1, KERNEL):
        part = grad * masks[s - 1]
        back = back + taps[KERNEL - 1 - s] * pltpu.roll(part, span - s, 0)
        tap_grads[KERNEL - 1 - s] = jnp.sum(part * pltpu.roll(x, s, 0), axis=0, keepdims=True)
    return back, tap_grads


def wide(column, count):
    return jnp.concatenate([column] * (count // LANES), axis=1)


def segment_masks(seg_ref):
    span = seg_ref.shape[-1]
    row = seg_ref[0:1, :]
    column = jnp.broadcast_to(row, (LANES, span)).T
    token = lax.broadcasted_iota(jnp.int32, (span, LANES), 0)
    masks = []
    for s in range(1, KERNEL):
        same = (pltpu.roll(column, s, 0) == column) & (token >= s)
        masks.append(jnp.where(same, 1.0, 0.0))
    return masks, wide(column, span), row


def ordered(span):
    i = lax.broadcasted_iota(jnp.int32, (span, span), 0)
    j = lax.broadcasted_iota(jnp.int32, (span, span), 1)
    return i >= j, i <= j


def row_setup(shared_ref, seg_ref, taps_ref, head_ref, member, per, affinity_ref, kept):
    mask_ref, afft_ref, step_ref, run_ref, runt_ref, raw_ref, act_ref, sum_ref = kept
    masks, column, row = segment_masks(seg_ref)
    after, _ = ordered(row.shape[1])
    for s in range(KERNEL - 1):
        mask_ref[:, s * LANES : (s + 1) * LANES] = masks[s]
    outs = []
    for c in range(2):
        at = slice(c * LANES, (c + 1) * LANES)
        taps = [taps_ref[k : k + 1, at] for k in range(KERNEL)]
        total = conv_forward(shared_ref[:, at], masks, taps, taps_ref[KERNEL : KERNEL + 1, at])
        active = total * sigmoid(total)
        outs.append(active)
        sum_ref[:, at] = total
        act_ref[:, at] = active
    affinity = jnp.where(after & (column == row), mm_fine(outs[1], outs[0], NT), 0.0)
    affinity_ref[...] = affinity
    afft_ref[...] = affinity.T
    raw = pltpu.roll(shared_ref[:, 2 * LANES :], lax.rem(LANES - member * per, LANES), 1)
    raw = raw + head_ref[0:1, :]
    step = jnp.maximum(raw, 0.0) + jnp.log1p(jnp.exp(-jnp.abs(raw)))
    run = mm_ones(jnp.where(after, 1.0, 0.0).astype(BF), -head_ref[1:2, :] * step, NN)
    raw_ref[...] = raw
    step_ref[...] = step
    run_ref[...] = run
    runt_ref[...] = run.T


def pair_columns(pair, run_ref, runt_ref, step_ref):
    back = lax.rem(LANES - 2 * pair, LANES)
    runs = pltpu.roll(run_ref[...], back, 1)
    steps = pltpu.roll(step_ref[...], back, 1)
    lane = lax.broadcasted_iota(jnp.int32, runs.shape, 1)
    low = lane < HEADDIM
    stepx = jnp.where(low, steps[:, 0:1], steps[:, 1:2])
    columns = [runs[:, e : e + 1] for e in range(2)]
    rows = [runt_ref[pl.ds(2 * pair + e, 1), :] for e in range(2)]
    return columns, rows, stepx, low, lane


def forward_kernel(
    per,
    place_ref,
    z_ref,
    v_ref,
    shared_ref,
    seg_ref,
    taps_s_ref,
    taps_v_ref,
    head_ref,
    scanned_ref,
    total_ref,
    gated_ref,
    square_ref,
    mask_ref,
    afft_ref,
    step_ref,
    run_ref,
    runt_ref,
    raw_ref,
    act_ref,
    sum_ref,
    affinity_ref,
    square_sum_ref,
):
    pair = pl.program_id(1)

    @pl.when(pair == 0)
    def _():
        kept = (mask_ref, afft_ref, step_ref, run_ref, runt_ref, raw_ref, act_ref, sum_ref)
        row_setup(shared_ref, seg_ref, taps_s_ref, head_ref, place_ref[0], per, affinity_ref, kept)
        square_sum_ref[...] = jnp.zeros_like(square_sum_ref)

    masks = [mask_ref[:, s * LANES : (s + 1) * LANES] for s in range(KERNEL - 1)]
    taps = [taps_v_ref[k : k + 1, :] for k in range(KERNEL)]
    total = conv_forward(v_ref[...], masks, taps, taps_v_ref[KERNEL : KERNEL + 1, :])
    total_ref[...] = total
    values = total * sigmoid(total)
    columns, rows, stepx, low, _ = pair_columns(pair, run_ref, runt_ref, step_ref)
    fed = (stepx * values).astype(BF)
    skipped = taps_v_ref[KERNEL + 1 : KERNEL + 2, :] * values
    cut = fed.shape[0] // 2
    for n in range(2):
        at = slice(n * cut, (n + 1) * cut)
        seen = (n + 1) * cut
        affinity = affinity_ref[at, :seen]
        parts = []
        for e in range(2):
            decay = jnp.exp(jnp.minimum(columns[e][at] - rows[e][:, :seen], 0.0))
            parts.append(mm((decay * affinity).astype(BF), fed[:seen], NN))
        scanned = jnp.where(low[at], parts[0], parts[1]) + skipped[at]
        z = z_ref[at, :]
        g = scanned * (z * sigmoid(z))
        scanned_ref[at, :] = scanned
        gated_ref[at, :] = (g * taps_v_ref[KERNEL + 2 : KERNEL + 3, :]).astype(BF)
        square_sum_ref[at, :] = square_sum_ref[at, :] + g * g

    @pl.when(pair == pl.num_programs(1) - 1)
    def _():
        row = jnp.sum(square_sum_ref[...].T, axis=0, keepdims=True)
        square_ref[...] = jnp.broadcast_to(row, square_ref.shape)


def mixgrad_kernel(groups, *refs):
    cots = refs[:groups]
    out_w_ref, gated_ref, square_ref, dm_ref, sums_ref = refs[groups:]
    span = cots[0].shape[0]
    width = 384 if out_w_ref.shape[0] % 384 == 0 else LANES

    def column(n, carry):
        cols = pl.ds(pl.multiple_of(n * width, LANES), width)
        weight = out_w_ref[cols, :]
        for r in range(groups):
            dm_ref[r * span : (r + 1) * span, cols] = mm(cots[r][...], weight, NT)
        return carry

    lax.fori_loop(0, out_w_ref.shape[0] // width, column, 0)
    for r in range(groups):
        at = slice(r * span, (r + 1) * span)
        prod = dm_ref[at, :] * gated_ref[at, :].astype(F32)
        part = prod[:, :LANES]
        for c in range(1, prod.shape[1] // LANES):
            part = part + prod[:, c * LANES : (c + 1) * LANES]
        row = jnp.sum(part.T, axis=0, keepdims=True)
        sub = lax.broadcasted_iota(jnp.int32, (8, span), 0)
        sums_ref[8 * r : 8 * r + 8, :] = jnp.where(sub == 0, square_ref[8 * r : 8 * r + 8, :], row)


def outproj_kernel(groups, gated_ref, out_w_ref, *outs):
    span, model = outs[0].shape
    width = 384 if model % 384 == 0 else LANES

    def column(n, carry):
        cols = pl.ds(pl.multiple_of(n * width, LANES), width)
        weight = out_w_ref[:, cols]
        for r in range(groups):
            outs[r][:, cols] = mm(gated_ref[r * span : (r + 1) * span, :], weight, NN).astype(outs[r].dtype)
        return carry

    lax.fori_loop(0, model // width, column, 0)


def gate_scales(parts, width):
    total = parts[0]
    for part in parts[1:]:
        total = total + part
    square, cross = total[0:1, :], total[1:2, :]
    factor = lax.rsqrt(square / width + EPSILON)
    bend = factor * factor * factor * (cross / width)
    span = total.shape[1]
    return (
        jnp.broadcast_to(factor, (LANES, span)).T,
        jnp.broadcast_to(bend, (LANES, span)).T,
    )


def gatebwd_kernel(groups, width, *refs):
    sums = refs[:groups]
    z_ref, scanned_ref, dm_ref, gain_ref, gz_ref, ds_ref, mixed_ref, gate_ref = refs[groups:]
    r = pl.program_id(0)
    factor, bend = gate_scales([s[...] for s in sums], width)

    @pl.when(r == 0)
    def _():
        gate_ref[...] = jnp.zeros_like(gate_ref)

    for c in range(z_ref.shape[1] // LANES):
        at = slice(c * LANES, (c + 1) * LANES)
        gain = gain_ref[0:1, at]
        sz, dsz = silu_parts(z_ref[:, at])
        scanned = scanned_ref[:, at]
        dm = dm_ref[:, at]
        g = scanned * sz
        scaled = g * factor
        dg = factor * (dm * gain) - g * bend
        mixed_ref[:, at] = (scaled * gain).astype(BF)
        gz_ref[:, at] = (dg * scanned * dsz).astype(BF)
        ds_ref[:, at] = dg * sz
        gate_ref[0:1, at] += jnp.sum(dm * scaled, axis=0, keepdims=True)


def backward_kernel(per, first, last, carried, *refs):
    (ds_ref, v_ref, total_in_ref, scanned_ref, mask_ref, afft_ref, step_ref, run_ref, runt_ref, taps_v_ref) = refs[:10]
    refs = refs[10:]
    if carried:
        carry, refs = refs[:3], refs[3:]
    if last:
        (shared_ref, raw_ref, act_ref, sum_ref, seg_ref, taps_s_ref, head_ref, place_ref) = refs[:8]
        gv_ref, vsum_ref, gs_ref, ssum_ref, daff_ref, dstep_ref, drun_ref = refs[8:]
    else:
        gv_ref, vsum_ref, daff_ref, dstep_ref, drun_ref = refs
    row, pair = pl.program_id(0), pl.program_id(1)
    head_pair = pair + first

    @pl.when((row == 0) & (pair == 0))
    def _():
        vsum_ref[...] = jnp.zeros_like(vsum_ref)
        if last:
            ssum_ref[...] = jnp.zeros_like(ssum_ref)

    @pl.when(pair == 0)
    def _():
        for n, target in enumerate((daff_ref, dstep_ref, drun_ref)):
            target[...] = carry[n][...] if carried else jnp.zeros_like(target)

    masks = [mask_ref[:, s * LANES : (s + 1) * LANES] for s in range(KERNEL - 1)]
    taps = [taps_v_ref[k : k + 1, :] for k in range(KERNEL)]
    skip = taps_v_ref[KERNEL + 1 : KERNEL + 2, :]
    values, dvalues = silu_parts(total_in_ref[...])
    columns, rows, stepx, low, lane = pair_columns(head_pair, run_ref, runt_ref, step_ref)
    ds = ds_ref[...]
    dsb = ds.astype(BF)
    fed = (stepx * values).astype(BF)
    zero = jnp.zeros_like(dsb)
    chosen = [jnp.where(low, dsb, zero), jnp.where(low, zero, dsb)]
    cut = fed.shape[0] // 2
    backs = []
    for n in range(2):
        at = slice(n * cut, (n + 1) * cut)
        begin = n * cut
        affinity = afft_ref[at, begin:]
        daff = daff_ref[at, begin:]
        parts = []
        for e in range(2):
            decay = jnp.exp(jnp.minimum(rows[e][:, begin:] - columns[e][at], 0.0))
            parts.append(mm((decay * affinity).astype(BF), dsb[begin:], NN))
            daff = daff + mm(fed[at], chosen[e][begin:], NT) * decay
        daff_ref[at, begin:] = daff
        backs.append(jnp.where(low[at], parts[0], parts[1]))
    back = jnp.concatenate(backs, axis=0)
    inner = scanned_ref[...] - skip * values
    direct = back * values
    moved = dsb.astype(F32) * inner - fed.astype(F32) * back
    dstep, drun = dstep_ref[...], drun_ref[...]
    for e in range(2):
        half = low if e == 0 else ~low
        spot = lane == 2 * head_pair + e
        dstep = dstep + jnp.where(spot, jnp.sum(jnp.where(half, direct, 0.0), axis=1, keepdims=True), 0.0)
        drun = drun + jnp.where(spot, jnp.sum(jnp.where(half, moved, 0.0), axis=1, keepdims=True), 0.0)
    dstep_ref[...] = dstep
    drun_ref[...] = drun
    dtotal = (stepx * back + skip * ds) * dvalues
    dx, tap_grads = conv_backward(dtotal, v_ref[...], masks, taps)
    gv_ref[...] = dx.astype(BF)
    sums = tap_grads + [
        jnp.sum(dtotal, axis=0, keepdims=True),
        jnp.sum(ds * values, axis=0, keepdims=True),
        jnp.zeros((2, LANES), F32),
    ]
    at = pl.ds(pl.multiple_of(pair * LANES, LANES), LANES)
    vsum_ref[:, at] = vsum_ref[:, at] + jnp.concatenate(sums, axis=0)
    if not last:
        return

    @pl.when(pair == pl.num_programs(1) - 1)
    def _():
        _, column, seg_row = segment_masks(seg_ref)
        _, before = ordered(seg_row.shape[1])
        allowed = before & (column == seg_row)
        full = jnp.where(allowed, daff_ref[...], 0.0)
        keys, queries = act_ref[:, :LANES], act_ref[:, LANES:]
        dkeys = mm_fine(full, queries, NN)
        dqueries = mm_fine(full, keys, TN)
        for c, dside in enumerate((dkeys, dqueries)):
            lanes = slice(c * LANES, (c + 1) * LANES)
            taps_c = [taps_s_ref[k : k + 1, lanes] for k in range(KERNEL)]
            dsum = dside * silu_parts(sum_ref[:, lanes])[1]
            dside_x, taps_g = conv_backward(dsum, shared_ref[:, lanes], masks, taps_c)
            gs_ref[:, lanes] = dside_x.astype(BF)
            more = taps_g + [jnp.sum(dsum, axis=0, keepdims=True), jnp.zeros((3, LANES), F32)]
            ssum_ref[:, lanes] = ssum_ref[:, lanes] + jnp.concatenate(more, axis=0)
        ddecay = mm_ones(jnp.where(before, 1.0, 0.0).astype(BF), drun_ref[...], NN)
        rate = -head_ref[1:2, :]
        draw = (dstep_ref[...] + ddecay * rate) * jax.nn.sigmoid(raw_ref[...])
        draw = draw * head_ref[2:3, :]
        gs_ref[:, 2 * LANES :] = pltpu.roll(draw, place_ref[0] * per, 1).astype(BF)
        heads = [
            jnp.sum(draw, axis=0, keepdims=True),
            jnp.sum(ddecay * (rate * step_ref[...]), axis=0, keepdims=True) * head_ref[2:3, :],
            jnp.zeros((6, LANES), F32),
        ]
        ssum_ref[:, 2 * LANES :] = ssum_ref[:, 2 * LANES :] + jnp.concatenate(heads, axis=0)


def weightgrad_kernel(lefts, rights, parts, *refs):
    place_ref = refs[0]
    left_refs = refs[1 : 1 + lefts]
    right_refs = refs[1 + lefts : 1 + lefts + rights]
    given_ref, kept_ref, stage_ref, sems = refs[1 + lefts + rights :]
    core = place_ref[1]
    model = stage_ref.shape[1]
    width = 384 if model % 384 == 0 else LANES

    def column(n, carry):
        cols = pl.ds(pl.multiple_of(n * width, LANES), width)
        right = jnp.concatenate([ref[:, cols] for ref in right_refs], axis=0)
        row = 0
        for ref in left_refs:
            rows = ref.shape[1]
            stage_ref[row : row + rows, cols] = mm(ref[...], right, TN).astype(BF)
            row += rows
        return carry

    lax.fori_loop(0, model // width, column, 0)
    copies = []
    for target, whose in ((given_ref, 1 - core), (kept_ref, core)):
        row = done = 0
        for half in parts:
            copies.append(
                pltpu.make_async_copy(
                    stage_ref.at[pl.ds(pl.multiple_of(row + whose * half, 16), half), :],
                    target.at[pl.ds(done, half), :],
                    sems.at[len(copies)],
                )
            )
            copies[-1].start()
            row += 2 * half
            done += half
    for copy in copies:
        copy.wait()


def weightgrad(place, lefts, rights, parts):
    rows, model = 2 * sum(parts), rights[0].shape[1]
    tokens = lefts[0].shape[0]
    half = jax.ShapeDtypeStruct((rows // 2, model), BF)
    return call(
        partial(weightgrad_kernel, len(lefts), len(rights), parts),
        (half, half),
        2 * tokens * rows * model,
        2 * tokens * (rows + model) + 2 * rows * model,
        in_specs=[pl.BlockSpec(memory_space=pltpu.SMEM)] + [VM] * (len(lefts) + len(rights)),
        out_specs=(HBM, HBM),
        scratch_shapes=[pltpu.VMEM((rows, model), BF), pltpu.SemaphoreType.DMA((2 * len(parts),))],
    )(place, *lefts, *rights)


def normgrad_kernel(groups, *refs):
    parts, weight_ref, outs = refs[: -groups - 1], refs[-groups - 1], refs[-groups:]
    span = outs[0].shape[0]
    model = weight_ref.shape[1]
    width = 384 if model % 384 == 0 else LANES

    def column(n, carry):
        cols = pl.ds(pl.multiple_of(n * width, LANES), width)
        weight = weight_ref[:, cols]
        for r in range(groups):
            at = slice(r * span, (r + 1) * span)
            terms = jnp.concatenate([part[at, :] for part in parts], axis=1)
            outs[r][:, cols] = mm(terms, weight, NN).astype(outs[r].dtype)
        return carry

    lax.fori_loop(0, model // width, column, 0)


def final_kernel(groups, aligned, width, *refs):
    outs = refs[:groups]
    grads = refs[groups : 2 * groups]
    sums = refs[2 * groups : 3 * groups]
    place_ref, tokens_ref, normal_ref, cot_ref, gain_ref, output_ref, tgrad_ref, gnorm_ref = refs[3 * groups :]
    member = place_ref[0]
    model = gain_ref.shape[1]
    rows = model // groups
    factor = gate_scales([s[...] for s in sums], width)[0]
    total = outs[0][...].astype(F32)
    for part in outs[1:]:
        total = total + part[...].astype(F32)
    output_ref[...] = (tokens_ref[...].astype(F32) + total * factor[:, 0:1]).astype(BF)
    xs, gained, square, cross = [], [], 0.0, 0.0
    for b in range(groups):
        at = slice(b * rows, (b + 1) * rows)
        grad = grads[0][:, at].astype(F32)
        for k in range(1, groups):
            grad = grad + grads[k][:, (b ^ k) * rows : ((b ^ k) + 1) * rows].astype(F32)
        x = normal_ref[:, lane_block(aligned, member, b, rows)].astype(F32)
        more = grad * gain_ref[:, at]
        square = square + jnp.sum(x * x, axis=-1, keepdims=True)
        cross = cross + jnp.sum(more * x, axis=-1, keepdims=True)
        xs.append((x, grad))
        gained.append(more)
    scale = lax.rsqrt(square / model + EPSILON)
    bend = scale * scale * scale * (cross / model)
    for b in range(groups):
        at = slice(b * rows, (b + 1) * rows)
        x, grad = xs[b]
        lanes = lane_block(aligned, member, b, rows)
        tgrad_ref[:, lanes] = (cot_ref[:, lanes].astype(F32) + (gained[b] * scale - x * bend)).astype(BF)
        gnorm_ref[0:1, at] = jnp.sum(grad * (x * scale), axis=0, keepdims=True)


def place_kernel(pieces, groups, *refs):
    place_ref = refs[0]
    count = len(pieces)
    sources = refs[1 : 1 + 2 * count]
    out_ref, stage_ref, sems = refs[-3:]
    member, core = place_ref[0], place_ref[1]
    copies = []
    row = 0
    later = []
    for n, (segments, stride, shared) in enumerate(pieces):
        each = sum(half for half, _ in segments)
        for which in range(2):
            whose = core if which == 0 else 1 - core
            source = sources[2 * n + which]
            for k in range(groups):
                stage_ref[row : row + each, :] = source[k * each : (k + 1) * each, :].astype(F32)
                for half, offset in segments:
                    target = offset + jnp.bitwise_xor(member, k) * stride + whose * half
                    copy = pltpu.make_async_copy(
                        stage_ref.at[pl.ds(row, half), :],
                        out_ref.at[pl.ds(pl.multiple_of(target, 8), half), :],
                        sems.at[len(copies)],
                    )
                    copy.start()
                    copies.append(copy)
                    row += half
            if shared:
                part = source.shape[0] - groups * each
                begin, tail = shared
                stage_ref[row : row + part, :] = source[groups * each :, :].astype(F32)
                later.append((whose, row, begin, part, tail, len(copies) + len(later) + which))
                row += part
    for whose, row, begin, part, tail, sem in later:
        for c, size in ((0, part), (1, tail - part)):

            @pl.when(whose == c)
            def _():
                copy = pltpu.make_async_copy(
                    stage_ref.at[pl.ds(row, size), :], out_ref.at[pl.ds(begin + c * part, size), :], sems.at[sem]
                )
                copy.start()
                copy.wait()

    for copy in copies:
        copy.wait()


def place_rows(place, groups, shape, pieces, values, onto=None):
    rows = sum(v.shape[0] for v in values)
    given = [] if onto is None else [onto]
    return call(
        partial(place_kernel, pieces, groups),
        jax.ShapeDtypeStruct(shape, F32),
        rows * shape[1],
        6 * rows * shape[1],
        in_specs=[pl.BlockSpec(memory_space=pltpu.SMEM)] + [VM] * len(values) + [HBM] * len(given),
        out_specs=HBM,
        scratch_shapes=[
            pltpu.VMEM((rows, shape[1]), F32),
            pltpu.SemaphoreType.DMA((4 * len(pieces) * (groups + 2),)),
        ],
        input_output_aliases={1 + len(values): 0} if given else {},
    )(place, *values, *given)


def swap(value, axis, step):
    size = lax.axis_size(axis)
    return lax.ppermute(value, axis, [(i, i ^ step) for i in range(size)])


def rounded_sum(a, b):
    return (a.astype(F32) + b.astype(F32)).astype(BF)


def line_sum(value):
    size = lax.axis_size("rep")
    bits = size.bit_length() - 1
    last = bits - 2 if bits >= 3 else bits
    for b in range(1, last):
        value = rounded_sum(value, swap(value, "rep", 1 << b))
    if bits < 3:
        return value
    low = size // 4
    where = lax.axis_index("rep") // low
    inward = [(low * a + i, low * b + i) for a, b in ((0, 1), (3, 2)) for i in range(low)]
    middle = [(low * a + i, low * b + i) for a, b in ((1, 2), (2, 1)) for i in range(low)]
    outward = [(low * a + i, low * b + i) for a, b in ((1, 0), (2, 3)) for i in range(low)]
    got = lax.ppermute(value, "rep", inward)
    value = rounded_sum(value, got)
    got = lax.ppermute(value, "rep", middle)
    value = rounded_sum(value, got)
    back = lax.ppermute(value, "rep", outward)
    return jnp.where((where == 0) | (where == 3), back, value)


def all_sum(value):
    for axis in ("fsdp", "rep"):
        size = lax.axis_size(axis)
        step = 1
        while step < size:
            if step * 4 <= size:
                near, far, both = (swap(value, axis, step * m) for m in (1, 2, 3))
                value = (value + near) + (far + both)
                step *= 4
            else:
                value = value + swap(value, axis, step)
                step *= 2
    return value


def to_owners(total, groups):
    rows = total.shape[1] // groups
    blocks = [total[:, k * rows : (k + 1) * rows] for k in range(groups)]
    return [blocks[0]] + [swap(blocks[k], "fsdp", k) for k in range(1, groups)]


def core_sum(halves_):
    given, kept = halves_
    got = swap(given, "rep", 1)
    return rounded_sum(kept, got)


def body(
    tokens,
    segment_ids,
    cotangent,
    norm_gain,
    in_weight,
    conv_weight,
    conv_bias,
    step_bias,
    rate_log,
    skip_gain,
    gate_gain,
    out_weight,
):
    groups = lax.axis_size("fsdp")
    member = lax.axis_index("fsdp")
    core = lax.axis_index("rep") % 2
    span, model = tokens.shape
    per = HEADS // groups
    inner = per * HEADDIM
    full = inner * groups
    conv = conv_bias.shape[0] * groups
    tail = in_weight.shape[1] - 2 * full
    padded = -(-tail // 384) * 384
    width = 2 * inner + padded
    pairs = per // 2
    whole = groups * span
    quarter = lax.axis_index("rep") % 4
    place = jnp.stack([member, core, quarter]).astype(jnp.int32)

    rows = in_weight.shape[0]
    aligned = rows % LANES == 0
    cols = conv // groups
    smem = pl.BlockSpec(memory_space=pltpu.SMEM)
    weight_t = in_weight.T

    xs = [tokens] + [swap(tokens, "fsdp", k) for k in range(1, groups)]
    small_width = -(-max(rows, cols, span) // LANES) * LANES
    packed = call(
        partial(pack_kernel, groups),
        tuple(jax.ShapeDtypeStruct((width // 4, rows), BF) for _ in range(1, groups))
        + (jax.ShapeDtypeStruct((8, small_width), F32),),
        1,
        4 * width * rows * groups,
        in_specs=[smem, HBM] + [VM] * 4,
        out_specs=(VM,) * groups,
        scratch_shapes=[pltpu.SemaphoreType.DMA((3 * groups,))],
    )(place, weight_t, norm_gain.reshape(1, -1), conv_weight, conv_bias.reshape(1, -1), segment_ids)
    near = [swap(packed[k - 1], "fsdp", k) for k in range(1, groups)]
    own_small = call(
        copy_kernel, jax.ShapeDtypeStruct(packed[-1].shape, F32), 1, 1, in_specs=[VM], out_specs=VM
    )(packed[-1])
    small = [own_small] + [swap(packed[-1], "fsdp", k) for k in range(1, groups)]
    near = jnp.concatenate(near, axis=0)
    across = swap(near, "rep", 2)
    given = [near, swap(near, "rep", 1), across, swap(across, "rep", 1)]
    late, _ = lax.optimization_barrier((cotangent, (near, xs[-1])))
    cots = [cotangent] + [swap(late, "fsdp", k) for k in range(1, groups)]

    gain_x = jnp.concatenate([t[0:1, :rows] for t in small], axis=1)
    order = jnp.arange(groups) ^ member
    table = jnp.take(jnp.stack(small), order, axis=0)
    taps_full = jnp.swapaxes(table[:, 1 : 2 + KERNEL, :cols], 0, 1).reshape(KERNEL + 1, conv)
    own_heads = lambda v: lax.dynamic_slice_in_dim(v.astype(F32), member * per, per, 0)
    taps_v = jnp.concatenate(
        [
            lax.dynamic_slice_in_dim(taps_full, member * inner, inner, 1),
            jnp.repeat(own_heads(skip_gain), HEADDIM).reshape(1, inner),
            gate_gain.astype(F32).reshape(1, inner),
            jnp.zeros((1, inner), F32),
        ],
        axis=0,
    )
    taps_s = jnp.concatenate([taps_full[:, full:], jnp.zeros((3, conv - full), F32)], axis=0)
    spread = lambda v: jnp.pad(v, (0, LANES - per)).reshape(1, LANES)
    heads = jnp.concatenate(
        [
            spread(own_heads(step_bias)),
            spread(jnp.exp(own_heads(rate_log))),
            spread(jnp.ones((per,), F32)),
            jnp.zeros((5, LANES), F32),
        ],
        axis=0,
    )
    segs = jnp.concatenate(
        [jnp.broadcast_to(s[2 + KERNEL : 3 + KERNEL, :span], (8, span)) for s in small], axis=0
    )

    def in_peer_order(value):
        if aligned:
            return value
        return jnp.take(value.reshape(value.shape[0], groups, rows), order, axis=1).reshape(value.shape)

    if aligned:
        sources = [weight_t] + given
    else:
        ranked = jnp.take(jnp.stack(given), jnp.arange(4) ^ quarter, axis=0)
        mine = jnp.concatenate(
            [
                lax.dynamic_slice_in_dim(weight_t, member * inner, inner, 0),
                lax.dynamic_slice_in_dim(weight_t, full + member * inner, inner, 0),
                jnp.pad(weight_t[2 * full :], ((0, padded - tail), (0, 0))),
            ],
            axis=0,
        )
        sent, share = width // 4, inner // 4

        def block(k):
            own = ranked[:, (k - 1) * sent : k * sent]
            pieces = (own[:, :share], own[:, share : 2 * share], own[:, 2 * share :])
            return jnp.concatenate([piece.reshape(-1, rows) for piece in pieces], axis=0)

        sources = [jnp.concatenate([mine] + [block(k) for k in range(1, groups)], axis=1)]
    sems = pltpu.SemaphoreType.DMA((12 * groups,))
    normed, projected, weight = call(
        partial(inproj_kernel, groups, aligned),
        (
            jax.ShapeDtypeStruct((whole, model), BF),
            jax.ShapeDtypeStruct((whole, width), F32),
            jax.ShapeDtypeStruct((width, model), BF),
        ),
        2 * whole * model * width,
        4 * whole * width + 4 * model * width + 4 * whole * model,
        mib=6 * groups,
        in_specs=[HBM] * groups + [VM, smem] + [HBM] * len(sources),
        out_specs=(VM, VM, HBM),
        scratch_shapes=[
            pltpu.VMEM((groups, span, model), BF),
            pltpu.VMEM((width, model), BF),
            sems,
            pltpu.SemaphoreType.DMA((groups,)),
        ],
    )(*[in_peer_order(x) for x in xs], gain_x, place, *sources)

    tile = lambda col: pl.BlockSpec((span, LANES), lambda r, p: (r, col + p))
    per_row = lambda cols_, col: pl.BlockSpec((span, cols_), lambda r, p: (r, col))
    fixed = lambda shape: pl.BlockSpec(shape, lambda r, p: (0, 0))
    pair_cols = pl.BlockSpec((8, LANES), lambda r, p: (0, p))
    seg_spec = pl.BlockSpec((8, span), lambda r, p: (r, 0))
    shared_spec = per_row(padded, 2 * inner // padded)
    scan_flops = 4 * whole * span * inner
    side = lambda w: jax.ShapeDtypeStruct((whole, w), F32)
    flipped_spec = pl.BlockSpec((LANES, span), lambda r, p: (r, 0))
    kept_shapes = (
        side((KERNEL - 1) * LANES),
        side(span),
        side(LANES),
        side(LANES),
        jax.ShapeDtypeStruct((groups * LANES, span), F32),
        side(LANES),
        side(2 * LANES),
        side(2 * LANES),
    )
    kept_specs = (
        per_row((KERNEL - 1) * LANES, 0),
        per_row(span, 0),
        per_row(LANES, 0),
        per_row(LANES, 0),
        flipped_spec,
        per_row(LANES, 0),
        per_row(2 * LANES, 0),
        per_row(2 * LANES, 0),
    )
    scanned, totals, gated, squares, *kept = call(
        partial(forward_kernel, per),
        (
            side(inner),
            side(inner),
            jax.ShapeDtypeStruct((whole, inner), BF),
            jax.ShapeDtypeStruct((8 * groups, span), F32),
        )
        + kept_shapes,
        8 * scan_flops,
        20 * whole * inner,
        mib=12,
        grid=(groups, pairs),
        in_specs=[
            smem,
            tile(0),
            tile(pairs),
            shared_spec,
            seg_spec,
            fixed((8, conv - full)),
            pair_cols,
            fixed((8, LANES)),
        ],
        out_specs=(tile(0), tile(0), tile(0), seg_spec) + kept_specs,
        scratch_shapes=[pltpu.VMEM((span, span), F32), pltpu.VMEM((span, LANES), F32)],
    )(place, projected, projected, projected, segs, taps_s, taps_v, heads)

    proj_flops = 2 * whole * inner * model
    dm, sums = call(
        partial(mixgrad_kernel, groups),
        (jax.ShapeDtypeStruct((whole, inner), F32), jax.ShapeDtypeStruct((8 * groups, span), F32)),
        proj_flops,
        2 * whole * model + 6 * whole * inner + 2 * inner * model,
        in_specs=[VM] * (groups + 3),
        out_specs=(VM, VM),
    )(*cots, out_weight, gated, squares)
    sums_all = [sums] + [swap(sums, "fsdp", k) for k in range(1, groups)]

    outs = call(
        partial(outproj_kernel, groups),
        tuple(jax.ShapeDtypeStruct((span, model), BF if k else F32) for k in range(groups)),
        proj_flops,
        2 * whole * model + 2 * whole * inner + 2 * inner * model,
        in_specs=[VM, VM],
        out_specs=(VM,) * groups,
    )(gated, out_weight)
    outs = [outs[0]] + [swap(outs[k], "fsdp", k) for k in range(1, groups)]

    row_spec = lambda cols_, col=0: pl.BlockSpec((span, cols_), lambda r: (r, col))
    gz, ds, mixed, gate_sum = call(
        partial(gatebwd_kernel, groups, float(full)),
        (
            jax.ShapeDtypeStruct((whole, inner), BF),
            jax.ShapeDtypeStruct((whole, inner), F32),
            jax.ShapeDtypeStruct((whole, inner), BF),
            jax.ShapeDtypeStruct((8, inner), F32),
        ),
        20 * whole * inner,
        20 * whole * inner,
        mib=16,
        grid=(groups,),
        in_specs=[
            pl.BlockSpec((8, span), (lambda k: lambda r: (jnp.bitwise_xor(r, k), 0))(k)) for k in range(groups)
        ]
        + [row_spec(inner), row_spec(inner), row_spec(inner), pl.BlockSpec((8, inner), lambda r: (0, 0))],
        out_specs=(
            row_spec(inner),
            row_spec(inner),
            row_spec(inner),
            pl.BlockSpec((8, inner), lambda r: (0, 0)),
        ),
    )(*sums_all, projected, scanned, dm, jnp.broadcast_to(gate_gain.astype(F32).reshape(1, inner), (8, inner)))

    z_sum = core_sum(weightgrad(place, [gz], [normed], (inner // 2,)))
    o_sum = core_sum(weightgrad(place, [mixed], cots, (inner // 2,)))
    out_part = line_sum(o_sum)
    z_part = line_sum(jnp.concatenate(to_owners(z_sum, groups), axis=0))

    third = pairs // 3
    cuts = (0, third, 2 * third, pairs)
    split = cuts[2]
    carry_shapes = (side(span), side(LANES), side(LANES))
    carry_specs = (per_row(span, 0), per_row(LANES, 0), per_row(LANES, 0))

    def backward(n, carry):
        first, count, last = cuts[n], cuts[n + 1] - cuts[n], n == 2
        cols_ = count * LANES
        outs_ = (jax.ShapeDtypeStruct((whole, cols_), BF), jax.ShapeDtypeStruct((8, cols_), F32))
        specs_ = (tile(0), fixed((8, cols_)))
        scratch, more, more_specs = [], [], []
        if last:
            outs_ += (jax.ShapeDtypeStruct((whole, padded), BF), jax.ShapeDtypeStruct((8, padded), F32))
            specs_ += (per_row(padded, 0), fixed((8, padded)))
            scratch = [
                pltpu.VMEM((span, span), F32),
                pltpu.VMEM((span, LANES), F32),
                pltpu.VMEM((span, LANES), F32),
            ]
            more = [projected, kept[5], kept[6], kept[7], segs, taps_s, heads, place]
            more_specs = [shared_spec, kept_specs[5], kept_specs[6], kept_specs[7], seg_spec]
            more_specs += [fixed((8, conv - full)), fixed((8, LANES)), smem]
        else:
            outs_ += carry_shapes
            specs_ += carry_specs
        return call(
            partial(backward_kernel, per, first, last, len(carry) > 0),
            outs_,
            16 * scan_flops * count // pairs,
            24 * whole * cols_,
            mib=48 if last else 12,
            grid=(groups, count),
            in_specs=[tile(first), tile(pairs + first), tile(first), tile(first)]
            + list(kept_specs[:5])
            + [pl.BlockSpec((8, LANES), lambda r, p: (0, first + p))]
            + (list(carry_specs) if carry else [])
            + more_specs,
            out_specs=specs_,
            scratch_shapes=scratch,
        )(ds, projected, totals, scanned, *kept[:5], taps_v, *carry, *more)

    gva, vsum1, *handed = backward(0, ())
    gvb, vsum2, *handed = backward(1, handed)
    v1_sum = core_sum(weightgrad(place, [gva, gvb], [normed], (third * HEADDIM, third * HEADDIM)))
    gv2, vsum3, gs, ssum = backward(2, handed)
    vsum = jnp.concatenate([vsum1, vsum2, vsum3], axis=1)

    backs = call(
        partial(normgrad_kernel, groups),
        tuple(jax.ShapeDtypeStruct((span, model), BF if k else F32) for k in range(groups)),
        2 * whole * width * model,
        2 * whole * model + 2 * whole * width + 2 * width * model,
        in_specs=[VM] * 6,
        out_specs=(VM,) * groups,
    )(gz, gva, gvb, gv2, gs, weight)
    backs = [backs[0]] + [swap(backs[k], "fsdp", k) for k in range(1, groups)]

    v1_part = line_sum(jnp.concatenate(to_owners(v1_sum, groups), axis=0))
    deep = (pairs - split) * HEADDIM
    s_sum = core_sum(weightgrad(place, [gv2, gs], [normed], (deep, padded // 2)))
    terms = to_owners(s_sum, groups)
    shared_sum = terms[0][deep:].astype(F32)
    for term in terms[1:]:
        shared_sum = shared_sum + term[deep:].astype(F32)
    s_part = line_sum(jnp.concatenate([t[:deep] for t in terms] + [shared_sum.astype(BF)], axis=0))

    whole_spec = lambda shape: pl.BlockSpec(shape, lambda i: (0,) * len(shape))
    output, tokens_grad, norm_sum = call(
        partial(final_kernel, groups, aligned, float(full)),
        (
            jax.ShapeDtypeStruct((span, model), BF),
            jax.ShapeDtypeStruct((span, model), BF),
            jax.ShapeDtypeStruct((8, model), F32),
        ),
        30 * span * model,
        24 * span * model,
        grid=(1,),
        in_specs=[whole_spec((span, model))] * (2 * groups)
        + [pl.BlockSpec((8, span), (lambda k: lambda i: (k, 0))(k)) for k in range(groups)]
        + [smem]
        + [whole_spec((span, model))] * 3
        + [whole_spec((1, model))],
        out_specs=(whole_spec((span, model)), whole_spec((span, model)), whole_spec((8, model))),
    )(*outs, *backs, *sums_all, place, tokens, in_peer_order(tokens), in_peer_order(cotangent), gain_x)
    tokens_grad = in_peer_order(tokens_grad)
    norm_sum = jnp.take(norm_sum[0].reshape(groups, rows), order, axis=0).reshape(1, model)

    def returned(part):
        return [part, swap(part, "rep", 1)]

    grad_outproj = place_rows(
        place, 1, out_weight.shape, ((((inner // 2, 0),), 0, None),), returned(out_part)
    )
    early = returned(z_part) + returned(v1_part)
    gin = place_rows(
        place,
        groups,
        weight_t.shape,
        (
            (((inner // 2, 0),), inner, None),
            (((third * HEADDIM, full), (third * HEADDIM, full + third * 2 * HEADDIM)), inner, None),
        ),
        early,
    )
    grad_inproj = place_rows(
        place,
        groups,
        weight_t.shape,
        ((((deep, full + split * 2 * HEADDIM),), inner, (2 * full, tail)),),
        returned(s_part),
        gin,
    ).T

    own_cols = lambda v: lax.dynamic_update_slice_in_dim(
        jnp.zeros((v.shape[0], full), F32), v, member * inner, 1
    )
    own_spot = lambda v: lax.dynamic_update_slice_in_dim(jnp.zeros((HEADS,), F32), v, member * per, 0)
    taps_grad = jnp.concatenate([own_cols(vsum[: KERNEL + 1]), ssum[: KERNEL + 1, : conv - full]], axis=1)
    head_grads = [
        own_spot(ssum[0, 2 * LANES : 2 * LANES + per]),
        own_spot(ssum[1, 2 * LANES : 2 * LANES + per]),
        own_spot(vsum[KERNEL + 1].reshape(per, HEADDIM).sum(axis=1)),
    ]
    flat = jnp.concatenate(
        [norm_sum[0], taps_grad.reshape(-1), own_cols(gate_sum[:1]).reshape(-1)] + head_grads
    )
    length = flat.shape[0]
    flat = jnp.pad(flat, (0, -length % 1024)).reshape(-1, LANES)
    flat = all_sum(flat).reshape(-1)
    at = 0
    grad_norm = lax.dynamic_slice_in_dim(flat, member * rows, rows, 0)
    at += model
    taps_all = flat[at : at + (KERNEL + 1) * conv].reshape(KERNEL + 1, conv)
    taps_own = lax.dynamic_slice_in_dim(taps_all, member * cols, cols, 1)
    at += (KERNEL + 1) * conv
    grad_gate = lax.dynamic_slice_in_dim(flat, at + member * inner, inner, 0)
    at += full
    return (
        output,
        tokens_grad,
        grad_norm,
        grad_inproj,
        taps_own[:KERNEL],
        taps_own[KERNEL],
        flat[at : at + HEADS],
        flat[at + HEADS : at + 2 * HEADS],
        flat[at + 2 * HEADS : at + 3 * HEADS],
        grad_gate,
        grad_outproj,
    )


def solution(mesh):
    rows = P(("rep", "fsdp"), None)
    in_specs = (
        rows,
        rows,
        rows,
        P("fsdp"),
        P("fsdp", None),
        P(None, "fsdp"),
        P("fsdp"),
        P(),
        P(),
        P(),
        P("fsdp"),
        P("fsdp", None),
    )
    out_specs = (
        rows,
        rows,
        P("fsdp"),
        P("fsdp", None),
        P(None, "fsdp"),
        P("fsdp"),
        P(),
        P(),
        P(),
        P("fsdp"),
        P("fsdp", None),
    )

    return jax.shard_map(body, mesh=mesh, in_specs=in_specs, out_specs=out_specs, check_vma=False)
```

```python
from functools import partial

import jax
import jax.numpy as jnp
from jax import lax
from jax.experimental import pallas as pl
from jax.experimental.pallas import tpu as pltpu
from jax.sharding import PartitionSpec as P


HEADS = 48
HEADDIM = 64
KERNEL = 4
LANES = 128
EPSILON = 1e-05
BF = jnp.bfloat16
F32 = jnp.float32

NN = (((1,), (0,)), ((), ()))
NT = (((1,), (1,)), ((), ()))
TN = (((0,), (0,)), ((), ()))


def mm(a, b, dims):
    return lax.dot_general(a, b, dims, preferred_element_type=F32)


def halves(x):
    top = x.astype(BF)
    return top, (x - top.astype(F32)).astype(BF)


def mm_fine(a, b, dims):
    a_top, a_low = halves(a)
    b_top, b_low = halves(b)
    return mm(a_top, b_top, dims) + (mm(a_top, b_low, dims) + mm(a_low, b_top, dims))


def mm_ones(ones, x, dims):
    top, low = halves(x)
    rest = (x - top.astype(F32) - low.astype(F32)).astype(BF)
    parts = mm(ones, jnp.concatenate([top, low, rest], axis=1), dims)
    lanes = x.shape[1]
    return parts[:, :lanes] + (parts[:, lanes : 2 * lanes] + parts[:, 2 * lanes :])


def sigmoid(v):
    return 0.5 * jnp.tanh(0.5 * v) + 0.5


def silu_parts(v):
    gate = sigmoid(v)
    return v * gate, gate * (1.0 + v * (1.0 - gate))


def call(kernel, out_shape, flops, moved, mib=None, **kw):
    grant = (mib or 4 * lax.axis_size("fsdp")) * 1024 * 1024

    def run(*operands):
        return pl.pallas_call(
            kernel,
            out_shape=out_shape,
            cost_estimate=pl.CostEstimate(flops=flops, bytes_accessed=moved, transcendentals=0),
            compiler_params=pltpu.CompilerParams(vmem_limit_bytes=grant),
            **kw,
        )(*operands)

    return run


VM = pl.BlockSpec(memory_space=pltpu.VMEM)
HBM = pl.BlockSpec(memory_space=pl.ANY)


def pack_kernel(groups, *refs):
    place_ref, weight_ref, gain_ref, taps_ref, shift_ref, seg_ref = refs[:6]
    sends = refs[6 : 5 + groups]
    small_ref, sems = refs[5 + groups :]
    member, quarter = place_ref[0], place_ref[2]
    inner, share, edge, part, tail = quarter_sizes(sends[0].shape[0], weight_ref.shape[0], groups)
    copies = []
    for k in range(1, groups):
        peer = jnp.bitwise_xor(member, k)
        for i in range(2):
            source = pl.multiple_of(i * (edge // 2) + peer * inner + quarter * share, 16)
            copies.append(
                pltpu.make_async_copy(
                    weight_ref.at[pl.ds(source, share), :],
                    sends[k - 1].at[pl.ds(i * share, share), :],
                    sems.at[2 * k - 2 + i],
                )
            )
    for copy in copies:
        copy.start()
    for q in range(4):
        count = max(0, min(part, tail - q * part))

        @pl.when(quarter == q)
        def _():
            more = [
                pltpu.make_async_copy(
                    weight_ref.at[pl.ds(edge + q * part, count), :],
                    sends[k - 1].at[pl.ds(2 * share, count), :],
                    sems.at[2 * groups - 3 + k],
                )
                for k in range(1, groups)
                if count > 0
            ]
            for copy in more:
                copy.start()
            if count < part:
                for k in range(1, groups):
                    sends[k - 1][2 * share + count :, :] = jnp.zeros((part - count, weight_ref.shape[1]), BF)
            for copy in more:
                copy.wait()

    small_ref[...] = jnp.zeros_like(small_ref)
    small_ref[0:1, : gain_ref.shape[1]] = gain_ref[...].astype(F32)
    small_ref[1 : 1 + KERNEL, : taps_ref.shape[1]] = taps_ref[...].astype(F32)
    small_ref[1 + KERNEL : 2 + KERNEL, : shift_ref.shape[1]] = shift_ref[...].astype(F32)
    small_ref[2 + KERNEL : 3 + KERNEL, : seg_ref.shape[1]] = seg_ref[...].astype(F32)
    for copy in copies:
        copy.wait()


def copy_kernel(source_ref, target_ref):
    target_ref[...] = source_ref[...]


def quarter_sizes(sent, columns, groups):
    full = HEADS * HEADDIM
    inner = full // groups
    return inner, inner // 4, 2 * full, sent - inner // 2, columns - 2 * full


def inproj_kernel(groups, aligned, *refs):
    tokens = refs[:groups]
    gain_ref, place_ref, own_ref = refs[groups : groups + 3]
    given = refs[groups + 3 : -7]
    normed_ref, proj_ref, weight_out_ref, token_ref, weight_ref, sems, token_sems = refs[-7:]
    member, quarter = place_ref[0], place_ref[2]
    model = gain_ref.shape[1]
    rows = model // groups
    span = tokens[0].shape[0]
    loads = [pltpu.make_async_copy(tokens[r], token_ref.at[r], token_sems.at[r]) for r in range(groups)]
    for load in loads:
        load.start()
    copies = []
    if aligned:
        sent = given[0].shape[0] // (groups - 1)
        inner, share, edge, part, tail = quarter_sizes(sent, own_ref.shape[0], groups)
        for i, (source, count) in enumerate(
            ((member * inner, inner), (edge // 2 + member * inner, inner), (edge, tail))
        ):
            copies.append(
                pltpu.make_async_copy(
                    own_ref.at[pl.ds(pl.multiple_of(source, 16), count), :],
                    weight_ref.at[pl.ds(i * inner, count), pl.ds(0, rows)],
                    sems.at[i],
                )
            )
        for n, piece in enumerate(given):
            whose = jnp.bitwise_xor(quarter, n)
            for k in range(1, groups):
                for i, count in enumerate((share, share, part)):
                    target = pl.multiple_of(i * inner + whose * count, 16)
                    copies.append(
                        pltpu.make_async_copy(
                            piece.at[pl.ds((k - 1) * sent + i * share, count), :],
                            weight_ref.at[pl.ds(target, count), pl.ds(k * rows, rows)],
                            sems.at[len(copies)],
                        )
                    )
    else:
        copies.append(pltpu.make_async_copy(own_ref, weight_ref, sems.at[0]))
    for copy in copies:
        copy.start()
    if aligned and part * 4 > tail:
        weight_ref[2 * inner + tail :, 0:rows] = jnp.zeros((4 * part - tail, rows), BF)
    for r in range(groups):
        loads[r].wait()
        blocks = [token_ref[r, :, lane_block(aligned, member, k, rows)].astype(F32) for k in range(groups)]
        total = jnp.sum(blocks[0] * blocks[0], axis=-1, keepdims=True)
        for x in blocks[1:]:
            total = total + jnp.sum(x * x, axis=-1, keepdims=True)
        factor = lax.rsqrt(total / model + EPSILON)
        for k in range(groups):
            at = slice(k * rows, (k + 1) * rows)
            normed_ref[r * span : (r + 1) * span, at] = (blocks[k] * factor * gain_ref[:, at]).astype(BF)
    for copy in copies:
        copy.wait()
    keep = pltpu.make_async_copy(weight_ref, weight_out_ref, sems.at[0])
    keep.start()
    width = 384
    total = weight_ref.shape[0] // width

    def column(n, carry):
        at = pl.multiple_of(n * width, LANES)
        for r in range(groups):
            proj_ref[r * span : (r + 1) * span, pl.ds(at, width)] = mm(
                normed_ref[r * span : (r + 1) * span, :], weight_ref[pl.ds(at, width), :], NT
            )
        return carry

    lax.fori_loop(0, total, column, 0)
    keep.wait()


def lane_block(aligned, member, k, rows):
    if aligned:
        return pl.ds(pl.multiple_of(jnp.bitwise_xor(member, k) * rows, LANES), rows)
    return slice(k * rows, (k + 1) * rows)


def conv_forward(x, masks, taps, shift):
    total = shift + taps[KERNEL - 1] * x
    for s in range(1, KERNEL):
        total = total + taps[KERNEL - 1 - s] * (pltpu.roll(x, s, 0) * masks[s - 1])
    return total


def conv_backward(grad, x, masks, taps):
    span = x.shape[0]
    back = taps[KERNEL - 1] * grad
    tap_grads = [None] * KERNEL
    tap_grads[KERNEL - 1] = jnp.sum(grad * x, axis=0, keepdims=True)
    for s in range(1, KERNEL):
        part = grad * masks[s - 1]
        back = back + taps[KERNEL - 1 - s] * pltpu.roll(part, span - s, 0)
        tap_grads[KERNEL - 1 - s] = jnp.sum(part * pltpu.roll(x, s, 0), axis=0, keepdims=True)
    return back, tap_grads


def wide(column, count):
    return jnp.concatenate([column] * (count // LANES), axis=1)


def segment_masks(seg_ref):
    span = seg_ref.shape[-1]
    row = seg_ref[0:1, :]
    column = jnp.broadcast_to(row, (LANES, span)).T
    token = lax.broadcasted_iota(jnp.int32, (span, LANES), 0)
    masks = []
    for s in range(1, KERNEL):
        same = (pltpu.roll(column, s, 0) == column) & (token >= s)
        masks.append(jnp.where(same, 1.0, 0.0))
    return masks, wide(column, span), row


def ordered(span):
    i = lax.broadcasted_iota(jnp.int32, (span, span), 0)
    j = lax.broadcasted_iota(jnp.int32, (span, span), 1)
    return i >= j, i <= j


def row_setup(shared_ref, seg_ref, taps_ref, head_ref, member, per, affinity_ref, kept):
    mask_ref, afft_ref, step_ref, run_ref, runt_ref, raw_ref, act_ref, sum_ref = kept
    masks, column, row = segment_masks(seg_ref)
    after, _ = ordered(row.shape[1])
    for s in range(KERNEL - 1):
        mask_ref[:, s * LANES : (s + 1) * LANES] = masks[s]
    outs = []
    for c in range(2):
        at = slice(c * LANES, (c + 1) * LANES)
        taps = [taps_ref[k : k + 1, at] for k in range(KERNEL)]
        total = conv_forward(shared_ref[:, at], masks, taps, taps_ref[KERNEL : KERNEL + 1, at])
        active = total * sigmoid(total)
        outs.append(active)
        sum_ref[:, at] = total
        act_ref[:, at] = active
    affinity = jnp.where(after & (column == row), mm_fine(outs[1], outs[0], NT), 0.0)
    affinity_ref[...] = affinity
    afft_ref[...] = affinity.T
    raw = pltpu.roll(shared_ref[:, 2 * LANES :], lax.rem(LANES - member * per, LANES), 1)
    raw = raw + head_ref[0:1, :]
    step = jnp.maximum(raw, 0.0) + jnp.log1p(jnp.exp(-jnp.abs(raw)))
    run = mm_ones(jnp.where(after, 1.0, 0.0).astype(BF), -head_ref[1:2, :] * step, NN)
    raw_ref[...] = raw
    step_ref[...] = step
    run_ref[...] = run
    runt_ref[...] = run.T


def pair_columns(pair, run_ref, runt_ref, step_ref):
    back = lax.rem(LANES - 2 * pair, LANES)
    runs = pltpu.roll(run_ref[...], back, 1)
    steps = pltpu.roll(step_ref[...], back, 1)
    lane = lax.broadcasted_iota(jnp.int32, runs.shape, 1)
    low = lane < HEADDIM
    stepx = jnp.where(low, steps[:, 0:1], steps[:, 1:2])
    columns = [runs[:, e : e + 1] for e in range(2)]
    rows = [runt_ref[pl.ds(2 * pair + e, 1), :] for e in range(2)]
    return columns, rows, stepx, low, lane


def forward_kernel(
    per,
    place_ref,
    z_ref,
    v_ref,
    shared_ref,
    seg_ref,
    taps_s_ref,
    taps_v_ref,
    head_ref,
    scanned_ref,
    total_ref,
    gated_ref,
    square_ref,
    mask_ref,
    afft_ref,
    step_ref,
    run_ref,
    runt_ref,
    raw_ref,
    act_ref,
    sum_ref,
    affinity_ref,
    square_sum_ref,
):
    pair = pl.program_id(1)

    @pl.when(pair == 0)
    def _():
        kept = (mask_ref, afft_ref, step_ref, run_ref, runt_ref, raw_ref, act_ref, sum_ref)
        row_setup(shared_ref, seg_ref, taps_s_ref, head_ref, place_ref[0], per, affinity_ref, kept)
        square_sum_ref[...] = jnp.zeros_like(square_sum_ref)

    masks = [mask_ref[:, s * LANES : (s + 1) * LANES] for s in range(KERNEL - 1)]
    count = v_ref.shape[1] // LANES
    squares = 0.0
    for m in range(count):
        lanes = slice(m * LANES, (m + 1) * LANES)
        taps = [taps_v_ref[k : k + 1, lanes] for k in range(KERNEL)]
        total = conv_forward(v_ref[:, lanes], masks, taps, taps_v_ref[KERNEL : KERNEL + 1, lanes])
        total_ref[:, lanes] = total
        values = total * sigmoid(total)
        columns, rows, stepx, low, _ = pair_columns(count * pair + m, run_ref, runt_ref, step_ref)
        fed = (stepx * values).astype(BF)
        skipped = taps_v_ref[KERNEL + 1 : KERNEL + 2, lanes] * values
        cut = fed.shape[0] // 2
        inner = []
        for n in range(2):
            at = slice(n * cut, (n + 1) * cut)
            seen = (n + 1) * cut
            affinity = affinity_ref[at, :seen]
            parts = []
            for e in range(2):
                decay = jnp.exp(jnp.minimum(columns[e][at] - rows[e][:, :seen], 0.0))
                parts.append(mm((decay * affinity).astype(BF), fed[:seen], NN))
            inner.append(jnp.where(low[at], parts[0], parts[1]))
        scanned = jnp.concatenate(inner, axis=0) + skipped
        z = z_ref[:, lanes]
        g = scanned * (z * sigmoid(z))
        scanned_ref[:, lanes] = scanned
        gated_ref[:, lanes] = (g * taps_v_ref[KERNEL + 2 : KERNEL + 3, lanes]).astype(BF)
        squares = squares + g * g
    square_sum_ref[...] = square_sum_ref[...] + squares

    @pl.when(pair == pl.num_programs(1) - 1)
    def _():
        row = jnp.sum(square_sum_ref[...].T, axis=0, keepdims=True)
        square_ref[...] = jnp.broadcast_to(row, square_ref.shape)


def mixgrad_kernel(groups, *refs):
    cots = refs[:groups]
    out_w_ref, gated_ref, square_ref, dm_ref, sums_ref, cot_ref, sems = refs[groups:]
    span = cots[0].shape[0]
    loads = [pltpu.make_async_copy(cots[r], cot_ref.at[r], sems.at[r]) for r in range(groups)]
    for load in loads:
        load.start()
    for load in loads:
        load.wait()
    width = 384 if out_w_ref.shape[0] % 384 == 0 else LANES

    def column(n, carry):
        cols = pl.ds(pl.multiple_of(n * width, LANES), width)
        weight = out_w_ref[cols, :]
        for r in range(groups):
            dm_ref[r * span : (r + 1) * span, cols] = mm(cot_ref[r], weight, NT)
        return carry

    lax.fori_loop(0, out_w_ref.shape[0] // width, column, 0)
    for r in range(groups):
        at = slice(r * span, (r + 1) * span)
        prod = dm_ref[at, :] * gated_ref[at, :].astype(F32)
        part = prod[:, :LANES]
        for c in range(1, prod.shape[1] // LANES):
            part = part + prod[:, c * LANES : (c + 1) * LANES]
        row = jnp.sum(part.T, axis=0, keepdims=True)
        sub = lax.broadcasted_iota(jnp.int32, (8, span), 0)
        sums_ref[8 * r : 8 * r + 8, :] = jnp.where(sub == 0, square_ref[8 * r : 8 * r + 8, :], row)


def outproj_kernel(groups, gated_ref, out_w_ref, *outs):
    span, model = outs[0].shape
    width = 384 if model % 384 == 0 else LANES

    def column(n, carry):
        cols = pl.ds(pl.multiple_of(n * width, LANES), width)
        weight = out_w_ref[:, cols]
        for r in range(groups):
            outs[r][:, cols] = mm(gated_ref[r * span : (r + 1) * span, :], weight, NN).astype(outs[r].dtype)
        return carry

    lax.fori_loop(0, model // width, column, 0)


def gate_scales(parts, width):
    total = parts[0]
    for part in parts[1:]:
        total = total + part
    square, cross = total[0:1, :], total[1:2, :]
    factor = lax.rsqrt(square / width + EPSILON)
    bend = factor * factor * factor * (cross / width)
    span = total.shape[1]
    return (
        jnp.broadcast_to(factor, (LANES, span)).T,
        jnp.broadcast_to(bend, (LANES, span)).T,
    )


def gatebwd_kernel(groups, width, *refs):
    sums = refs[:groups]
    z_ref, scanned_ref, dm_ref, gain_ref, gz_ref, ds_ref, mixed_ref, gate_ref = refs[groups:]
    r = pl.program_id(0)
    factor, bend = gate_scales([s[...] for s in sums], width)

    @pl.when(r == 0)
    def _():
        gate_ref[...] = jnp.zeros_like(gate_ref)

    for c in range(z_ref.shape[1] // LANES):
        at = slice(c * LANES, (c + 1) * LANES)
        gain = gain_ref[0:1, at]
        sz, dsz = silu_parts(z_ref[:, at])
        scanned = scanned_ref[:, at]
        dm = dm_ref[:, at]
        g = scanned * sz
        scaled = g * factor
        dg = factor * (dm * gain) - g * bend
        mixed_ref[:, at] = (scaled * gain).astype(BF)
        gz_ref[:, at] = (dg * scanned * dsz).astype(BF)
        ds_ref[:, at] = dg * sz
        gate_ref[0:1, at] += jnp.sum(dm * scaled, axis=0, keepdims=True)


def backward_kernel(per, first, last, carried, *refs):
    (ds_ref, v_ref, total_in_ref, scanned_ref, mask_ref, afft_ref, step_ref, run_ref, runt_ref, taps_v_ref) = refs[:10]
    refs = refs[10:]
    if carried:
        carry, refs = refs[:3], refs[3:]
    if last:
        (shared_ref, raw_ref, act_ref, sum_ref, seg_ref, taps_s_ref, head_ref, place_ref) = refs[:8]
        gv_ref, vsum_ref, gs_ref, ssum_ref, daff_ref, dstep_ref, drun_ref = refs[8:]
    else:
        gv_ref, vsum_ref, daff_ref, dstep_ref, drun_ref = refs
    row, pair = pl.program_id(0), pl.program_id(1)
    head_pair = pair + first

    @pl.when((row == 0) & (pair == 0))
    def _():
        vsum_ref[...] = jnp.zeros_like(vsum_ref)
        if last:
            ssum_ref[...] = jnp.zeros_like(ssum_ref)

    @pl.when(pair == 0)
    def _():
        for n, target in enumerate((daff_ref, dstep_ref, drun_ref)):
            target[...] = carry[n][...] if carried else jnp.zeros_like(target)

    masks = [mask_ref[:, s * LANES : (s + 1) * LANES] for s in range(KERNEL - 1)]
    taps = [taps_v_ref[k : k + 1, :] for k in range(KERNEL)]
    skip = taps_v_ref[KERNEL + 1 : KERNEL + 2, :]
    values, dvalues = silu_parts(total_in_ref[...])
    columns, rows, stepx, low, lane = pair_columns(head_pair, run_ref, runt_ref, step_ref)
    ds = ds_ref[...]
    dsb = ds.astype(BF)
    fed = (stepx * values).astype(BF)
    zero = jnp.zeros_like(dsb)
    chosen = [jnp.where(low, dsb, zero), jnp.where(low, zero, dsb)]
    cut = fed.shape[0] // 2
    backs = []
    for n in range(2):
        at = slice(n * cut, (n + 1) * cut)
        begin = n * cut
        affinity = afft_ref[at, begin:]
        daff = daff_ref[at, begin:]
        parts = []
        for e in range(2):
            decay = jnp.exp(jnp.minimum(rows[e][:, begin:] - columns[e][at], 0.0))
            parts.append(mm((decay * affinity).astype(BF), dsb[begin:], NN))
            daff = daff + mm(fed[at], chosen[e][begin:], NT) * decay
        daff_ref[at, begin:] = daff
        backs.append(jnp.where(low[at], parts[0], parts[1]))
    back = jnp.concatenate(backs, axis=0)
    inner = scanned_ref[...] - skip * values
    direct = back * values
    moved = dsb.astype(F32) * inner - fed.astype(F32) * back
    dstep, drun = dstep_ref[...], drun_ref[...]
    for e in range(2):
        half = low if e == 0 else ~low
        spot = lane == 2 * head_pair + e
        dstep = dstep + jnp.where(spot, jnp.sum(jnp.where(half, direct, 0.0), axis=1, keepdims=True), 0.0)
        drun = drun + jnp.where(spot, jnp.sum(jnp.where(half, moved, 0.0), axis=1, keepdims=True), 0.0)
    dstep_ref[...] = dstep
    drun_ref[...] = drun
    dtotal = (stepx * back + skip * ds) * dvalues
    dx, tap_grads = conv_backward(dtotal, v_ref[...], masks, taps)
    gv_ref[...] = dx.astype(BF)
    sums = tap_grads + [
        jnp.sum(dtotal, axis=0, keepdims=True),
        jnp.sum(ds * values, axis=0, keepdims=True),
        jnp.zeros((2, LANES), F32),
    ]
    at = pl.ds(pl.multiple_of(pair * LANES, LANES), LANES)
    vsum_ref[:, at] = vsum_ref[:, at] + jnp.concatenate(sums, axis=0)
    if not last:
        return

    @pl.when(pair == pl.num_programs(1) - 1)
    def _():
        _, column, seg_row = segment_masks(seg_ref)
        _, before = ordered(seg_row.shape[1])
        allowed = before & (column == seg_row)
        full = jnp.where(allowed, daff_ref[...], 0.0)
        keys, queries = act_ref[:, :LANES], act_ref[:, LANES:]
        dkeys = mm_fine(full, queries, NN)
        dqueries = mm_fine(full, keys, TN)
        for c, dside in enumerate((dkeys, dqueries)):
            lanes = slice(c * LANES, (c + 1) * LANES)
            taps_c = [taps_s_ref[k : k + 1, lanes] for k in range(KERNEL)]
            dsum = dside * silu_parts(sum_ref[:, lanes])[1]
            dside_x, taps_g = conv_backward(dsum, shared_ref[:, lanes], masks, taps_c)
            gs_ref[:, lanes] = dside_x.astype(BF)
            more = taps_g + [jnp.sum(dsum, axis=0, keepdims=True), jnp.zeros((3, LANES), F32)]
            ssum_ref[:, lanes] = ssum_ref[:, lanes] + jnp.concatenate(more, axis=0)
        ddecay = mm_ones(jnp.where(before, 1.0, 0.0).astype(BF), drun_ref[...], NN)
        rate = -head_ref[1:2, :]
        draw = (dstep_ref[...] + ddecay * rate) * jax.nn.sigmoid(raw_ref[...])
        draw = draw * head_ref[2:3, :]
        gs_ref[:, 2 * LANES :] = pltpu.roll(draw, place_ref[0] * per, 1).astype(BF)
        heads = [
            jnp.sum(draw, axis=0, keepdims=True),
            jnp.sum(ddecay * (rate * step_ref[...]), axis=0, keepdims=True) * head_ref[2:3, :],
            jnp.zeros((6, LANES), F32),
        ]
        ssum_ref[:, 2 * LANES :] = ssum_ref[:, 2 * LANES :] + jnp.concatenate(heads, axis=0)


def weightgrad_kernel(lefts, rights, parts, *refs):
    place_ref = refs[0]
    left_refs = refs[1 : 1 + lefts]
    right_refs = refs[1 + lefts : 1 + lefts + rights]
    given_ref, kept_ref, stage_ref, sems, right_ref, right_sems = refs[1 + lefts + rights :]
    core = place_ref[1]
    model = stage_ref.shape[1]
    loads = [pltpu.make_async_copy(right_refs[n], right_ref.at[n], right_sems.at[n]) for n in range(rights)]
    for load in loads:
        load.start()
    for load in loads:
        load.wait()
    width = 384 if model % 384 == 0 else LANES

    def column(n, carry):
        cols = pl.ds(pl.multiple_of(n * width, LANES), width)
        right = jnp.concatenate([right_ref[n, :, cols] for n in range(rights)], axis=0)
        row = 0
        for ref in left_refs:
            rows = ref.shape[1]
            stage_ref[row : row + rows, cols] = mm(ref[...], right, TN).astype(BF)
            row += rows
        return carry

    lax.fori_loop(0, model // width, column, 0)
    copies = []
    for target, whose in ((given_ref, 1 - core), (kept_ref, core)):
        row = done = 0
        for half in parts:
            copies.append(
                pltpu.make_async_copy(
                    stage_ref.at[pl.ds(pl.multiple_of(row + whose * half, 16), half), :],
                    target.at[pl.ds(done, half), :],
                    sems.at[len(copies)],
                )
            )
            copies[-1].start()
            row += 2 * half
            done += half
    for copy in copies:
        copy.wait()


def weightgrad(place, lefts, rights, parts):
    rows, model = 2 * sum(parts), rights[0].shape[1]
    tokens = lefts[0].shape[0]
    half = jax.ShapeDtypeStruct((rows // 2, model), BF)
    return call(
        partial(weightgrad_kernel, len(lefts), len(rights), parts),
        (half, half),
        2 * tokens * rows * model,
        2 * tokens * (rows + model) + 2 * rows * model,
        in_specs=[pl.BlockSpec(memory_space=pltpu.SMEM)] + [VM] * len(lefts) + [HBM] * len(rights),
        out_specs=(HBM, HBM),
        scratch_shapes=[
            pltpu.VMEM((rows, model), BF),
            pltpu.SemaphoreType.DMA((2 * len(parts),)),
            pltpu.VMEM((len(rights), rights[0].shape[0], model), BF),
            pltpu.SemaphoreType.DMA((len(rights),)),
        ],
    )(place, *lefts, *rights)


def normgrad_kernel(groups, *refs):
    parts, weight_ref, outs = refs[: -groups - 1], refs[-groups - 1], refs[-groups:]
    span = outs[0].shape[0]
    model = weight_ref.shape[1]
    width = 384 if model % 384 == 0 else LANES

    def column(n, carry):
        cols = pl.ds(pl.multiple_of(n * width, LANES), width)
        weight = weight_ref[:, cols]
        for r in range(groups):
            at = slice(r * span, (r + 1) * span)
            terms = jnp.concatenate([part[at, :] for part in parts], axis=1)
            outs[r][:, cols] = mm(terms, weight, NN).astype(outs[r].dtype)
        return carry

    lax.fori_loop(0, model // width, column, 0)


def final_kernel(groups, aligned, width, *refs):
    outs = refs[:groups]
    grads = refs[groups : 2 * groups]
    sums = refs[2 * groups : 3 * groups]
    place_ref, tokens_ref, normal_ref, cot_ref, gain_ref, output_ref, tgrad_ref, gnorm_ref = refs[3 * groups :]
    member = place_ref[0]
    model = gain_ref.shape[1]
    rows = model // groups
    factor = gate_scales([s[...] for s in sums], width)[0]
    total = outs[0][...].astype(F32)
    for part in outs[1:]:
        total = total + part[...].astype(F32)
    output_ref[...] = (tokens_ref[...].astype(F32) + total * factor[:, 0:1]).astype(BF)
    xs, gained, square, cross = [], [], 0.0, 0.0
    for b in range(groups):
        at = slice(b * rows, (b + 1) * rows)
        grad = grads[0][:, at].astype(F32)
        for k in range(1, groups):
            grad = grad + grads[k][:, (b ^ k) * rows : ((b ^ k) + 1) * rows].astype(F32)
        x = normal_ref[:, lane_block(aligned, member, b, rows)].astype(F32)
        more = grad * gain_ref[:, at]
        square = square + jnp.sum(x * x, axis=-1, keepdims=True)
        cross = cross + jnp.sum(more * x, axis=-1, keepdims=True)
        xs.append((x, grad))
        gained.append(more)
    scale = lax.rsqrt(square / model + EPSILON)
    bend = scale * scale * scale * (cross / model)
    for b in range(groups):
        at = slice(b * rows, (b + 1) * rows)
        x, grad = xs[b]
        lanes = lane_block(aligned, member, b, rows)
        tgrad_ref[:, lanes] = (cot_ref[:, lanes].astype(F32) + (gained[b] * scale - x * bend)).astype(BF)
        gnorm_ref[0:1, at] = jnp.sum(grad * (x * scale), axis=0, keepdims=True)


def place_kernel(pieces, groups, *refs):
    place_ref = refs[0]
    count = len(pieces)
    sources = refs[1 : 1 + 2 * count]
    out_ref, stage_ref, sems = refs[-3:]
    member, core = place_ref[0], place_ref[1]
    copies = []
    row = 0
    later = []
    for n, (segments, stride, shared) in enumerate(pieces):
        each = sum(half for half, _ in segments)
        for which in range(2):
            whose = core if which == 0 else 1 - core
            source = sources[2 * n + which]
            for k in range(groups):
                stage_ref[row : row + each, :] = source[k * each : (k + 1) * each, :].astype(F32)
                for half, offset in segments:
                    target = offset + jnp.bitwise_xor(member, k) * stride + whose * half
                    copy = pltpu.make_async_copy(
                        stage_ref.at[pl.ds(row, half), :],
                        out_ref.at[pl.ds(pl.multiple_of(target, 8), half), :],
                        sems.at[len(copies)],
                    )
                    copy.start()
                    copies.append(copy)
                    row += half
            if shared:
                part = source.shape[0] - groups * each
                begin, tail = shared
                stage_ref[row : row + part, :] = source[groups * each :, :].astype(F32)
                later.append((whose, row, begin, part, tail, len(copies) + len(later) + which))
                row += part
    for whose, row, begin, part, tail, sem in later:
        for c, size in ((0, part), (1, tail - part)):

            @pl.when(whose == c)
            def _():
                copy = pltpu.make_async_copy(
                    stage_ref.at[pl.ds(row, size), :], out_ref.at[pl.ds(begin + c * part, size), :], sems.at[sem]
                )
                copy.start()
                copy.wait()

    for copy in copies:
        copy.wait()


def place_rows(place, groups, shape, pieces, values, onto=None):
    rows = sum(v.shape[0] for v in values)
    given = [] if onto is None else [onto]
    return call(
        partial(place_kernel, pieces, groups),
        jax.ShapeDtypeStruct(shape, F32),
        rows * shape[1],
        6 * rows * shape[1],
        in_specs=[pl.BlockSpec(memory_space=pltpu.SMEM)] + [VM] * len(values) + [HBM] * len(given),
        out_specs=HBM,
        scratch_shapes=[
            pltpu.VMEM((rows, shape[1]), F32),
            pltpu.SemaphoreType.DMA((4 * len(pieces) * (groups + 2),)),
        ],
        input_output_aliases={1 + len(values): 0} if given else {},
    )(place, *values, *given)


def swap(value, axis, step):
    size = lax.axis_size(axis)
    return lax.ppermute(value, axis, [(i, i ^ step) for i in range(size)])


def rounded_sum(a, b):
    return (a.astype(F32) + b.astype(F32)).astype(BF)


def line_sum(value):
    size = lax.axis_size("rep")
    bits = size.bit_length() - 1
    last = bits - 2 if bits >= 3 else bits
    for b in range(1, last):
        value = rounded_sum(value, swap(value, "rep", 1 << b))
    if bits < 3:
        return value
    low = size // 4
    where = lax.axis_index("rep") // low
    inward = [(low * a + i, low * b + i) for a, b in ((0, 1), (3, 2)) for i in range(low)]
    middle = [(low * a + i, low * b + i) for a, b in ((1, 2), (2, 1)) for i in range(low)]
    outward = [(low * a + i, low * b + i) for a, b in ((1, 0), (2, 3)) for i in range(low)]
    got = lax.ppermute(value, "rep", inward)
    value = rounded_sum(value, got)
    got = lax.ppermute(value, "rep", middle)
    value = rounded_sum(value, got)
    back = lax.ppermute(value, "rep", outward)
    return jnp.where((where == 0) | (where == 3), back, value)


def all_sum(value):
    for axis in ("fsdp", "rep"):
        size = lax.axis_size(axis)
        step = 1
        while step < size:
            if step * 4 <= size:
                near, far, both = (swap(value, axis, step * m) for m in (1, 2, 3))
                value = (value + near) + (far + both)
                step *= 4
            else:
                value = value + swap(value, axis, step)
                step *= 2
    return value


def to_owners(total, groups):
    rows = total.shape[1] // groups
    blocks = [total[:, k * rows : (k + 1) * rows] for k in range(groups)]
    return [blocks[0]] + [swap(blocks[k], "fsdp", k) for k in range(1, groups)]


def core_sum(halves_):
    given, kept = halves_
    got = swap(given, "rep", 1)
    return rounded_sum(kept, got)


def body(
    tokens,
    segment_ids,
    cotangent,
    norm_gain,
    in_weight,
    conv_weight,
    conv_bias,
    step_bias,
    rate_log,
    skip_gain,
    gate_gain,
    out_weight,
):
    groups = lax.axis_size("fsdp")
    member = lax.axis_index("fsdp")
    core = lax.axis_index("rep") % 2
    span, model = tokens.shape
    per = HEADS // groups
    inner = per * HEADDIM
    full = inner * groups
    conv = conv_bias.shape[0] * groups
    tail = in_weight.shape[1] - 2 * full
    padded = -(-tail // 384) * 384
    width = 2 * inner + padded
    pairs = per // 2
    whole = groups * span
    quarter = lax.axis_index("rep") % 4
    place = jnp.stack([member, core, quarter]).astype(jnp.int32)

    rows = in_weight.shape[0]
    aligned = rows % LANES == 0
    cols = conv // groups
    smem = pl.BlockSpec(memory_space=pltpu.SMEM)
    weight_t = in_weight.T

    xs = [tokens] + [swap(tokens, "fsdp", k) for k in range(1, groups)]
    small_width = -(-max(rows, cols, span) // LANES) * LANES
    packed = call(
        partial(pack_kernel, groups),
        tuple(jax.ShapeDtypeStruct((width // 4, rows), BF) for _ in range(1, groups))
        + (jax.ShapeDtypeStruct((8, small_width), F32),),
        1,
        4 * width * rows * groups,
        in_specs=[smem, HBM] + [VM] * 4,
        out_specs=(VM,) * groups,
        scratch_shapes=[pltpu.SemaphoreType.DMA((3 * groups,))],
    )(place, weight_t, norm_gain.reshape(1, -1), conv_weight, conv_bias.reshape(1, -1), segment_ids)
    near = [swap(packed[k - 1], "fsdp", k) for k in range(1, groups)]
    own_small = call(
        copy_kernel, jax.ShapeDtypeStruct(packed[-1].shape, F32), 1, 1, in_specs=[VM], out_specs=VM
    )(packed[-1])
    small = [own_small] + [swap(packed[-1], "fsdp", k) for k in range(1, groups)]
    near = jnp.concatenate(near, axis=0)
    across = swap(near, "rep", 2)
    given = [near, swap(near, "rep", 1), across, swap(across, "rep", 1)]
    late, _ = lax.optimization_barrier((cotangent, (near, xs[-1])))
    cots = [cotangent] + [swap(late, "fsdp", k) for k in range(1, groups)]

    gain_x = jnp.concatenate([t[0:1, :rows] for t in small], axis=1)
    order = jnp.arange(groups) ^ member
    table = jnp.take(jnp.stack(small), order, axis=0)
    taps_full = jnp.swapaxes(table[:, 1 : 2 + KERNEL, :cols], 0, 1).reshape(KERNEL + 1, conv)
    own_heads = lambda v: lax.dynamic_slice_in_dim(v.astype(F32), member * per, per, 0)
    taps_v = jnp.concatenate(
        [
            lax.dynamic_slice_in_dim(taps_full, member * inner, inner, 1),
            jnp.repeat(own_heads(skip_gain), HEADDIM).reshape(1, inner),
            gate_gain.astype(F32).reshape(1, inner),
            jnp.zeros((1, inner), F32),
        ],
        axis=0,
    )
    taps_s = jnp.concatenate([taps_full[:, full:], jnp.zeros((3, conv - full), F32)], axis=0)
    spread = lambda v: jnp.pad(v, (0, LANES - per)).reshape(1, LANES)
    heads = jnp.concatenate(
        [
            spread(own_heads(step_bias)),
            spread(jnp.exp(own_heads(rate_log))),
            spread(jnp.ones((per,), F32)),
            jnp.zeros((5, LANES), F32),
        ],
        axis=0,
    )
    segs = jnp.concatenate(
        [jnp.broadcast_to(s[2 + KERNEL : 3 + KERNEL, :span], (8, span)) for s in small], axis=0
    )

    def in_peer_order(value):
        if aligned:
            return value
        return jnp.take(value.reshape(value.shape[0], groups, rows), order, axis=1).reshape(value.shape)

    if aligned:
        sources = [weight_t] + given
    else:
        ranked = jnp.take(jnp.stack(given), jnp.arange(4) ^ quarter, axis=0)
        mine = jnp.concatenate(
            [
                lax.dynamic_slice_in_dim(weight_t, member * inner, inner, 0),
                lax.dynamic_slice_in_dim(weight_t, full + member * inner, inner, 0),
                jnp.pad(weight_t[2 * full :], ((0, padded - tail), (0, 0))),
            ],
            axis=0,
        )
        sent, share = width // 4, inner // 4

        def block(k):
            own = ranked[:, (k - 1) * sent : k * sent]
            pieces = (own[:, :share], own[:, share : 2 * share], own[:, 2 * share :])
            return jnp.concatenate([piece.reshape(-1, rows) for piece in pieces], axis=0)

        sources = [jnp.concatenate([mine] + [block(k) for k in range(1, groups)], axis=1)]
    sems = pltpu.SemaphoreType.DMA((12 * groups,))
    normed, projected, weight = call(
        partial(inproj_kernel, groups, aligned),
        (
            jax.ShapeDtypeStruct((whole, model), BF),
            jax.ShapeDtypeStruct((whole, width), F32),
            jax.ShapeDtypeStruct((width, model), BF),
        ),
        2 * whole * model * width,
        4 * whole * width + 4 * model * width + 4 * whole * model,
        mib=6 * groups,
        in_specs=[HBM] * groups + [VM, smem] + [HBM] * len(sources),
        out_specs=(VM, VM, HBM),
        scratch_shapes=[
            pltpu.VMEM((groups, span, model), BF),
            pltpu.VMEM((width, model), BF),
            sems,
            pltpu.SemaphoreType.DMA((groups,)),
        ],
    )(*[in_peer_order(x) for x in xs], gain_x, place, *sources)

    tile = lambda col: pl.BlockSpec((span, LANES), lambda r, p: (r, col + p))
    per_row = lambda cols_, col: pl.BlockSpec((span, cols_), lambda r, p: (r, col))
    fixed = lambda shape: pl.BlockSpec(shape, lambda r, p: (0, 0))
    pair_cols = pl.BlockSpec((8, LANES), lambda r, p: (0, p))
    seg_spec = pl.BlockSpec((8, span), lambda r, p: (r, 0))
    shared_spec = per_row(padded, 2 * inner // padded)
    scan_flops = 4 * whole * span * inner
    joint = 2 if pairs % 2 == 0 else 1
    broad = lambda col: pl.BlockSpec((span, joint * LANES), lambda r, p: (r, col + p))
    side = lambda w: jax.ShapeDtypeStruct((whole, w), F32)
    flipped_spec = pl.BlockSpec((LANES, span), lambda r, p: (r, 0))
    kept_shapes = (
        side((KERNEL - 1) * LANES),
        side(span),
        side(LANES),
        side(LANES),
        jax.ShapeDtypeStruct((groups * LANES, span), F32),
        side(LANES),
        side(2 * LANES),
        side(2 * LANES),
    )
    kept_specs = (
        per_row((KERNEL - 1) * LANES, 0),
        per_row(span, 0),
        per_row(LANES, 0),
        per_row(LANES, 0),
        flipped_spec,
        per_row(LANES, 0),
        per_row(2 * LANES, 0),
        per_row(2 * LANES, 0),
    )
    scanned, totals, gated, squares, *kept = call(
        partial(forward_kernel, per),
        (
            side(inner),
            side(inner),
            jax.ShapeDtypeStruct((whole, inner), BF),
            jax.ShapeDtypeStruct((8 * groups, span), F32),
        )
        + kept_shapes,
        8 * scan_flops,
        20 * whole * inner,
        mib=12,
        grid=(groups, pairs // joint),
        in_specs=[
            smem,
            broad(0),
            broad(pairs // joint),
            shared_spec,
            seg_spec,
            fixed((8, conv - full)),
            pl.BlockSpec((8, joint * LANES), lambda r, p: (0, p)),
            fixed((8, LANES)),
        ],
        out_specs=(broad(0), broad(0), broad(0), seg_spec) + kept_specs,
        scratch_shapes=[pltpu.VMEM((span, span), F32), pltpu.VMEM((span, LANES), F32)],
    )(place, projected, projected, projected, segs, taps_s, taps_v, heads)

    proj_flops = 2 * whole * inner * model
    dm, sums = call(
        partial(mixgrad_kernel, groups),
        (jax.ShapeDtypeStruct((whole, inner), F32), jax.ShapeDtypeStruct((8 * groups, span), F32)),
        proj_flops,
        2 * whole * model + 6 * whole * inner + 2 * inner * model,
        in_specs=[HBM] * groups + [VM] * 3,
        out_specs=(VM, VM),
        scratch_shapes=[pltpu.VMEM((groups, span, model), BF), pltpu.SemaphoreType.DMA((groups,))],
    )(*cots, out_weight, gated, squares)
    sums_all = [sums] + [swap(sums, "fsdp", k) for k in range(1, groups)]

    outs = call(
        partial(outproj_kernel, groups),
        tuple(jax.ShapeDtypeStruct((span, model), BF if k else F32) for k in range(groups)),
        proj_flops,
        2 * whole * model + 2 * whole * inner + 2 * inner * model,
        in_specs=[VM, VM],
        out_specs=(VM,) * groups,
    )(gated, out_weight)
    outs = [outs[0]] + [swap(outs[k], "fsdp", k) for k in range(1, groups)]

    row_spec = lambda cols_, col=0: pl.BlockSpec((span, cols_), lambda r: (r, col))
    gz, ds, mixed, gate_sum = call(
        partial(gatebwd_kernel, groups, float(full)),
        (
            jax.ShapeDtypeStruct((whole, inner), BF),
            jax.ShapeDtypeStruct((whole, inner), F32),
            jax.ShapeDtypeStruct((whole, inner), BF),
            jax.ShapeDtypeStruct((8, inner), F32),
        ),
        20 * whole * inner,
        20 * whole * inner,
        mib=16,
        grid=(groups,),
        in_specs=[
            pl.BlockSpec((8, span), (lambda k: lambda r: (jnp.bitwise_xor(r, k), 0))(k)) for k in range(groups)
        ]
        + [row_spec(inner), row_spec(inner), row_spec(inner), pl.BlockSpec((8, inner), lambda r: (0, 0))],
        out_specs=(
            row_spec(inner),
            row_spec(inner),
            row_spec(inner),
            pl.BlockSpec((8, inner), lambda r: (0, 0)),
        ),
    )(*sums_all, projected, scanned, dm, jnp.broadcast_to(gate_gain.astype(F32).reshape(1, inner), (8, inner)))

    z_sum = core_sum(weightgrad(place, [gz], [normed], (inner // 2,)))
    o_sum = core_sum(weightgrad(place, [mixed], cots, (inner // 2,)))
    out_part = line_sum(o_sum)
    z_part = line_sum(jnp.concatenate(to_owners(z_sum, groups), axis=0))

    third = pairs // 3
    cuts = (0, third, 2 * third, pairs)
    split = cuts[2]
    carry_shapes = (side(span), side(LANES), side(LANES))
    carry_specs = (per_row(span, 0), per_row(LANES, 0), per_row(LANES, 0))

    def backward(n, carry):
        first, count, last = cuts[n], cuts[n + 1] - cuts[n], n == 2
        cols_ = count * LANES
        outs_ = (jax.ShapeDtypeStruct((whole, cols_), BF), jax.ShapeDtypeStruct((8, cols_), F32))
        specs_ = (tile(0), fixed((8, cols_)))
        scratch, more, more_specs = [], [], []
        if last:
            outs_ += (jax.ShapeDtypeStruct((whole, padded), BF), jax.ShapeDtypeStruct((8, padded), F32))
            specs_ += (per_row(padded, 0), fixed((8, padded)))
            scratch = [
                pltpu.VMEM((span, span), F32),
                pltpu.VMEM((span, LANES), F32),
                pltpu.VMEM((span, LANES), F32),
            ]
            more = [projected, kept[5], kept[6], kept[7], segs, taps_s, heads, place]
            more_specs = [shared_spec, kept_specs[5], kept_specs[6], kept_specs[7], seg_spec]
            more_specs += [fixed((8, conv - full)), fixed((8, LANES)), smem]
        else:
            outs_ += carry_shapes
            specs_ += carry_specs
        return call(
            partial(backward_kernel, per, first, last, len(carry) > 0),
            outs_,
            16 * scan_flops * count // pairs,
            24 * whole * cols_,
            mib=48 if last else 12,
            grid=(groups, count),
            in_specs=[tile(first), tile(pairs + first), tile(first), tile(first)]
            + list(kept_specs[:5])
            + [pl.BlockSpec((8, LANES), lambda r, p: (0, first + p))]
            + (list(carry_specs) if carry else [])
            + more_specs,
            out_specs=specs_,
            scratch_shapes=scratch,
        )(ds, projected, totals, scanned, *kept[:5], taps_v, *carry, *more)

    gva, vsum1, *handed = backward(0, ())
    gvb, vsum2, *handed = backward(1, handed)
    v1_sum = core_sum(weightgrad(place, [gva, gvb], [normed], (third * HEADDIM, third * HEADDIM)))
    gv2, vsum3, gs, ssum = backward(2, handed)
    vsum = jnp.concatenate([vsum1, vsum2, vsum3], axis=1)

    backs = call(
        partial(normgrad_kernel, groups),
        tuple(jax.ShapeDtypeStruct((span, model), BF if k else F32) for k in range(groups)),
        2 * whole * width * model,
        2 * whole * model + 2 * whole * width + 2 * width * model,
        in_specs=[VM] * 6,
        out_specs=(VM,) * groups,
    )(gz, gva, gvb, gv2, gs, weight)
    backs = [backs[0]] + [swap(backs[k], "fsdp", k) for k in range(1, groups)]

    v1_part = line_sum(jnp.concatenate(to_owners(v1_sum, groups), axis=0))
    deep = (pairs - split) * HEADDIM
    s_sum = core_sum(weightgrad(place, [gv2, gs], [normed], (deep, padded // 2)))
    terms = to_owners(s_sum, groups)
    shared_sum = terms[0][deep:].astype(F32)
    for term in terms[1:]:
        shared_sum = shared_sum + term[deep:].astype(F32)
    s_part = line_sum(jnp.concatenate([t[:deep] for t in terms] + [shared_sum.astype(BF)], axis=0))

    whole_spec = lambda shape: pl.BlockSpec(shape, lambda i: (0,) * len(shape))
    output, tokens_grad, norm_sum = call(
        partial(final_kernel, groups, aligned, float(full)),
        (
            jax.ShapeDtypeStruct((span, model), BF),
            jax.ShapeDtypeStruct((span, model), BF),
            jax.ShapeDtypeStruct((8, model), F32),
        ),
        30 * span * model,
        24 * span * model,
        grid=(1,),
        in_specs=[whole_spec((span, model))] * (2 * groups)
        + [pl.BlockSpec((8, span), (lambda k: lambda i: (k, 0))(k)) for k in range(groups)]
        + [smem]
        + [whole_spec((span, model))] * 3
        + [whole_spec((1, model))],
        out_specs=(whole_spec((span, model)), whole_spec((span, model)), whole_spec((8, model))),
    )(*outs, *backs, *sums_all, place, tokens, in_peer_order(tokens), in_peer_order(cotangent), gain_x)
    tokens_grad = in_peer_order(tokens_grad)
    norm_sum = jnp.take(norm_sum[0].reshape(groups, rows), order, axis=0).reshape(1, model)

    def returned(part):
        return [part, swap(part, "rep", 1)]

    grad_outproj = place_rows(place, 1, out_weight.shape, ((((inner // 2, 0),), 0, None),), returned(out_part))
    early = returned(z_part) + returned(v1_part)
    gin = place_rows(
        place,
        groups,
        weight_t.shape,
        (
            (((inner // 2, 0),), inner, None),
            (((third * HEADDIM, full), (third * HEADDIM, full + third * 2 * HEADDIM)), inner, None),
        ),
        early,
    )
    grad_inproj = place_rows(
        place,
        groups,
        weight_t.shape,
        ((((deep, full + split * 2 * HEADDIM),), inner, (2 * full, tail)),),
        returned(s_part),
        gin,
    ).T

    own_cols = lambda v: lax.dynamic_update_slice_in_dim(
        jnp.zeros((v.shape[0], full), F32), v, member * inner, 1
    )
    own_spot = lambda v: lax.dynamic_update_slice_in_dim(jnp.zeros((HEADS,), F32), v, member * per, 0)
    taps_grad = jnp.concatenate([own_cols(vsum[: KERNEL + 1]), ssum[: KERNEL + 1, : conv - full]], axis=1)
    head_grads = [
        own_spot(ssum[0, 2 * LANES : 2 * LANES + per]),
        own_spot(ssum[1, 2 * LANES : 2 * LANES + per]),
        own_spot(vsum[KERNEL + 1].reshape(per, HEADDIM).sum(axis=1)),
    ]
    flat = jnp.concatenate(
        [norm_sum[0], taps_grad.reshape(-1), own_cols(gate_sum[:1]).reshape(-1)] + head_grads
    )
    length = flat.shape[0]
    flat = jnp.pad(flat, (0, -length % 1024)).reshape(-1, LANES)
    flat = all_sum(flat).reshape(-1)
    at = 0
    grad_norm = lax.dynamic_slice_in_dim(flat, member * rows, rows, 0)
    at += model
    taps_all = flat[at : at + (KERNEL + 1) * conv].reshape(KERNEL + 1, conv)
    taps_own = lax.dynamic_slice_in_dim(taps_all, member * cols, cols, 1)
    at += (KERNEL + 1) * conv
    grad_gate = lax.dynamic_slice_in_dim(flat, at + member * inner, inner, 0)
    at += full
    return (
        output,
        tokens_grad,
        grad_norm,
        grad_inproj,
        taps_own[:KERNEL],
        taps_own[KERNEL],
        flat[at : at + HEADS],
        flat[at + HEADS : at + 2 * HEADS],
        flat[at + 2 * HEADS : at + 3 * HEADS],
        grad_gate,
        grad_outproj,
    )


def solution(mesh):
    rows = P(("rep", "fsdp"), None)
    in_specs = (
        rows,
        rows,
        rows,
        P("fsdp"),
        P("fsdp", None),
        P(None, "fsdp"),
        P("fsdp"),
        P(),
        P(),
        P(),
        P("fsdp"),
        P("fsdp", None),
    )
    out_specs = (
        rows,
        rows,
        P("fsdp"),
        P("fsdp", None),
        P(None, "fsdp"),
        P("fsdp"),
        P(),
        P(),
        P(),
        P("fsdp"),
        P("fsdp", None),
    )

    return jax.shard_map(body, mesh=mesh, in_specs=in_specs, out_specs=out_specs, check_vma=False)
```

```python
from functools import partial

import jax
import jax.numpy as jnp
from jax import lax
from jax.experimental import pallas as pl
from jax.experimental.pallas import tpu as pltpu
from jax.sharding import PartitionSpec as P


HEADS = 48
HEADDIM = 64
KERNEL = 4
FS = "fsdp"
REP = "rep"
LANES = 128
EPSILON = 1e-05
BF = jnp.bfloat16
F32 = jnp.float32

NN = (((1,), (0,)), ((), ()))
NT = (((1,), (1,)), ((), ()))
TN = (((0,), (0,)), ((), ()))


def mm(a, b, dims):
    return lax.dot_general(a, b, dims, preferred_element_type=F32)


def halves(x):
    top = x.astype(BF)
    return top, (x - top.astype(F32)).astype(BF)


def mm_fine(a, b, dims):
    a_top, a_low = halves(a)
    b_top, b_low = halves(b)
    return mm(a_top, b_top, dims) + (mm(a_top, b_low, dims) + mm(a_low, b_top, dims))


def mm_ones(ones, x, dims):
    top, low = halves(x)
    rest = (x - top.astype(F32) - low.astype(F32)).astype(BF)
    parts = mm(ones, jnp.concatenate([top, low, rest], axis=1), dims)
    lanes = x.shape[1]
    return parts[:, :lanes] + (parts[:, lanes : 2 * lanes] + parts[:, 2 * lanes :])


def sigmoid(v):
    return 0.5 * jnp.tanh(0.5 * v) + 0.5


def silu_parts(v):
    gate = sigmoid(v)
    return v * gate, gate * (1.0 + v * (1.0 - gate))


def call(kernel, out_shape, flops, moved, mib=None, **kw):
    grant = (mib or 4 * lax.axis_size(FS)) * 1024 * 1024

    def run(*operands):
        return pl.pallas_call(
            kernel,
            out_shape=out_shape,
            cost_estimate=pl.CostEstimate(flops=flops, bytes_accessed=moved, transcendentals=0),
            compiler_params=pltpu.CompilerParams(vmem_limit_bytes=grant),
            **kw,
        )(*operands)

    return run


VM = pl.BlockSpec(memory_space=pltpu.VMEM)
HBM = pl.BlockSpec(memory_space=pl.ANY)


def pack_kernel(groups, *refs):
    place_ref, weight_ref, gain_ref, taps_ref, shift_ref, seg_ref = refs[:6]
    sends = refs[6 : 5 + groups]
    small_ref, sems = refs[5 + groups :]
    member, quarter = place_ref[0], place_ref[2]
    inner, share, edge, part, tail = quarter_sizes(sends[0].shape[0], weight_ref.shape[0], groups)
    copies = []
    for k in range(1, groups):
        peer = jnp.bitwise_xor(member, k)
        for i in range(2):
            source = pl.multiple_of(i * (edge // 2) + peer * inner + quarter * share, 16)
            copies.append(
                pltpu.make_async_copy(
                    weight_ref.at[pl.ds(source, share), :],
                    sends[k - 1].at[pl.ds(i * share, share), :],
                    sems.at[2 * k - 2 + i],
                )
            )
    for copy in copies:
        copy.start()
    for q in range(4):
        count = max(0, min(part, tail - q * part))

        @pl.when(quarter == q)
        def _():
            more = [
                pltpu.make_async_copy(
                    weight_ref.at[pl.ds(edge + q * part, count), :],
                    sends[k - 1].at[pl.ds(2 * share, count), :],
                    sems.at[2 * groups - 3 + k],
                )
                for k in range(1, groups)
                if count > 0
            ]
            for copy in more:
                copy.start()
            if count < part:
                for k in range(1, groups):
                    sends[k - 1][2 * share + count :, :] = jnp.zeros((part - count, weight_ref.shape[1]), BF)
            for copy in more:
                copy.wait()

    small_ref[...] = jnp.zeros_like(small_ref)
    small_ref[0:1, : gain_ref.shape[1]] = gain_ref[...].astype(F32)
    small_ref[1 : 1 + KERNEL, : taps_ref.shape[1]] = taps_ref[...].astype(F32)
    small_ref[1 + KERNEL : 2 + KERNEL, : shift_ref.shape[1]] = shift_ref[...].astype(F32)
    small_ref[2 + KERNEL : 3 + KERNEL, : seg_ref.shape[1]] = seg_ref[...].astype(F32)
    for copy in copies:
        copy.wait()


def copy_kernel(source_ref, target_ref):
    target_ref[...] = source_ref[...]


def quarter_sizes(sent, columns, groups):
    full = HEADS * HEADDIM
    inner = full // groups
    return inner, inner // 4, 2 * full, sent - inner // 2, columns - 2 * full


def inproj_kernel(groups, aligned, *refs):
    tokens = refs[:groups]
    gain_ref, place_ref, own_ref = refs[groups : groups + 3]
    given = refs[groups + 3 : -7]
    normed_ref, proj_ref, weight_out_ref, token_ref, weight_ref, sems, token_sems = refs[-7:]
    member, quarter = place_ref[0], place_ref[2]
    model = gain_ref.shape[1]
    rows = model // groups
    span = tokens[0].shape[0]
    loads = [pltpu.make_async_copy(tokens[r], token_ref.at[r], token_sems.at[r]) for r in range(groups)]
    for load in loads:
        load.start()
    copies = []
    if aligned:
        sent = given[0].shape[0] // (groups - 1)
        inner, share, edge, part, tail = quarter_sizes(sent, own_ref.shape[0], groups)
        for i, (source, count) in enumerate(
            ((member * inner, inner), (edge // 2 + member * inner, inner), (edge, tail))
        ):
            copies.append(
                pltpu.make_async_copy(
                    own_ref.at[pl.ds(pl.multiple_of(source, 16), count), :],
                    weight_ref.at[pl.ds(i * inner, count), pl.ds(0, rows)],
                    sems.at[i],
                )
            )
        for n, piece in enumerate(given):
            whose = jnp.bitwise_xor(quarter, n)
            for k in range(1, groups):
                for i, count in enumerate((share, share, part)):
                    target = pl.multiple_of(i * inner + whose * count, 16)
                    copies.append(
                        pltpu.make_async_copy(
                            piece.at[pl.ds((k - 1) * sent + i * share, count), :],
                            weight_ref.at[pl.ds(target, count), pl.ds(k * rows, rows)],
                            sems.at[len(copies)],
                        )
                    )
    else:
        copies.append(pltpu.make_async_copy(own_ref, weight_ref, sems.at[0]))
    for copy in copies:
        copy.start()
    if aligned and part * 4 > tail:
        weight_ref[2 * inner + tail :, 0:rows] = jnp.zeros((4 * part - tail, rows), BF)
    for r in range(groups):
        loads[r].wait()
        blocks = [token_ref[r, :, lane_block(aligned, member, k, rows)].astype(F32) for k in range(groups)]
        total = jnp.sum(blocks[0] * blocks[0], axis=-1, keepdims=True)
        for x in blocks[1:]:
            total = total + jnp.sum(x * x, axis=-1, keepdims=True)
        factor = lax.rsqrt(total / model + EPSILON)
        for k in range(groups):
            at = slice(k * rows, (k + 1) * rows)
            normed_ref[r * span : (r + 1) * span, at] = (blocks[k] * factor * gain_ref[:, at]).astype(BF)
    for copy in copies:
        copy.wait()
    keep = pltpu.make_async_copy(weight_ref, weight_out_ref, sems.at[0])
    keep.start()
    width = 384
    total = weight_ref.shape[0] // width

    def column(n, carry):
        at = pl.multiple_of(n * width, LANES)
        for r in range(groups):
            proj_ref[r * span : (r + 1) * span, pl.ds(at, width)] = mm(
                normed_ref[r * span : (r + 1) * span, :], weight_ref[pl.ds(at, width), :], NT
            )
        return carry

    lax.fori_loop(0, total, column, 0)
    keep.wait()


def lane_block(aligned, member, k, rows):
    if aligned:
        return pl.ds(pl.multiple_of(jnp.bitwise_xor(member, k) * rows, LANES), rows)
    return slice(k * rows, (k + 1) * rows)


def conv_forward(x, masks, taps, shift):
    total = shift + taps[KERNEL - 1] * x
    for s in range(1, KERNEL):
        total = total + taps[KERNEL - 1 - s] * (pltpu.roll(x, s, 0) * masks[s - 1])
    return total


def conv_backward(grad, x, masks, taps):
    span = x.shape[0]
    back = taps[KERNEL - 1] * grad
    tap_grads = [None] * KERNEL
    tap_grads[KERNEL - 1] = jnp.sum(grad * x, axis=0, keepdims=True)
    for s in range(1, KERNEL):
        part = grad * masks[s - 1]
        back = back + taps[KERNEL - 1 - s] * pltpu.roll(part, span - s, 0)
        tap_grads[KERNEL - 1 - s] = jnp.sum(part * pltpu.roll(x, s, 0), axis=0, keepdims=True)
    return back, tap_grads


def wide(column, count):
    return jnp.concatenate([column] * (count // LANES), axis=1)


def segment_masks(seg_ref):
    span = seg_ref.shape[-1]
    row = seg_ref[0:1, :]
    column = jnp.broadcast_to(row, (LANES, span)).T
    token = lax.broadcasted_iota(jnp.int32, (span, LANES), 0)
    masks = []
    for s in range(1, KERNEL):
        same = (pltpu.roll(column, s, 0) == column) & (token >= s)
        masks.append(jnp.where(same, 1.0, 0.0))
    return masks, wide(column, span), row


def ordered(span):
    i = lax.broadcasted_iota(jnp.int32, (span, span), 0)
    j = lax.broadcasted_iota(jnp.int32, (span, span), 1)
    return i >= j, i <= j


def row_setup(shared_ref, seg_ref, taps_ref, head_ref, member, per, affinity_ref, kept):
    mask_ref, afft_ref, step_ref, run_ref, runt_ref, raw_ref, act_ref, sum_ref = kept
    masks, column, row = segment_masks(seg_ref)
    after, _ = ordered(row.shape[1])
    for s in range(KERNEL - 1):
        mask_ref[:, s * LANES : (s + 1) * LANES] = masks[s]
    outs = []
    for c in range(2):
        at = slice(c * LANES, (c + 1) * LANES)
        taps = [taps_ref[k : k + 1, at] for k in range(KERNEL)]
        total = conv_forward(shared_ref[:, at], masks, taps, taps_ref[KERNEL : KERNEL + 1, at])
        active = total * sigmoid(total)
        outs.append(active)
        sum_ref[:, at] = total
        act_ref[:, at] = active
    affinity = jnp.where(after & (column == row), mm_fine(outs[1], outs[0], NT), 0.0)
    affinity_ref[...] = affinity
    afft_ref[...] = affinity.T
    raw = pltpu.roll(shared_ref[:, 2 * LANES :], lax.rem(LANES - member * per, LANES), 1)
    raw = raw + head_ref[0:1, :]
    step = jnp.maximum(raw, 0.0) + jnp.log1p(jnp.exp(-jnp.abs(raw)))
    run = mm_ones(jnp.where(after, 1.0, 0.0).astype(BF), -head_ref[1:2, :] * step, NN)
    raw_ref[...] = raw
    step_ref[...] = step
    run_ref[...] = run
    runt_ref[...] = run.T


def pair_columns(pair, run_ref, runt_ref, step_ref):
    back = lax.rem(LANES - 2 * pair, LANES)
    runs = pltpu.roll(run_ref[...], back, 1)
    steps = pltpu.roll(step_ref[...], back, 1)
    lane = lax.broadcasted_iota(jnp.int32, runs.shape, 1)
    low = lane < HEADDIM
    stepx = jnp.where(low, steps[:, 0:1], steps[:, 1:2])
    columns = [runs[:, e : e + 1] for e in range(2)]
    rows = [runt_ref[pl.ds(2 * pair + e, 1), :] for e in range(2)]
    return columns, rows, stepx, low, lane


def forward_kernel(
    per,
    place_ref,
    z_ref,
    v_ref,
    shared_ref,
    seg_ref,
    taps_s_ref,
    taps_v_ref,
    head_ref,
    scanned_ref,
    total_ref,
    gated_ref,
    square_ref,
    mask_ref,
    afft_ref,
    step_ref,
    run_ref,
    runt_ref,
    raw_ref,
    act_ref,
    sum_ref,
    affinity_ref,
    square_sum_ref,
):
    pair = pl.program_id(1)

    @pl.when(pair == 0)
    def _():
        kept = (mask_ref, afft_ref, step_ref, run_ref, runt_ref, raw_ref, act_ref, sum_ref)
        row_setup(shared_ref, seg_ref, taps_s_ref, head_ref, place_ref[0], per, affinity_ref, kept)
        square_sum_ref[...] = jnp.zeros_like(square_sum_ref)

    masks = [mask_ref[:, s * LANES : (s + 1) * LANES] for s in range(KERNEL - 1)]
    count = v_ref.shape[1] // LANES
    squares = 0.0
    for m in range(count):
        lanes = slice(m * LANES, (m + 1) * LANES)
        taps = [taps_v_ref[k : k + 1, lanes] for k in range(KERNEL)]
        total = conv_forward(v_ref[:, lanes], masks, taps, taps_v_ref[KERNEL : KERNEL + 1, lanes])
        total_ref[:, lanes] = total
        values = total * sigmoid(total)
        columns, rows, stepx, low, _ = pair_columns(count * pair + m, run_ref, runt_ref, step_ref)
        fed = (stepx * values).astype(BF)
        skipped = taps_v_ref[KERNEL + 1 : KERNEL + 2, lanes] * values
        cut = fed.shape[0] // 2
        inner = []
        for n in range(2):
            at = slice(n * cut, (n + 1) * cut)
            seen = (n + 1) * cut
            affinity = affinity_ref[at, :seen]
            parts = []
            for e in range(2):
                decay = jnp.exp(jnp.minimum(columns[e][at] - rows[e][:, :seen], 0.0))
                parts.append(mm((decay * affinity).astype(BF), fed[:seen], NN))
            inner.append(jnp.where(low[at], parts[0], parts[1]))
        scanned = jnp.concatenate(inner, axis=0) + skipped
        z = z_ref[:, lanes]
        g = scanned * (z * sigmoid(z))
        scanned_ref[:, lanes] = scanned
        gated_ref[:, lanes] = (g * taps_v_ref[KERNEL + 2 : KERNEL + 3, lanes]).astype(BF)
        squares = squares + g * g
    square_sum_ref[...] = square_sum_ref[...] + squares

    @pl.when(pair == pl.num_programs(1) - 1)
    def _():
        row = jnp.sum(square_sum_ref[...].T, axis=0, keepdims=True)
        square_ref[...] = jnp.broadcast_to(row, square_ref.shape)


def mixgrad_kernel(groups, *refs):
    cots = refs[:groups]
    out_w_ref, gated_ref, square_ref, dm_ref, sums_ref, cot_ref, sems = refs[groups:]
    span = cots[0].shape[0]
    loads = [pltpu.make_async_copy(cots[r], cot_ref.at[r], sems.at[r]) for r in range(groups)]
    for load in loads:
        load.start()
    for load in loads:
        load.wait()
    width = 384 if out_w_ref.shape[0] % 384 == 0 else LANES

    def column(n, carry):
        cols = pl.ds(pl.multiple_of(n * width, LANES), width)
        weight = out_w_ref[cols, :]
        for r in range(groups):
            dm_ref[r * span : (r + 1) * span, cols] = mm(cot_ref[r], weight, NT)
        return carry

    lax.fori_loop(0, out_w_ref.shape[0] // width, column, 0)
    for r in range(groups):
        at = slice(r * span, (r + 1) * span)
        prod = dm_ref[at, :] * gated_ref[at, :].astype(F32)
        part = prod[:, :LANES]
        for c in range(1, prod.shape[1] // LANES):
            part = part + prod[:, c * LANES : (c + 1) * LANES]
        row = jnp.sum(part.T, axis=0, keepdims=True)
        sub = lax.broadcasted_iota(jnp.int32, (8, span), 0)
        sums_ref[8 * r : 8 * r + 8, :] = jnp.where(sub == 0, square_ref[8 * r : 8 * r + 8, :], row)


def outproj_kernel(groups, gated_ref, out_w_ref, *outs):
    span, model = outs[0].shape
    width = 384 if model % 384 == 0 else LANES

    def column(n, carry):
        cols = pl.ds(pl.multiple_of(n * width, LANES), width)
        weight = out_w_ref[:, cols]
        for r in range(groups):
            outs[r][:, cols] = mm(gated_ref[r * span : (r + 1) * span, :], weight, NN).astype(outs[r].dtype)
        return carry

    lax.fori_loop(0, model // width, column, 0)


def gate_scales(parts, width):
    total = parts[0]
    for part in parts[1:]:
        total = total + part
    square, cross = total[0:1, :], total[1:2, :]
    factor = lax.rsqrt(square / width + EPSILON)
    bend = factor * factor * factor * (cross / width)
    span = total.shape[1]
    return (
        jnp.broadcast_to(factor, (LANES, span)).T,
        jnp.broadcast_to(bend, (LANES, span)).T,
    )


def gatebwd_kernel(groups, width, *refs):
    sums = refs[:groups]
    z_ref, scanned_ref, dm_ref, gain_ref, gz_ref, ds_ref, mixed_ref, gate_ref = refs[groups:]
    r = pl.program_id(0)
    factor, bend = gate_scales([s[...] for s in sums], width)

    @pl.when(r == 0)
    def _():
        gate_ref[...] = jnp.zeros_like(gate_ref)

    for c in range(z_ref.shape[1] // LANES):
        at = slice(c * LANES, (c + 1) * LANES)
        gain = gain_ref[0:1, at]
        sz, dsz = silu_parts(z_ref[:, at])
        scanned = scanned_ref[:, at]
        dm = dm_ref[:, at]
        g = scanned * sz
        scaled = g * factor
        dg = factor * (dm * gain) - g * bend
        mixed_ref[:, at] = (scaled * gain).astype(BF)
        gz_ref[:, at] = (dg * scanned * dsz).astype(BF)
        ds_ref[:, at] = dg * sz
        gate_ref[0:1, at] += jnp.sum(dm * scaled, axis=0, keepdims=True)


def backward_kernel(per, first, last, carried, *refs):
    (ds_ref, v_ref, total_in_ref, scanned_ref, mask_ref, afft_ref, step_ref, run_ref, runt_ref, taps_v_ref) = refs[:10]
    refs = refs[10:]
    if carried:
        carry, refs = refs[:3], refs[3:]
    if last:
        (shared_ref, raw_ref, act_ref, sum_ref, seg_ref, taps_s_ref, head_ref, place_ref) = refs[:8]
        gv_ref, vsum_ref, gs_ref, ssum_ref, daff_ref, dstep_ref, drun_ref = refs[8:]
    else:
        gv_ref, vsum_ref, daff_ref, dstep_ref, drun_ref = refs
    row, pair = pl.program_id(0), pl.program_id(1)
    head_pair = pair + first

    @pl.when((row == 0) & (pair == 0))
    def _():
        vsum_ref[...] = jnp.zeros_like(vsum_ref)
        if last:
            ssum_ref[...] = jnp.zeros_like(ssum_ref)

    @pl.when(pair == 0)
    def _():
        for n, target in enumerate((daff_ref, dstep_ref, drun_ref)):
            target[...] = carry[n][...] if carried else jnp.zeros_like(target)

    masks = [mask_ref[:, s * LANES : (s + 1) * LANES] for s in range(KERNEL - 1)]
    taps = [taps_v_ref[k : k + 1, :] for k in range(KERNEL)]
    skip = taps_v_ref[KERNEL + 1 : KERNEL + 2, :]
    values, dvalues = silu_parts(total_in_ref[...])
    columns, rows, stepx, low, lane = pair_columns(head_pair, run_ref, runt_ref, step_ref)
    ds = ds_ref[...]
    dsb = ds.astype(BF)
    fed = (stepx * values).astype(BF)
    zero = jnp.zeros_like(dsb)
    chosen = [jnp.where(low, dsb, zero), jnp.where(low, zero, dsb)]
    cut = fed.shape[0] // 2
    backs = []
    for n in range(2):
        at = slice(n * cut, (n + 1) * cut)
        begin = n * cut
        affinity = afft_ref[at, begin:]
        daff = daff_ref[at, begin:]
        parts = []
        for e in range(2):
            decay = jnp.exp(jnp.minimum(rows[e][:, begin:] - columns[e][at], 0.0))
            parts.append(mm((decay * affinity).astype(BF), dsb[begin:], NN))
            daff = daff + mm(fed[at], chosen[e][begin:], NT) * decay
        daff_ref[at, begin:] = daff
        backs.append(jnp.where(low[at], parts[0], parts[1]))
    back = jnp.concatenate(backs, axis=0)
    inner = scanned_ref[...] - skip * values
    direct = back * values
    moved = dsb.astype(F32) * inner - fed.astype(F32) * back
    dstep, drun = dstep_ref[...], drun_ref[...]
    for e in range(2):
        half = low if e == 0 else ~low
        spot = lane == 2 * head_pair + e
        dstep = dstep + jnp.where(spot, jnp.sum(jnp.where(half, direct, 0.0), axis=1, keepdims=True), 0.0)
        drun = drun + jnp.where(spot, jnp.sum(jnp.where(half, moved, 0.0), axis=1, keepdims=True), 0.0)
    dstep_ref[...] = dstep
    drun_ref[...] = drun
    dtotal = (stepx * back + skip * ds) * dvalues
    dx, tap_grads = conv_backward(dtotal, v_ref[...], masks, taps)
    gv_ref[...] = dx.astype(BF)
    sums = tap_grads + [
        jnp.sum(dtotal, axis=0, keepdims=True),
        jnp.sum(ds * values, axis=0, keepdims=True),
        jnp.zeros((2, LANES), F32),
    ]
    at = pl.ds(pl.multiple_of(pair * LANES, LANES), LANES)
    vsum_ref[:, at] = vsum_ref[:, at] + jnp.concatenate(sums, axis=0)
    if not last:
        return

    @pl.when(pair == pl.num_programs(1) - 1)
    def _():
        _, column, seg_row = segment_masks(seg_ref)
        _, before = ordered(seg_row.shape[1])
        allowed = before & (column == seg_row)
        full = jnp.where(allowed, daff_ref[...], 0.0)
        keys, queries = act_ref[:, :LANES], act_ref[:, LANES:]
        dkeys = mm_fine(full, queries, NN)
        dqueries = mm_fine(full, keys, TN)
        for c, dside in enumerate((dkeys, dqueries)):
            lanes = slice(c * LANES, (c + 1) * LANES)
            taps_c = [taps_s_ref[k : k + 1, lanes] for k in range(KERNEL)]
            dsum = dside * silu_parts(sum_ref[:, lanes])[1]
            dside_x, taps_g = conv_backward(dsum, shared_ref[:, lanes], masks, taps_c)
            gs_ref[:, lanes] = dside_x.astype(BF)
            more = taps_g + [jnp.sum(dsum, axis=0, keepdims=True), jnp.zeros((3, LANES), F32)]
            ssum_ref[:, lanes] = ssum_ref[:, lanes] + jnp.concatenate(more, axis=0)
        ddecay = mm_ones(jnp.where(before, 1.0, 0.0).astype(BF), drun_ref[...], NN)
        rate = -head_ref[1:2, :]
        draw = (dstep_ref[...] + ddecay * rate) * jax.nn.sigmoid(raw_ref[...])
        draw = draw * head_ref[2:3, :]
        gs_ref[:, 2 * LANES :] = pltpu.roll(draw, place_ref[0] * per, 1).astype(BF)
        heads = [
            jnp.sum(draw, axis=0, keepdims=True),
            jnp.sum(ddecay * (rate * step_ref[...]), axis=0, keepdims=True) * head_ref[2:3, :],
            jnp.zeros((6, LANES), F32),
        ]
        ssum_ref[:, 2 * LANES :] = ssum_ref[:, 2 * LANES :] + jnp.concatenate(heads, axis=0)


def weightgrad_kernel(lefts, rights, parts, *refs):
    place_ref = refs[0]
    left_refs = refs[1 : 1 + lefts]
    right_refs = refs[1 + lefts : 1 + lefts + rights]
    given_ref, kept_ref, stage_ref, sems, right_ref, right_sems = refs[1 + lefts + rights :]
    core = place_ref[1]
    model = stage_ref.shape[1]
    loads = [pltpu.make_async_copy(right_refs[n], right_ref.at[n], right_sems.at[n]) for n in range(rights)]
    for load in loads:
        load.start()
    for load in loads:
        load.wait()
    width = 384 if model % 384 == 0 else LANES

    def column(n, carry):
        cols = pl.ds(pl.multiple_of(n * width, LANES), width)
        right = jnp.concatenate([right_ref[n, :, cols] for n in range(rights)], axis=0)
        row = 0
        for ref in left_refs:
            rows = ref.shape[1]
            stage_ref[row : row + rows, cols] = mm(ref[...], right, TN).astype(BF)
            row += rows
        return carry

    lax.fori_loop(0, model // width, column, 0)
    copies = []
    for target, whose in ((given_ref, 1 - core), (kept_ref, core)):
        row = done = 0
        for half in parts:
            copies.append(
                pltpu.make_async_copy(
                    stage_ref.at[pl.ds(pl.multiple_of(row + whose * half, 16), half), :],
                    target.at[pl.ds(done, half), :],
                    sems.at[len(copies)],
                )
            )
            copies[-1].start()
            row += 2 * half
            done += half
    for copy in copies:
        copy.wait()


def weightgrad(place, lefts, rights, parts):
    rows, model = 2 * sum(parts), rights[0].shape[1]
    tokens = lefts[0].shape[0]
    half = jax.ShapeDtypeStruct((rows // 2, model), BF)
    return call(
        partial(weightgrad_kernel, len(lefts), len(rights), parts),
        (half, half),
        2 * tokens * rows * model,
        2 * tokens * (rows + model) + 2 * rows * model,
        in_specs=[pl.BlockSpec(memory_space=pltpu.SMEM)] + [VM] * len(lefts) + [HBM] * len(rights),
        out_specs=(HBM, HBM),
        scratch_shapes=[
            pltpu.VMEM((rows, model), BF),
            pltpu.SemaphoreType.DMA((2 * len(parts),)),
            pltpu.VMEM((len(rights), rights[0].shape[0], model), BF),
            pltpu.SemaphoreType.DMA((len(rights),)),
        ],
    )(place, *lefts, *rights)


def normgrad_kernel(groups, *refs):
    parts, weight_ref, outs = refs[: -groups - 1], refs[-groups - 1], refs[-groups:]
    span = outs[0].shape[0]
    model = weight_ref.shape[1]
    width = 384 if model % 384 == 0 else LANES

    def column(n, carry):
        cols = pl.ds(pl.multiple_of(n * width, LANES), width)
        weight = weight_ref[:, cols]
        for r in range(groups):
            at = slice(r * span, (r + 1) * span)
            terms = jnp.concatenate([part[at, :] for part in parts], axis=1)
            outs[r][:, cols] = mm(terms, weight, NN).astype(outs[r].dtype)
        return carry

    lax.fori_loop(0, model // width, column, 0)


def final_kernel(groups, aligned, width, *refs):
    outs = refs[:groups]
    grads = refs[groups : 2 * groups]
    sums = refs[2 * groups : 3 * groups]
    place_ref, tokens_ref, normal_ref, cot_ref, gain_ref, output_ref, tgrad_ref, gnorm_ref = refs[3 * groups :]
    member = place_ref[0]
    model = gain_ref.shape[1]
    rows = model // groups
    factor = gate_scales([s[...] for s in sums], width)[0]
    total = outs[0][...].astype(F32)
    for part in outs[1:]:
        total = total + part[...].astype(F32)
    output_ref[...] = (tokens_ref[...].astype(F32) + total * factor[:, 0:1]).astype(BF)
    xs, gained, square, cross = [], [], 0.0, 0.0
    for b in range(groups):
        at = slice(b * rows, (b + 1) * rows)
        grad = grads[0][:, at].astype(F32)
        for k in range(1, groups):
            grad = grad + grads[k][:, (b ^ k) * rows : ((b ^ k) + 1) * rows].astype(F32)
        x = normal_ref[:, lane_block(aligned, member, b, rows)].astype(F32)
        more = grad * gain_ref[:, at]
        square = square + jnp.sum(x * x, axis=-1, keepdims=True)
        cross = cross + jnp.sum(more * x, axis=-1, keepdims=True)
        xs.append((x, grad))
        gained.append(more)
    scale = lax.rsqrt(square / model + EPSILON)
    bend = scale * scale * scale * (cross / model)
    for b in range(groups):
        at = slice(b * rows, (b + 1) * rows)
        x, grad = xs[b]
        lanes = lane_block(aligned, member, b, rows)
        tgrad_ref[:, lanes] = (cot_ref[:, lanes].astype(F32) + (gained[b] * scale - x * bend)).astype(BF)
        gnorm_ref[0:1, at] = jnp.sum(grad * (x * scale), axis=0, keepdims=True)


def place_kernel(pieces, groups, *refs):
    place_ref = refs[0]
    count = len(pieces)
    sources = refs[1 : 1 + 2 * count]
    out_ref, stage_ref, sems = refs[-3:]
    member, core = place_ref[0], place_ref[1]
    copies = []
    row = 0
    later = []
    for n, (segments, stride, shared) in enumerate(pieces):
        each = sum(half for half, _ in segments)
        for which in range(2):
            whose = core if which == 0 else 1 - core
            source = sources[2 * n + which]
            for k in range(groups):
                stage_ref[row : row + each, :] = source[k * each : (k + 1) * each, :].astype(F32)
                for half, offset in segments:
                    target = offset + jnp.bitwise_xor(member, k) * stride + whose * half
                    copy = pltpu.make_async_copy(
                        stage_ref.at[pl.ds(row, half), :],
                        out_ref.at[pl.ds(pl.multiple_of(target, 8), half), :],
                        sems.at[len(copies)],
                    )
                    copy.start()
                    copies.append(copy)
                    row += half
            if shared:
                part = source.shape[0] - groups * each
                begin, tail = shared
                stage_ref[row : row + part, :] = source[groups * each :, :].astype(F32)
                later.append((whose, row, begin, part, tail, len(copies) + len(later) + which))
                row += part
    for whose, row, begin, part, tail, sem in later:
        for c, size in ((0, part), (1, tail - part)):

            @pl.when(whose == c)
            def _():
                copy = pltpu.make_async_copy(
                    stage_ref.at[pl.ds(row, size), :], out_ref.at[pl.ds(begin + c * part, size), :], sems.at[sem]
                )
                copy.start()
                copy.wait()

    for copy in copies:
        copy.wait()


def place_rows(place, groups, shape, pieces, values, onto=None):
    rows = sum(v.shape[0] for v in values)
    given = [] if onto is None else [onto]
    return call(
        partial(place_kernel, pieces, groups),
        jax.ShapeDtypeStruct(shape, F32),
        rows * shape[1],
        6 * rows * shape[1],
        in_specs=[pl.BlockSpec(memory_space=pltpu.SMEM)] + [VM] * len(values) + [HBM] * len(given),
        out_specs=HBM,
        scratch_shapes=[
            pltpu.VMEM((rows, shape[1]), F32),
            pltpu.SemaphoreType.DMA((4 * len(pieces) * (groups + 2),)),
        ],
        input_output_aliases={1 + len(values): 0} if given else {},
    )(place, *values, *given)


def swap(value, axis, step):
    size = lax.axis_size(axis)
    return lax.ppermute(value, axis, [(i, i ^ step) for i in range(size)])


def rounded_sum(a, b):
    return (a.astype(F32) + b.astype(F32)).astype(BF)


def line_sum(value):
    size = lax.axis_size(REP)
    bits = size.bit_length() - 1
    last = bits - 2 if bits >= 3 else bits
    for b in range(1, last):
        value = rounded_sum(value, swap(value, REP, 1 << b))
    if bits < 3:
        return value
    low = size // 4
    where = lax.axis_index(REP) // low
    inward = [(low * a + i, low * b + i) for a, b in ((0, 1), (3, 2)) for i in range(low)]
    middle = [(low * a + i, low * b + i) for a, b in ((1, 2), (2, 1)) for i in range(low)]
    outward = [(low * a + i, low * b + i) for a, b in ((1, 0), (2, 3)) for i in range(low)]
    got = lax.ppermute(value, REP, inward)
    value = rounded_sum(value, got)
    got = lax.ppermute(value, REP, middle)
    value = rounded_sum(value, got)
    back = lax.ppermute(value, REP, outward)
    return jnp.where((where == 0) | (where == 3), back, value)


def all_sum(value):
    for axis in (FS, REP):
        size = lax.axis_size(axis)
        step = 1
        while step < size:
            if step * 4 <= size:
                near, far, both = (swap(value, axis, step * m) for m in (1, 2, 3))
                value = (value + near) + (far + both)
                step *= 4
            else:
                value = value + swap(value, axis, step)
                step *= 2
    return value


def to_owners(total, groups):
    rows = total.shape[1] // groups
    blocks = [total[:, k * rows : (k + 1) * rows] for k in range(groups)]
    return [blocks[0]] + [swap(blocks[k], FS, k) for k in range(1, groups)]


def core_sum(halves_):
    given, kept = halves_
    got = swap(given, REP, 1)
    return rounded_sum(kept, got)


def body(
    tokens,
    segment_ids,
    cotangent,
    norm_gain,
    in_weight,
    conv_weight,
    conv_bias,
    step_bias,
    rate_log,
    skip_gain,
    gate_gain,
    out_weight,
):
    groups = lax.axis_size(FS)
    member = lax.axis_index(FS)
    core = lax.axis_index(REP) % 2
    span, model = tokens.shape
    per = HEADS // groups
    inner = per * HEADDIM
    full = inner * groups
    conv = conv_bias.shape[0] * groups
    tail = in_weight.shape[1] - 2 * full
    padded = -(-tail // 384) * 384
    width = 2 * inner + padded
    pairs = per // 2
    whole = groups * span
    quarter = lax.axis_index(REP) % 4
    place = jnp.stack([member, core, quarter]).astype(jnp.int32)

    rows = in_weight.shape[0]
    aligned = rows % LANES == 0
    cols = conv // groups
    smem = pl.BlockSpec(memory_space=pltpu.SMEM)
    weight_t = in_weight.T

    xs = [tokens] + [swap(tokens, FS, k) for k in range(1, groups)]
    small_width = -(-max(rows, cols, span) // LANES) * LANES
    packed = call(
        partial(pack_kernel, groups),
        tuple(jax.ShapeDtypeStruct((width // 4, rows), BF) for _ in range(1, groups))
        + (jax.ShapeDtypeStruct((8, small_width), F32),),
        1,
        4 * width * rows * groups,
        in_specs=[smem, HBM] + [VM] * 4,
        out_specs=(VM,) * groups,
        scratch_shapes=[pltpu.SemaphoreType.DMA((3 * groups,))],
    )(place, weight_t, norm_gain.reshape(1, -1), conv_weight, conv_bias.reshape(1, -1), segment_ids)
    near = [swap(packed[k - 1], FS, k) for k in range(1, groups)]
    own_small = call(
        copy_kernel, jax.ShapeDtypeStruct(packed[-1].shape, F32), 1, 1, in_specs=[VM], out_specs=VM
    )(packed[-1])
    small = [own_small] + [swap(packed[-1], FS, k) for k in range(1, groups)]
    near = jnp.concatenate(near, axis=0)
    across = swap(near, REP, 2)
    given = [near, swap(near, REP, 1), across, swap(across, REP, 1)]
    late, _ = lax.optimization_barrier((cotangent, (near, xs[-1])))
    cots = [cotangent] + [swap(late, FS, k) for k in range(1, groups)]

    gain_x = jnp.concatenate([t[0:1, :rows] for t in small], axis=1)
    order = jnp.arange(groups) ^ member
    table = jnp.take(jnp.stack(small), order, axis=0)
    taps_full = jnp.swapaxes(table[:, 1 : 2 + KERNEL, :cols], 0, 1).reshape(KERNEL + 1, conv)
    own_heads = lambda v: lax.dynamic_slice_in_dim(v.astype(F32), member * per, per, 0)
    taps_v = jnp.concatenate(
        [
            lax.dynamic_slice_in_dim(taps_full, member * inner, inner, 1),
            jnp.repeat(own_heads(skip_gain), HEADDIM).reshape(1, inner),
            gate_gain.astype(F32).reshape(1, inner),
            jnp.zeros((1, inner), F32),
        ],
        axis=0,
    )
    taps_s = jnp.concatenate([taps_full[:, full:], jnp.zeros((3, conv - full), F32)], axis=0)
    spread = lambda v: jnp.pad(v, (0, LANES - per)).reshape(1, LANES)
    heads = jnp.concatenate(
        [
            spread(own_heads(step_bias)),
            spread(jnp.exp(own_heads(rate_log))),
            spread(jnp.ones((per,), F32)),
            jnp.zeros((5, LANES), F32),
        ],
        axis=0,
    )
    segs = jnp.concatenate(
        [jnp.broadcast_to(s[2 + KERNEL : 3 + KERNEL, :span], (8, span)) for s in small], axis=0
    )

    def in_peer_order(value):
        if aligned:
            return value
        return jnp.take(value.reshape(value.shape[0], groups, rows), order, axis=1).reshape(value.shape)

    if aligned:
        sources = [weight_t] + given
    else:
        ranked = jnp.take(jnp.stack(given), jnp.arange(4) ^ quarter, axis=0)
        mine = jnp.concatenate(
            [
                lax.dynamic_slice_in_dim(weight_t, member * inner, inner, 0),
                lax.dynamic_slice_in_dim(weight_t, full + member * inner, inner, 0),
                jnp.pad(weight_t[2 * full :], ((0, padded - tail), (0, 0))),
            ],
            axis=0,
        )
        sent, share = width // 4, inner // 4

        def block(k):
            own = ranked[:, (k - 1) * sent : k * sent]
            pieces = (own[:, :share], own[:, share : 2 * share], own[:, 2 * share :])
            return jnp.concatenate([piece.reshape(-1, rows) for piece in pieces], axis=0)

        sources = [jnp.concatenate([mine] + [block(k) for k in range(1, groups)], axis=1)]
    sems = pltpu.SemaphoreType.DMA((12 * groups,))
    normed, projected, weight = call(
        partial(inproj_kernel, groups, aligned),
        (
            jax.ShapeDtypeStruct((whole, model), BF),
            jax.ShapeDtypeStruct((whole, width), F32),
            jax.ShapeDtypeStruct((width, model), BF),
        ),
        2 * whole * model * width,
        4 * whole * width + 4 * model * width + 4 * whole * model,
        mib=6 * groups,
        in_specs=[HBM] * groups + [VM, smem] + [HBM] * len(sources),
        out_specs=(VM, VM, HBM),
        scratch_shapes=[
            pltpu.VMEM((groups, span, model), BF),
            pltpu.VMEM((width, model), BF),
            sems,
            pltpu.SemaphoreType.DMA((groups,)),
        ],
    )(*[in_peer_order(x) for x in xs], gain_x, place, *sources)

    tile = lambda col: pl.BlockSpec((span, LANES), lambda r, p: (r, col + p))
    per_row = lambda cols_, col: pl.BlockSpec((span, cols_), lambda r, p: (r, col))
    fixed = lambda shape: pl.BlockSpec(shape, lambda r, p: (0, 0))
    pair_cols = pl.BlockSpec((8, LANES), lambda r, p: (0, p))
    seg_spec = pl.BlockSpec((8, span), lambda r, p: (r, 0))
    shared_spec = per_row(padded, 2 * inner // padded)
    scan_flops = 4 * whole * span * inner
    joint = 2 if pairs % 2 == 0 else 1
    broad = lambda col: pl.BlockSpec((span, joint * LANES), lambda r, p: (r, col + p))
    side = lambda w: jax.ShapeDtypeStruct((whole, w), F32)
    flipped_spec = pl.BlockSpec((LANES, span), lambda r, p: (r, 0))
    kept_shapes = (
        side((KERNEL - 1) * LANES),
        side(span),
        side(LANES),
        side(LANES),
        jax.ShapeDtypeStruct((groups * LANES, span), F32),
        side(LANES),
        side(2 * LANES),
        side(2 * LANES),
    )
    kept_specs = (
        per_row((KERNEL - 1) * LANES, 0),
        per_row(span, 0),
        per_row(LANES, 0),
        per_row(LANES, 0),
        flipped_spec,
        per_row(LANES, 0),
        per_row(2 * LANES, 0),
        per_row(2 * LANES, 0),
    )
    scanned, totals, gated, squares, *kept = call(
        partial(forward_kernel, per),
        (
            side(inner),
            side(inner),
            jax.ShapeDtypeStruct((whole, inner), BF),
            jax.ShapeDtypeStruct((8 * groups, span), F32),
        )
        + kept_shapes,
        8 * scan_flops,
        20 * whole * inner,
        mib=12,
        grid=(groups, pairs // joint),
        in_specs=[
            smem,
            broad(0),
            broad(pairs // joint),
            shared_spec,
            seg_spec,
            fixed((8, conv - full)),
            pl.BlockSpec((8, joint * LANES), lambda r, p: (0, p)),
            fixed((8, LANES)),
        ],
        out_specs=(broad(0), broad(0), broad(0), seg_spec) + kept_specs,
        scratch_shapes=[pltpu.VMEM((span, span), F32), pltpu.VMEM((span, LANES), F32)],
    )(place, projected, projected, projected, segs, taps_s, taps_v, heads)

    proj_flops = 2 * whole * inner * model
    dm, sums = call(
        partial(mixgrad_kernel, groups),
        (jax.ShapeDtypeStruct((whole, inner), F32), jax.ShapeDtypeStruct((8 * groups, span), F32)),
        proj_flops,
        2 * whole * model + 6 * whole * inner + 2 * inner * model,
        in_specs=[HBM] * groups + [VM] * 3,
        out_specs=(VM, VM),
        scratch_shapes=[pltpu.VMEM((groups, span, model), BF), pltpu.SemaphoreType.DMA((groups,))],
    )(*cots, out_weight, gated, squares)
    sums_all = [sums] + [swap(sums, FS, k) for k in range(1, groups)]

    outs = call(
        partial(outproj_kernel, groups),
        tuple(jax.ShapeDtypeStruct((span, model), BF if k else F32) for k in range(groups)),
        proj_flops,
        2 * whole * model + 2 * whole * inner + 2 * inner * model,
        in_specs=[VM, VM],
        out_specs=(VM,) * groups,
    )(gated, out_weight)
    outs = [outs[0]] + [swap(outs[k], FS, k) for k in range(1, groups)]

    row_spec = lambda cols_, col=0: pl.BlockSpec((span, cols_), lambda r: (r, col))
    gz, ds, mixed, gate_sum = call(
        partial(gatebwd_kernel, groups, float(full)),
        (
            jax.ShapeDtypeStruct((whole, inner), BF),
            jax.ShapeDtypeStruct((whole, inner), F32),
            jax.ShapeDtypeStruct((whole, inner), BF),
            jax.ShapeDtypeStruct((8, inner), F32),
        ),
        20 * whole * inner,
        20 * whole * inner,
        mib=16,
        grid=(groups,),
        in_specs=[
            pl.BlockSpec((8, span), (lambda k: lambda r: (jnp.bitwise_xor(r, k), 0))(k)) for k in range(groups)
        ]
        + [row_spec(inner), row_spec(inner), row_spec(inner), pl.BlockSpec((8, inner), lambda r: (0, 0))],
        out_specs=(
            row_spec(inner),
            row_spec(inner),
            row_spec(inner),
            pl.BlockSpec((8, inner), lambda r: (0, 0)),
        ),
    )(*sums_all, projected, scanned, dm, jnp.broadcast_to(gate_gain.astype(F32).reshape(1, inner), (8, inner)))

    z_sum = core_sum(weightgrad(place, [gz], [normed], (inner // 2,)))
    o_sum = core_sum(weightgrad(place, [mixed], cots, (inner // 2,)))
    out_part = line_sum(o_sum)
    z_part = line_sum(jnp.concatenate(to_owners(z_sum, groups), axis=0))

    third = pairs // 3
    cuts = (0, third, 2 * third, pairs)
    split = cuts[2]
    carry_shapes = (side(span), side(LANES), side(LANES))
    carry_specs = (per_row(span, 0), per_row(LANES, 0), per_row(LANES, 0))

    def backward(n, carry):
        first, count, last = cuts[n], cuts[n + 1] - cuts[n], n == 2
        cols_ = count * LANES
        outs_ = (jax.ShapeDtypeStruct((whole, cols_), BF), jax.ShapeDtypeStruct((8, cols_), F32))
        specs_ = (tile(0), fixed((8, cols_)))
        scratch, more, more_specs = [], [], []
        if last:
            outs_ += (jax.ShapeDtypeStruct((whole, padded), BF), jax.ShapeDtypeStruct((8, padded), F32))
            specs_ += (per_row(padded, 0), fixed((8, padded)))
            scratch = [
                pltpu.VMEM((span, span), F32),
                pltpu.VMEM((span, LANES), F32),
                pltpu.VMEM((span, LANES), F32),
            ]
            more = [projected, kept[5], kept[6], kept[7], segs, taps_s, heads, place]
            more_specs = [shared_spec, kept_specs[5], kept_specs[6], kept_specs[7], seg_spec]
            more_specs += [fixed((8, conv - full)), fixed((8, LANES)), smem]
        else:
            outs_ += carry_shapes
            specs_ += carry_specs
        return call(
            partial(backward_kernel, per, first, last, len(carry) > 0),
            outs_,
            16 * scan_flops * count // pairs,
            24 * whole * cols_,
            mib=48 if last else 12,
            grid=(groups, count),
            in_specs=[tile(first), tile(pairs + first), tile(first), tile(first)]
            + list(kept_specs[:5])
            + [pl.BlockSpec((8, LANES), lambda r, p: (0, first + p))]
            + (list(carry_specs) if carry else [])
            + more_specs,
            out_specs=specs_,
            scratch_shapes=scratch,
        )(ds, projected, totals, scanned, *kept[:5], taps_v, *carry, *more)

    gva, vsum1, *handed = backward(0, ())
    gvb, vsum2, *handed = backward(1, handed)
    v1_sum = core_sum(weightgrad(place, [gva, gvb], [normed], (third * HEADDIM, third * HEADDIM)))
    gv2, vsum3, gs, ssum = backward(2, handed)
    vsum = jnp.concatenate([vsum1, vsum2, vsum3], axis=1)

    backs = call(
        partial(normgrad_kernel, groups),
        tuple(jax.ShapeDtypeStruct((span, model), BF if k else F32) for k in range(groups)),
        2 * whole * width * model,
        2 * whole * model + 2 * whole * width + 2 * width * model,
        in_specs=[VM] * 6,
        out_specs=(VM,) * groups,
    )(gz, gva, gvb, gv2, gs, weight)
    backs = [backs[0]] + [swap(backs[k], FS, k) for k in range(1, groups)]

    v1_part = line_sum(jnp.concatenate(to_owners(v1_sum, groups), axis=0))
    deep = (pairs - split) * HEADDIM
    s_sum = core_sum(weightgrad(place, [gv2, gs], [normed], (deep, padded // 2)))
    terms = to_owners(s_sum, groups)
    shared_sum = terms[0][deep:].astype(F32)
    for term in terms[1:]:
        shared_sum = shared_sum + term[deep:].astype(F32)
    s_part = line_sum(jnp.concatenate([t[:deep] for t in terms] + [shared_sum.astype(BF)], axis=0))

    whole_spec = lambda shape: pl.BlockSpec(shape, lambda i: (0,) * len(shape))
    output, tokens_grad, norm_sum = call(
        partial(final_kernel, groups, aligned, float(full)),
        (
            jax.ShapeDtypeStruct((span, model), BF),
            jax.ShapeDtypeStruct((span, model), BF),
            jax.ShapeDtypeStruct((8, model), F32),
        ),
        30 * span * model,
        24 * span * model,
        grid=(1,),
        in_specs=[whole_spec((span, model))] * (2 * groups)
        + [pl.BlockSpec((8, span), (lambda k: lambda i: (k, 0))(k)) for k in range(groups)]
        + [smem]
        + [whole_spec((span, model))] * 3
        + [whole_spec((1, model))],
        out_specs=(whole_spec((span, model)), whole_spec((span, model)), whole_spec((8, model))),
    )(*outs, *backs, *sums_all, place, tokens, in_peer_order(tokens), in_peer_order(cotangent), gain_x)
    tokens_grad = in_peer_order(tokens_grad)
    norm_sum = jnp.take(norm_sum[0].reshape(groups, rows), order, axis=0).reshape(1, model)

    def returned(part):
        return [part, swap(part, REP, 1)]

    grad_outproj = place_rows(place, 1, out_weight.shape, ((((inner // 2, 0),), 0, None),), returned(out_part))
    early = returned(z_part) + returned(v1_part)
    gin = place_rows(
        place,
        groups,
        weight_t.shape,
        (
            (((inner // 2, 0),), inner, None),
            (((third * HEADDIM, full), (third * HEADDIM, full + third * 2 * HEADDIM)), inner, None),
        ),
        early,
    )
    grad_inproj = place_rows(
        place,
        groups,
        weight_t.shape,
        ((((deep, full + split * 2 * HEADDIM),), inner, (2 * full, tail)),),
        returned(s_part),
        gin,
    ).T

    own_cols = lambda v: lax.dynamic_update_slice_in_dim(
        jnp.zeros((v.shape[0], full), F32), v, member * inner, 1
    )
    own_spot = lambda v: lax.dynamic_update_slice_in_dim(jnp.zeros((HEADS,), F32), v, member * per, 0)
    taps_grad = jnp.concatenate([own_cols(vsum[: KERNEL + 1]), ssum[: KERNEL + 1, : conv - full]], axis=1)
    head_grads = [
        own_spot(ssum[0, 2 * LANES : 2 * LANES + per]),
        own_spot(ssum[1, 2 * LANES : 2 * LANES + per]),
        own_spot(vsum[KERNEL + 1].reshape(per, HEADDIM).sum(axis=1)),
    ]
    flat = jnp.concatenate(
        [norm_sum[0], taps_grad.reshape(-1), own_cols(gate_sum[:1]).reshape(-1)] + head_grads
    )
    length = flat.shape[0]
    flat = jnp.pad(flat, (0, -length % 1024)).reshape(-1, LANES)
    flat = all_sum(flat).reshape(-1)
    at = 0
    grad_norm = lax.dynamic_slice_in_dim(flat, member * rows, rows, 0)
    at += model
    taps_all = flat[at : at + (KERNEL + 1) * conv].reshape(KERNEL + 1, conv)
    taps_own = lax.dynamic_slice_in_dim(taps_all, member * cols, cols, 1)
    at += (KERNEL + 1) * conv
    grad_gate = lax.dynamic_slice_in_dim(flat, at + member * inner, inner, 0)
    at += full
    return (
        output,
        tokens_grad,
        grad_norm,
        grad_inproj,
        taps_own[:KERNEL],
        taps_own[KERNEL],
        flat[at : at + HEADS],
        flat[at + HEADS : at + 2 * HEADS],
        flat[at + 2 * HEADS : at + 3 * HEADS],
        grad_gate,
        grad_outproj,
    )


def solution(mesh):
    rows = P((REP, FS), None)
    in_specs = (
        rows,
        rows,
        rows,
        P(FS),
        P(FS, None),
        P(None, FS),
        P(FS),
        P(),
        P(),
        P(),
        P(FS),
        P(FS, None),
    )
    out_specs = (
        rows,
        rows,
        P(FS),
        P(FS, None),
        P(None, FS),
        P(FS),
        P(),
        P(),
        P(),
        P(FS),
        P(FS, None),
    )

    return jax.shard_map(body, mesh=mesh, in_specs=in_specs, out_specs=out_specs, check_vma=False)
```

```python
from functools import partial

import jax
import jax.numpy as jnp
from jax import lax
from jax.experimental import pallas as pl
from jax.experimental.pallas import tpu as pltpu
from jax.sharding import PartitionSpec as P


HEADS = 48
HEADDIM = 64
KERNEL = 4
FS = "fsdp"
REP = "rep"
LANES = 128
EPSILON = 1e-05
BF = jnp.bfloat16
F32 = jnp.float32

NN = (((1,), (0,)), ((), ()))
NT = (((1,), (1,)), ((), ()))
TN = (((0,), (0,)), ((), ()))


def mm(a, b, dims):
    return lax.dot_general(a, b, dims, preferred_element_type=F32)


def halves(x):
    top = x.astype(BF)
    return top, (x - top.astype(F32)).astype(BF)


def mm_fine(a, b, dims):
    a_top, a_low = halves(a)
    b_top, b_low = halves(b)
    return mm(a_top, b_top, dims) + (mm(a_top, b_low, dims) + mm(a_low, b_top, dims))


def mm_ones(ones, x, dims):
    top, low = halves(x)
    rest = (x - top.astype(F32) - low.astype(F32)).astype(BF)
    parts = mm(ones, jnp.concatenate([top, low, rest], axis=1), dims)
    lanes = x.shape[1]
    return parts[:, :lanes] + (parts[:, lanes : 2 * lanes] + parts[:, 2 * lanes :])


def sigmoid(v):
    return 0.5 * jnp.tanh(0.5 * v) + 0.5


def silu_parts(v):
    gate = sigmoid(v)
    return v * gate, gate * (1.0 + v * (1.0 - gate))


def call(kernel, out_shape, flops, moved, mib=None, **kw):
    grant = (mib or 4 * lax.axis_size(FS)) * 1024 * 1024

    def run(*operands):
        return pl.pallas_call(
            kernel,
            out_shape=out_shape,
            cost_estimate=pl.CostEstimate(flops=flops, bytes_accessed=moved, transcendentals=0),
            compiler_params=pltpu.CompilerParams(vmem_limit_bytes=grant),
            **kw,
        )(*operands)

    return run


VM = pl.BlockSpec(memory_space=pltpu.VMEM)
HBM = pl.BlockSpec(memory_space=pl.ANY)


def pack_kernel(groups, *refs):
    place_ref, weight_ref, gain_ref, taps_ref, shift_ref, seg_ref = refs[:6]
    sends = refs[6 : 5 + groups]
    small_ref, sems = refs[5 + groups :]
    member, quarter = place_ref[0], place_ref[2]
    inner, share, edge, part, tail = quarter_sizes(sends[0].shape[0], weight_ref.shape[0], groups)
    copies = []
    for k in range(1, groups):
        peer = jnp.bitwise_xor(member, k)
        for i in range(2):
            source = pl.multiple_of(i * (edge // 2) + peer * inner + quarter * share, 16)
            copies.append(
                pltpu.make_async_copy(
                    weight_ref.at[pl.ds(source, share), :],
                    sends[k - 1].at[pl.ds(i * share, share), :],
                    sems.at[2 * k - 2 + i],
                )
            )
    for copy in copies:
        copy.start()
    for q in range(4):
        count = max(0, min(part, tail - q * part))

        @pl.when(quarter == q)
        def _():
            more = [
                pltpu.make_async_copy(
                    weight_ref.at[pl.ds(edge + q * part, count), :],
                    sends[k - 1].at[pl.ds(2 * share, count), :],
                    sems.at[2 * groups - 3 + k],
                )
                for k in range(1, groups)
                if count > 0
            ]
            for copy in more:
                copy.start()
            if count < part:
                for k in range(1, groups):
                    sends[k - 1][2 * share + count :, :] = jnp.zeros((part - count, weight_ref.shape[1]), BF)
            for copy in more:
                copy.wait()

    small_ref[...] = jnp.zeros_like(small_ref)
    small_ref[0:1, : gain_ref.shape[1]] = gain_ref[...].astype(F32)
    small_ref[1 : 1 + KERNEL, : taps_ref.shape[1]] = taps_ref[...].astype(F32)
    small_ref[1 + KERNEL : 2 + KERNEL, : shift_ref.shape[1]] = shift_ref[...].astype(F32)
    small_ref[2 + KERNEL : 3 + KERNEL, : seg_ref.shape[1]] = seg_ref[...].astype(F32)
    for copy in copies:
        copy.wait()


def copy_kernel(source_ref, target_ref):
    target_ref[...] = source_ref[...]


def quarter_sizes(sent, columns, groups):
    full = HEADS * HEADDIM
    inner = full // groups
    return inner, inner // 4, 2 * full, sent - inner // 2, columns - 2 * full


def inproj_kernel(groups, aligned, *refs):
    tokens = refs[:groups]
    gain_ref, place_ref, own_ref = refs[groups : groups + 3]
    given = refs[groups + 3 : -7]
    normed_ref, proj_ref, weight_out_ref, token_ref, weight_ref, sems, token_sems = refs[-7:]
    member, quarter = place_ref[0], place_ref[2]
    model = gain_ref.shape[1]
    rows = model // groups
    span = tokens[0].shape[0]
    loads = [pltpu.make_async_copy(tokens[r], token_ref.at[r], token_sems.at[r]) for r in range(groups)]
    for load in loads:
        load.start()
    copies = []
    if aligned:
        sent = given[0].shape[0] // (groups - 1)
        inner, share, edge, part, tail = quarter_sizes(sent, own_ref.shape[0], groups)
        for i, (source, count) in enumerate(
            ((member * inner, inner), (edge // 2 + member * inner, inner), (edge, tail))
        ):
            copies.append(
                pltpu.make_async_copy(
                    own_ref.at[pl.ds(pl.multiple_of(source, 16), count), :],
                    weight_ref.at[pl.ds(i * inner, count), pl.ds(0, rows)],
                    sems.at[i],
                )
            )
        for n, piece in enumerate(given):
            whose = jnp.bitwise_xor(quarter, n)
            for k in range(1, groups):
                for i, count in enumerate((share, share, part)):
                    target = pl.multiple_of(i * inner + whose * count, 16)
                    copies.append(
                        pltpu.make_async_copy(
                            piece.at[pl.ds((k - 1) * sent + i * share, count), :],
                            weight_ref.at[pl.ds(target, count), pl.ds(k * rows, rows)],
                            sems.at[len(copies)],
                        )
                    )
    else:
        copies.append(pltpu.make_async_copy(own_ref, weight_ref, sems.at[0]))
    for copy in copies:
        copy.start()
    if aligned and part * 4 > tail:
        weight_ref[2 * inner + tail :, 0:rows] = jnp.zeros((4 * part - tail, rows), BF)
    for r in range(groups):
        loads[r].wait()
        blocks = [token_ref[r, :, lane_block(aligned, member, k, rows)].astype(F32) for k in range(groups)]
        total = jnp.sum(blocks[0] * blocks[0], axis=-1, keepdims=True)
        for x in blocks[1:]:
            total = total + jnp.sum(x * x, axis=-1, keepdims=True)
        factor = lax.rsqrt(total / model + EPSILON)
        for k in range(groups):
            at = slice(k * rows, (k + 1) * rows)
            normed_ref[r * span : (r + 1) * span, at] = (blocks[k] * factor * gain_ref[:, at]).astype(BF)
    for copy in copies:
        copy.wait()
    keep = pltpu.make_async_copy(weight_ref, weight_out_ref, sems.at[0])
    keep.start()
    width = 384
    total = weight_ref.shape[0] // width

    def column(n, carry):
        at = pl.multiple_of(n * width, LANES)
        for r in range(groups):
            proj_ref[r * span : (r + 1) * span, pl.ds(at, width)] = mm(
                normed_ref[r * span : (r + 1) * span, :], weight_ref[pl.ds(at, width), :], NT
            )
        return carry

    lax.fori_loop(0, total, column, 0)
    keep.wait()


def lane_block(aligned, member, k, rows):
    if aligned:
        return pl.ds(pl.multiple_of(jnp.bitwise_xor(member, k) * rows, LANES), rows)
    return slice(k * rows, (k + 1) * rows)


def conv_forward(x, masks, taps, shift):
    total = shift + taps[KERNEL - 1] * x
    for s in range(1, KERNEL):
        total = total + taps[KERNEL - 1 - s] * (pltpu.roll(x, s, 0) * masks[s - 1])
    return total


def conv_backward(grad, x, masks, taps):
    span = x.shape[0]
    back = taps[KERNEL - 1] * grad
    tap_grads = [None] * KERNEL
    tap_grads[KERNEL - 1] = jnp.sum(grad * x, axis=0, keepdims=True)
    for s in range(1, KERNEL):
        part = grad * masks[s - 1]
        back = back + taps[KERNEL - 1 - s] * pltpu.roll(part, span - s, 0)
        tap_grads[KERNEL - 1 - s] = jnp.sum(part * pltpu.roll(x, s, 0), axis=0, keepdims=True)
    return back, tap_grads


def wide(column, count):
    return jnp.concatenate([column] * (count // LANES), axis=1)


def segment_masks(seg_ref):
    span = seg_ref.shape[-1]
    row = seg_ref[0:1, :]
    column = jnp.broadcast_to(row, (LANES, span)).T
    token = lax.broadcasted_iota(jnp.int32, (span, LANES), 0)
    masks = []
    for s in range(1, KERNEL):
        same = (pltpu.roll(column, s, 0) == column) & (token >= s)
        masks.append(jnp.where(same, 1.0, 0.0))
    return masks, wide(column, span), row


def ordered(span):
    i = lax.broadcasted_iota(jnp.int32, (span, span), 0)
    j = lax.broadcasted_iota(jnp.int32, (span, span), 1)
    return i >= j, i <= j


def row_setup(shared_ref, seg_ref, taps_ref, head_ref, member, per, affinity_ref, kept):
    mask_ref, afft_ref, step_ref, run_ref, runt_ref, raw_ref, act_ref, sum_ref = kept
    masks, column, row = segment_masks(seg_ref)
    after, _ = ordered(row.shape[1])
    for s in range(KERNEL - 1):
        mask_ref[:, s * LANES : (s + 1) * LANES] = masks[s]
    outs = []
    for c in range(2):
        at = slice(c * LANES, (c + 1) * LANES)
        taps = [taps_ref[k : k + 1, at] for k in range(KERNEL)]
        total = conv_forward(shared_ref[:, at], masks, taps, taps_ref[KERNEL : KERNEL + 1, at])
        active = total * sigmoid(total)
        outs.append(active)
        sum_ref[:, at] = total
        act_ref[:, at] = active
    affinity = jnp.where(after & (column == row), mm_fine(outs[1], outs[0], NT), 0.0)
    affinity_ref[...] = affinity
    afft_ref[...] = affinity.T
    raw = pltpu.roll(shared_ref[:, 2 * LANES :], lax.rem(LANES - member * per, LANES), 1)
    raw = raw + head_ref[0:1, :]
    step = jnp.maximum(raw, 0.0) + jnp.log1p(jnp.exp(-jnp.abs(raw)))
    run = mm_ones(jnp.where(after, 1.0, 0.0).astype(BF), -head_ref[1:2, :] * step, NN)
    raw_ref[...] = raw
    step_ref[...] = step
    run_ref[...] = run
    runt_ref[...] = run.T


def pair_columns(pair, run_ref, runt_ref, step_ref):
    back = lax.rem(LANES - 2 * pair, LANES)
    runs = pltpu.roll(run_ref[...], back, 1)
    steps = pltpu.roll(step_ref[...], back, 1)
    lane = lax.broadcasted_iota(jnp.int32, runs.shape, 1)
    low = lane < HEADDIM
    stepx = jnp.where(low, steps[:, 0:1], steps[:, 1:2])
    columns = [runs[:, e : e + 1] for e in range(2)]
    rows = [runt_ref[pl.ds(2 * pair + e, 1), :] for e in range(2)]
    return columns, rows, stepx, low, lane


def forward_kernel(
    per,
    place_ref,
    z_ref,
    v_ref,
    shared_ref,
    seg_ref,
    taps_s_ref,
    taps_v_ref,
    head_ref,
    scanned_ref,
    total_ref,
    gated_ref,
    square_ref,
    mask_ref,
    afft_ref,
    step_ref,
    run_ref,
    runt_ref,
    raw_ref,
    act_ref,
    sum_ref,
    affinity_ref,
    square_sum_ref,
):
    pair = pl.program_id(1)

    @pl.when(pair == 0)
    def _():
        kept = (mask_ref, afft_ref, step_ref, run_ref, runt_ref, raw_ref, act_ref, sum_ref)
        row_setup(shared_ref, seg_ref, taps_s_ref, head_ref, place_ref[0], per, affinity_ref, kept)
        square_sum_ref[...] = jnp.zeros_like(square_sum_ref)

    masks = [mask_ref[:, s * LANES : (s + 1) * LANES] for s in range(KERNEL - 1)]
    count = v_ref.shape[1] // LANES
    squares = 0.0
    for m in range(count):
        lanes = slice(m * LANES, (m + 1) * LANES)
        taps = [taps_v_ref[k : k + 1, lanes] for k in range(KERNEL)]
        total = conv_forward(v_ref[:, lanes], masks, taps, taps_v_ref[KERNEL : KERNEL + 1, lanes])
        total_ref[:, lanes] = total
        values = total * sigmoid(total)
        columns, rows, stepx, low, _ = pair_columns(count * pair + m, run_ref, runt_ref, step_ref)
        fed = (stepx * values).astype(BF)
        skipped = taps_v_ref[KERNEL + 1 : KERNEL + 2, lanes] * values
        cut = fed.shape[0] // 2
        inner = []
        for n in range(2):
            at = slice(n * cut, (n + 1) * cut)
            seen = (n + 1) * cut
            affinity = affinity_ref[at, :seen]
            parts = []
            for e in range(2):
                decay = jnp.exp(jnp.minimum(columns[e][at] - rows[e][:, :seen], 0.0))
                parts.append(mm((decay * affinity).astype(BF), fed[:seen], NN))
            inner.append(jnp.where(low[at], parts[0], parts[1]))
        scanned = jnp.concatenate(inner, axis=0) + skipped
        z = z_ref[:, lanes]
        g = scanned * (z * sigmoid(z))
        scanned_ref[:, lanes] = scanned
        gated_ref[:, lanes] = (g * taps_v_ref[KERNEL + 2 : KERNEL + 3, lanes]).astype(BF)
        squares = squares + g * g
    square_sum_ref[...] = square_sum_ref[...] + squares

    @pl.when(pair == pl.num_programs(1) - 1)
    def _():
        row = jnp.sum(square_sum_ref[...].T, axis=0, keepdims=True)
        square_ref[...] = jnp.broadcast_to(row, square_ref.shape)


def mixgrad_kernel(groups, *refs):
    cots = refs[:groups]
    out_w_ref, gated_ref, square_ref, dm_ref, sums_ref, cot_ref, sems = refs[groups:]
    span = cots[0].shape[0]
    loads = [pltpu.make_async_copy(cots[r], cot_ref.at[r], sems.at[r]) for r in range(groups)]
    for load in loads:
        load.start()
    for load in loads:
        load.wait()
    width = 384 if out_w_ref.shape[0] % 384 == 0 else LANES

    def column(n, carry):
        cols = pl.ds(pl.multiple_of(n * width, LANES), width)
        weight = out_w_ref[cols, :]
        for r in range(groups):
            dm_ref[r * span : (r + 1) * span, cols] = mm(cot_ref[r], weight, NT)
        return carry

    lax.fori_loop(0, out_w_ref.shape[0] // width, column, 0)
    for r in range(groups):
        at = slice(r * span, (r + 1) * span)
        prod = dm_ref[at, :] * gated_ref[at, :].astype(F32)
        part = prod[:, :LANES]
        for c in range(1, prod.shape[1] // LANES):
            part = part + prod[:, c * LANES : (c + 1) * LANES]
        row = jnp.sum(part.T, axis=0, keepdims=True)
        sub = lax.broadcasted_iota(jnp.int32, (8, span), 0)
        sums_ref[8 * r : 8 * r + 8, :] = jnp.where(sub == 0, square_ref[8 * r : 8 * r + 8, :], row)


def outproj_kernel(groups, gated_ref, out_w_ref, *outs):
    span, model = outs[0].shape
    width = 384 if model % 384 == 0 else LANES

    def column(n, carry):
        cols = pl.ds(pl.multiple_of(n * width, LANES), width)
        weight = out_w_ref[:, cols]
        for r in range(groups):
            outs[r][:, cols] = mm(gated_ref[r * span : (r + 1) * span, :], weight, NN).astype(outs[r].dtype)
        return carry

    lax.fori_loop(0, model // width, column, 0)


def gate_scales(parts, width):
    total = parts[0]
    for part in parts[1:]:
        total = total + part
    square, cross = total[0:1, :], total[1:2, :]
    factor = lax.rsqrt(square / width + EPSILON)
    bend = factor * factor * factor * (cross / width)
    span = total.shape[1]
    return (
        jnp.broadcast_to(factor, (LANES, span)).T,
        jnp.broadcast_to(bend, (LANES, span)).T,
    )


def gatebwd_kernel(groups, width, *refs):
    sums = refs[:groups]
    z_ref, scanned_ref, dm_ref, gain_ref, gz_ref, ds_ref, mixed_ref, gate_ref = refs[groups:]
    r = pl.program_id(0)
    factor, bend = gate_scales([s[...] for s in sums], width)

    @pl.when(r == 0)
    def _():
        gate_ref[...] = jnp.zeros_like(gate_ref)

    for c in range(z_ref.shape[1] // LANES):
        at = slice(c * LANES, (c + 1) * LANES)
        gain = gain_ref[0:1, at]
        sz, dsz = silu_parts(z_ref[:, at])
        scanned = scanned_ref[:, at]
        dm = dm_ref[:, at]
        g = scanned * sz
        scaled = g * factor
        dg = factor * (dm * gain) - g * bend
        mixed_ref[:, at] = (scaled * gain).astype(BF)
        gz_ref[:, at] = (dg * scanned * dsz).astype(BF)
        ds_ref[:, at] = dg * sz
        gate_ref[0:1, at] += jnp.sum(dm * scaled, axis=0, keepdims=True)


def backward_kernel(per, first, last, carried, *refs):
    (ds_ref, v_ref, total_in_ref, scanned_ref, mask_ref, afft_ref, step_ref, run_ref, runt_ref, taps_v_ref) = refs[:10]
    refs = refs[10:]
    if carried:
        carry, refs = refs[:3], refs[3:]
    if last:
        (shared_ref, raw_ref, act_ref, sum_ref, seg_ref, taps_s_ref, head_ref, place_ref) = refs[:8]
        gv_ref, vsum_ref, gs_ref, ssum_ref, daff_ref, dstep_ref, drun_ref = refs[8:]
    else:
        gv_ref, vsum_ref, daff_ref, dstep_ref, drun_ref = refs
    row, pair = pl.program_id(0), pl.program_id(1)
    head_pair = pair + first

    @pl.when((row == 0) & (pair == 0))
    def _():
        vsum_ref[...] = jnp.zeros_like(vsum_ref)
        if last:
            ssum_ref[...] = jnp.zeros_like(ssum_ref)

    @pl.when(pair == 0)
    def _():
        for n, target in enumerate((daff_ref, dstep_ref, drun_ref)):
            target[...] = carry[n][...] if carried else jnp.zeros_like(target)

    masks = [mask_ref[:, s * LANES : (s + 1) * LANES] for s in range(KERNEL - 1)]
    taps = [taps_v_ref[k : k + 1, :] for k in range(KERNEL)]
    skip = taps_v_ref[KERNEL + 1 : KERNEL + 2, :]
    values, dvalues = silu_parts(total_in_ref[...])
    columns, rows, stepx, low, lane = pair_columns(head_pair, run_ref, runt_ref, step_ref)
    ds = ds_ref[...]
    dsb = ds.astype(BF)
    fed = (stepx * values).astype(BF)
    zero = jnp.zeros_like(dsb)
    chosen = [jnp.where(low, dsb, zero), jnp.where(low, zero, dsb)]
    cut = fed.shape[0] // 2
    backs = []
    for n in range(2):
        at = slice(n * cut, (n + 1) * cut)
        begin = n * cut
        affinity = afft_ref[at, begin:]
        daff = daff_ref[at, begin:]
        parts = []
        for e in range(2):
            decay = jnp.exp(jnp.minimum(rows[e][:, begin:] - columns[e][at], 0.0))
            parts.append(mm((decay * affinity).astype(BF), dsb[begin:], NN))
            daff = daff + mm(fed[at], chosen[e][begin:], NT) * decay
        daff_ref[at, begin:] = daff
        backs.append(jnp.where(low[at], parts[0], parts[1]))
    back = jnp.concatenate(backs, axis=0)
    inner = scanned_ref[...] - skip * values
    direct = back * values
    moved = dsb.astype(F32) * inner - fed.astype(F32) * back
    dstep, drun = dstep_ref[...], drun_ref[...]
    for e in range(2):
        half = low if e == 0 else ~low
        spot = lane == 2 * head_pair + e
        dstep = dstep + jnp.where(spot, jnp.sum(jnp.where(half, direct, 0.0), axis=1, keepdims=True), 0.0)
        drun = drun + jnp.where(spot, jnp.sum(jnp.where(half, moved, 0.0), axis=1, keepdims=True), 0.0)
    dstep_ref[...] = dstep
    drun_ref[...] = drun
    dtotal = (stepx * back + skip * ds) * dvalues
    dx, tap_grads = conv_backward(dtotal, v_ref[...], masks, taps)
    gv_ref[...] = dx.astype(BF)
    sums = tap_grads + [
        jnp.sum(dtotal, axis=0, keepdims=True),
        jnp.sum(ds * values, axis=0, keepdims=True),
        jnp.zeros((2, LANES), F32),
    ]
    at = pl.ds(pl.multiple_of(pair * LANES, LANES), LANES)
    vsum_ref[:, at] = vsum_ref[:, at] + jnp.concatenate(sums, axis=0)
    if not last:
        return

    @pl.when(pair == pl.num_programs(1) - 1)
    def _():
        _, column, seg_row = segment_masks(seg_ref)
        _, before = ordered(seg_row.shape[1])
        allowed = before & (column == seg_row)
        full = jnp.where(allowed, daff_ref[...], 0.0)
        keys, queries = act_ref[:, :LANES], act_ref[:, LANES:]
        dkeys = mm_fine(full, queries, NN)
        dqueries = mm_fine(full, keys, TN)
        for c, dside in enumerate((dkeys, dqueries)):
            lanes = slice(c * LANES, (c + 1) * LANES)
            taps_c = [taps_s_ref[k : k + 1, lanes] for k in range(KERNEL)]
            dsum = dside * silu_parts(sum_ref[:, lanes])[1]
            dside_x, taps_g = conv_backward(dsum, shared_ref[:, lanes], masks, taps_c)
            gs_ref[:, lanes] = dside_x.astype(BF)
            more = taps_g + [jnp.sum(dsum, axis=0, keepdims=True), jnp.zeros((3, LANES), F32)]
            ssum_ref[:, lanes] = ssum_ref[:, lanes] + jnp.concatenate(more, axis=0)
        ddecay = mm_ones(jnp.where(before, 1.0, 0.0).astype(BF), drun_ref[...], NN)
        rate = -head_ref[1:2, :]
        draw = (dstep_ref[...] + ddecay * rate) * jax.nn.sigmoid(raw_ref[...])
        draw = draw * head_ref[2:3, :]
        gs_ref[:, 2 * LANES :] = pltpu.roll(draw, place_ref[0] * per, 1).astype(BF)
        heads = [
            jnp.sum(draw, axis=0, keepdims=True),
            jnp.sum(ddecay * (rate * step_ref[...]), axis=0, keepdims=True) * head_ref[2:3, :],
            jnp.zeros((6, LANES), F32),
        ]
        ssum_ref[:, 2 * LANES :] = ssum_ref[:, 2 * LANES :] + jnp.concatenate(heads, axis=0)


def weightgrad_kernel(lefts, rights, parts, *refs):
    place_ref = refs[0]
    left_refs = refs[1 : 1 + lefts]
    right_refs = refs[1 + lefts : 1 + lefts + rights]
    given_ref, kept_ref, stage_ref, sems = refs[1 + lefts + rights :]
    core = place_ref[1]
    model = stage_ref.shape[1]
    width = 384 if model % 384 == 0 else LANES

    def column(n, carry):
        cols = pl.ds(pl.multiple_of(n * width, LANES), width)
        right = jnp.concatenate([ref[:, cols] for ref in right_refs], axis=0)
        row = 0
        for ref in left_refs:
            rows = ref.shape[1]
            stage_ref[row : row + rows, cols] = mm(ref[...], right, TN).astype(BF)
            row += rows
        return carry

    lax.fori_loop(0, model // width, column, 0)
    copies = []
    for target, whose in ((given_ref, 1 - core), (kept_ref, core)):
        row = done = 0
        for half in parts:
            copies.append(
                pltpu.make_async_copy(
                    stage_ref.at[pl.ds(pl.multiple_of(row + whose * half, 16), half), :],
                    target.at[pl.ds(done, half), :],
                    sems.at[len(copies)],
                )
            )
            copies[-1].start()
            row += 2 * half
            done += half
    for copy in copies:
        copy.wait()


def weightgrad(place, lefts, rights, parts):
    rows, model = 2 * sum(parts), rights[0].shape[1]
    tokens = lefts[0].shape[0]
    half = jax.ShapeDtypeStruct((rows // 2, model), BF)
    return call(
        partial(weightgrad_kernel, len(lefts), len(rights), parts),
        (half, half),
        2 * tokens * rows * model,
        2 * tokens * (rows + model) + 2 * rows * model,
        in_specs=[pl.BlockSpec(memory_space=pltpu.SMEM)] + [VM] * (len(lefts) + len(rights)),
        out_specs=(HBM, HBM),
        scratch_shapes=[
            pltpu.VMEM((rows, model), BF),
            pltpu.SemaphoreType.DMA((2 * len(parts),)),
        ],
    )(place, *lefts, *rights)


def normgrad_kernel(groups, *refs):
    parts, weight_ref, outs = refs[: -groups - 1], refs[-groups - 1], refs[-groups:]
    span = outs[0].shape[0]
    model = weight_ref.shape[1]
    width = 384 if model % 384 == 0 else LANES

    def column(n, carry):
        cols = pl.ds(pl.multiple_of(n * width, LANES), width)
        weight = weight_ref[:, cols]
        for r in range(groups):
            at = slice(r * span, (r + 1) * span)
            terms = jnp.concatenate([part[at, :] for part in parts], axis=1)
            outs[r][:, cols] = mm(terms, weight, NN).astype(outs[r].dtype)
        return carry

    lax.fori_loop(0, model // width, column, 0)


def final_kernel(groups, aligned, width, *refs):
    outs = refs[:groups]
    grads = refs[groups : 2 * groups]
    sums = refs[2 * groups : 3 * groups]
    place_ref, tokens_ref, normal_ref, cot_ref, gain_ref, output_ref, tgrad_ref, gnorm_ref = refs[3 * groups :]
    member = place_ref[0]
    model = gain_ref.shape[1]
    rows = model // groups
    factor = gate_scales([s[...] for s in sums], width)[0]
    total = outs[0][...].astype(F32)
    for part in outs[1:]:
        total = total + part[...].astype(F32)
    output_ref[...] = (tokens_ref[...].astype(F32) + total * factor[:, 0:1]).astype(BF)
    xs, gained, square, cross = [], [], 0.0, 0.0
    for b in range(groups):
        at = slice(b * rows, (b + 1) * rows)
        grad = grads[0][:, at].astype(F32)
        for k in range(1, groups):
            grad = grad + grads[k][:, (b ^ k) * rows : ((b ^ k) + 1) * rows].astype(F32)
        x = normal_ref[:, lane_block(aligned, member, b, rows)].astype(F32)
        more = grad * gain_ref[:, at]
        square = square + jnp.sum(x * x, axis=-1, keepdims=True)
        cross = cross + jnp.sum(more * x, axis=-1, keepdims=True)
        xs.append((x, grad))
        gained.append(more)
    scale = lax.rsqrt(square / model + EPSILON)
    bend = scale * scale * scale * (cross / model)
    for b in range(groups):
        at = slice(b * rows, (b + 1) * rows)
        x, grad = xs[b]
        lanes = lane_block(aligned, member, b, rows)
        tgrad_ref[:, lanes] = (cot_ref[:, lanes].astype(F32) + (gained[b] * scale - x * bend)).astype(BF)
        gnorm_ref[0:1, at] = jnp.sum(grad * (x * scale), axis=0, keepdims=True)


def place_kernel(pieces, groups, *refs):
    place_ref = refs[0]
    count = len(pieces)
    sources = refs[1 : 1 + 2 * count]
    out_ref, stage_ref, sems = refs[-3:]
    member, core = place_ref[0], place_ref[1]
    copies = []
    row = 0
    later = []
    for n, (segments, stride, shared) in enumerate(pieces):
        each = sum(half for half, _ in segments)
        for which in range(2):
            whose = core if which == 0 else 1 - core
            source = sources[2 * n + which]
            for k in range(groups):
                stage_ref[row : row + each, :] = source[k * each : (k + 1) * each, :].astype(F32)
                for half, offset in segments:
                    target = offset + jnp.bitwise_xor(member, k) * stride + whose * half
                    copy = pltpu.make_async_copy(
                        stage_ref.at[pl.ds(row, half), :],
                        out_ref.at[pl.ds(pl.multiple_of(target, 8), half), :],
                        sems.at[len(copies)],
                    )
                    copy.start()
                    copies.append(copy)
                    row += half
            if shared:
                part = source.shape[0] - groups * each
                begin, tail = shared
                stage_ref[row : row + part, :] = source[groups * each :, :].astype(F32)
                later.append((whose, row, begin, part, tail, len(copies) + len(later) + which))
                row += part
    for whose, row, begin, part, tail, sem in later:
        for c, size in ((0, part), (1, tail - part)):

            @pl.when(whose == c)
            def _():
                copy = pltpu.make_async_copy(
                    stage_ref.at[pl.ds(row, size), :], out_ref.at[pl.ds(begin + c * part, size), :], sems.at[sem]
                )
                copy.start()
                copy.wait()

    for copy in copies:
        copy.wait()


def place_rows(place, groups, shape, pieces, values, onto=None):
    rows = sum(v.shape[0] for v in values)
    given = [] if onto is None else [onto]
    return call(
        partial(place_kernel, pieces, groups),
        jax.ShapeDtypeStruct(shape, F32),
        rows * shape[1],
        6 * rows * shape[1],
        in_specs=[pl.BlockSpec(memory_space=pltpu.SMEM)] + [VM] * len(values) + [HBM] * len(given),
        out_specs=HBM,
        scratch_shapes=[
            pltpu.VMEM((rows, shape[1]), F32),
            pltpu.SemaphoreType.DMA((4 * len(pieces) * (groups + 2),)),
        ],
        input_output_aliases={1 + len(values): 0} if given else {},
    )(place, *values, *given)


def swap(value, axis, step):
    size = lax.axis_size(axis)
    return lax.ppermute(value, axis, [(i, i ^ step) for i in range(size)])


def rounded_sum(a, b):
    return (a.astype(F32) + b.astype(F32)).astype(BF)


def line_sum(value):
    size = lax.axis_size(REP)
    bits = size.bit_length() - 1
    last = bits - 2 if bits >= 3 else bits
    for b in range(1, last):
        value = rounded_sum(value, swap(value, REP, 1 << b))
    if bits < 3:
        return value
    low = size // 4
    where = lax.axis_index(REP) // low
    inward = [(low * a + i, low * b + i) for a, b in ((0, 1), (3, 2)) for i in range(low)]
    middle = [(low * a + i, low * b + i) for a, b in ((1, 2), (2, 1)) for i in range(low)]
    outward = [(low * a + i, low * b + i) for a, b in ((1, 0), (2, 3)) for i in range(low)]
    got = lax.ppermute(value, REP, inward)
    value = rounded_sum(value, got)
    got = lax.ppermute(value, REP, middle)
    value = rounded_sum(value, got)
    back = lax.ppermute(value, REP, outward)
    return jnp.where((where == 0) | (where == 3), back, value)


def all_sum(value):
    for axis in (FS, REP):
        size = lax.axis_size(axis)
        step = 1
        while step < size:
            if step * 4 <= size:
                near, far, both = (swap(value, axis, step * m) for m in (1, 2, 3))
                value = (value + near) + (far + both)
                step *= 4
            else:
                value = value + swap(value, axis, step)
                step *= 2
    return value


def to_owners(total, groups):
    rows = total.shape[1] // groups
    blocks = [total[:, k * rows : (k + 1) * rows] for k in range(groups)]
    return [blocks[0]] + [swap(blocks[k], FS, k) for k in range(1, groups)]


def core_sum(halves_):
    given, kept = halves_
    got = swap(given, REP, 1)
    return rounded_sum(kept, got)


def body(
    tokens,
    segment_ids,
    cotangent,
    norm_gain,
    in_weight,
    conv_weight,
    conv_bias,
    step_bias,
    rate_log,
    skip_gain,
    gate_gain,
    out_weight,
):
    groups = lax.axis_size(FS)
    member = lax.axis_index(FS)
    core = lax.axis_index(REP) % 2
    span, model = tokens.shape
    per = HEADS // groups
    inner = per * HEADDIM
    full = inner * groups
    conv = conv_bias.shape[0] * groups
    tail = in_weight.shape[1] - 2 * full
    padded = -(-tail // 384) * 384
    width = 2 * inner + padded
    pairs = per // 2
    whole = groups * span
    quarter = lax.axis_index(REP) % 4
    place = jnp.stack([member, core, quarter]).astype(jnp.int32)

    rows = in_weight.shape[0]
    aligned = rows % LANES == 0
    cols = conv // groups
    smem = pl.BlockSpec(memory_space=pltpu.SMEM)
    weight_t = in_weight.T

    xs = [tokens] + [swap(tokens, FS, k) for k in range(1, groups)]
    small_width = -(-max(rows, cols, span) // LANES) * LANES
    packed = call(
        partial(pack_kernel, groups),
        tuple(jax.ShapeDtypeStruct((width // 4, rows), BF) for _ in range(1, groups))
        + (jax.ShapeDtypeStruct((8, small_width), F32),),
        1,
        4 * width * rows * groups,
        in_specs=[smem, HBM] + [VM] * 4,
        out_specs=(VM,) * groups,
        scratch_shapes=[pltpu.SemaphoreType.DMA((3 * groups,))],
    )(place, weight_t, norm_gain.reshape(1, -1), conv_weight, conv_bias.reshape(1, -1), segment_ids)
    near = [swap(packed[k - 1], FS, k) for k in range(1, groups)]
    own_small = call(
        copy_kernel, jax.ShapeDtypeStruct(packed[-1].shape, F32), 1, 1, in_specs=[VM], out_specs=VM
    )(packed[-1])
    small = [own_small] + [swap(packed[-1], FS, k) for k in range(1, groups)]
    near = jnp.concatenate(near, axis=0)
    across = swap(near, REP, 2)
    given = [near, swap(near, REP, 1), across, swap(across, REP, 1)]
    late, _ = lax.optimization_barrier((cotangent, (near, xs[-1])))
    cots = [cotangent] + [swap(late, FS, k) for k in range(1, groups)]

    gain_x = jnp.concatenate([t[0:1, :rows] for t in small], axis=1)
    order = jnp.arange(groups) ^ member
    table = jnp.take(jnp.stack(small), order, axis=0)
    taps_full = jnp.swapaxes(table[:, 1 : 2 + KERNEL, :cols], 0, 1).reshape(KERNEL + 1, conv)
    own_heads = lambda v: lax.dynamic_slice_in_dim(v.astype(F32), member * per, per, 0)
    taps_v = jnp.concatenate(
        [
            lax.dynamic_slice_in_dim(taps_full, member * inner, inner, 1),
            jnp.repeat(own_heads(skip_gain), HEADDIM).reshape(1, inner),
            gate_gain.astype(F32).reshape(1, inner),
            jnp.zeros((1, inner), F32),
        ],
        axis=0,
    )
    taps_s = jnp.concatenate([taps_full[:, full:], jnp.zeros((3, conv - full), F32)], axis=0)
    spread = lambda v: jnp.pad(v, (0, LANES - per)).reshape(1, LANES)
    heads = jnp.concatenate(
        [
            spread(own_heads(step_bias)),
            spread(jnp.exp(own_heads(rate_log))),
            spread(jnp.ones((per,), F32)),
            jnp.zeros((5, LANES), F32),
        ],
        axis=0,
    )
    segs = jnp.concatenate(
        [jnp.broadcast_to(s[2 + KERNEL : 3 + KERNEL, :span], (8, span)) for s in small], axis=0
    )

    def in_peer_order(value):
        if aligned:
            return value
        return jnp.take(value.reshape(value.shape[0], groups, rows), order, axis=1).reshape(value.shape)

    if aligned:
        sources = [weight_t] + given
    else:
        ranked = jnp.take(jnp.stack(given), jnp.arange(4) ^ quarter, axis=0)
        mine = jnp.concatenate(
            [
                lax.dynamic_slice_in_dim(weight_t, member * inner, inner, 0),
                lax.dynamic_slice_in_dim(weight_t, full + member * inner, inner, 0),
                jnp.pad(weight_t[2 * full :], ((0, padded - tail), (0, 0))),
            ],
            axis=0,
        )
        sent, share = width // 4, inner // 4

        def block(k):
            own = ranked[:, (k - 1) * sent : k * sent]
            pieces = (own[:, :share], own[:, share : 2 * share], own[:, 2 * share :])
            return jnp.concatenate([piece.reshape(-1, rows) for piece in pieces], axis=0)

        sources = [jnp.concatenate([mine] + [block(k) for k in range(1, groups)], axis=1)]
    sems = pltpu.SemaphoreType.DMA((12 * groups,))
    normed, projected, weight = call(
        partial(inproj_kernel, groups, aligned),
        (
            jax.ShapeDtypeStruct((whole, model), BF),
            jax.ShapeDtypeStruct((whole, width), F32),
            jax.ShapeDtypeStruct((width, model), BF),
        ),
        2 * whole * model * width,
        4 * whole * width + 4 * model * width + 4 * whole * model,
        mib=6 * groups,
        in_specs=[HBM] * groups + [VM, smem] + [HBM] * len(sources),
        out_specs=(VM, VM, HBM),
        scratch_shapes=[
            pltpu.VMEM((groups, span, model), BF),
            pltpu.VMEM((width, model), BF),
            sems,
            pltpu.SemaphoreType.DMA((groups,)),
        ],
    )(*[in_peer_order(x) for x in xs], gain_x, place, *sources)

    tile = lambda col: pl.BlockSpec((span, LANES), lambda r, p: (r, col + p))
    per_row = lambda cols_, col: pl.BlockSpec((span, cols_), lambda r, p: (r, col))
    fixed = lambda shape: pl.BlockSpec(shape, lambda r, p: (0, 0))
    pair_cols = pl.BlockSpec((8, LANES), lambda r, p: (0, p))
    seg_spec = pl.BlockSpec((8, span), lambda r, p: (r, 0))
    shared_spec = per_row(padded, 2 * inner // padded)
    scan_flops = 4 * whole * span * inner
    joint = 3 if pairs % 3 == 0 else 1
    broad = lambda col: pl.BlockSpec((span, joint * LANES), lambda r, p: (r, col + p))
    side = lambda w: jax.ShapeDtypeStruct((whole, w), F32)
    flipped_spec = pl.BlockSpec((LANES, span), lambda r, p: (r, 0))
    kept_shapes = (
        side((KERNEL - 1) * LANES),
        side(span),
        side(LANES),
        side(LANES),
        jax.ShapeDtypeStruct((groups * LANES, span), F32),
        side(LANES),
        side(2 * LANES),
        side(2 * LANES),
    )
    kept_specs = (
        per_row((KERNEL - 1) * LANES, 0),
        per_row(span, 0),
        per_row(LANES, 0),
        per_row(LANES, 0),
        flipped_spec,
        per_row(LANES, 0),
        per_row(2 * LANES, 0),
        per_row(2 * LANES, 0),
    )
    scanned, totals, gated, squares, *kept = call(
        partial(forward_kernel, per),
        (
            side(inner),
            side(inner),
            jax.ShapeDtypeStruct((whole, inner), BF),
            jax.ShapeDtypeStruct((8 * groups, span), F32),
        )
        + kept_shapes,
        8 * scan_flops,
        20 * whole * inner,
        mib=12,
        grid=(groups, pairs // joint),
        in_specs=[
            smem,
            broad(0),
            broad(pairs // joint),
            shared_spec,
            seg_spec,
            fixed((8, conv - full)),
            pl.BlockSpec((8, joint * LANES), lambda r, p: (0, p)),
            fixed((8, LANES)),
        ],
        out_specs=(broad(0), broad(0), broad(0), seg_spec) + kept_specs,
        scratch_shapes=[pltpu.VMEM((span, span), F32), pltpu.VMEM((span, LANES), F32)],
    )(place, projected, projected, projected, segs, taps_s, taps_v, heads)

    proj_flops = 2 * whole * inner * model
    dm, sums = call(
        partial(mixgrad_kernel, groups),
        (jax.ShapeDtypeStruct((whole, inner), F32), jax.ShapeDtypeStruct((8 * groups, span), F32)),
        proj_flops,
        2 * whole * model + 6 * whole * inner + 2 * inner * model,
        in_specs=[HBM] * groups + [VM] * 3,
        out_specs=(VM, VM),
        scratch_shapes=[pltpu.VMEM((groups, span, model), BF), pltpu.SemaphoreType.DMA((groups,))],
    )(*cots, out_weight, gated, squares)
    sums_all = [sums] + [swap(sums, FS, k) for k in range(1, groups)]

    outs = call(
        partial(outproj_kernel, groups),
        tuple(jax.ShapeDtypeStruct((span, model), BF if k else F32) for k in range(groups)),
        proj_flops,
        2 * whole * model + 2 * whole * inner + 2 * inner * model,
        in_specs=[VM, VM],
        out_specs=(VM,) * groups,
    )(gated, out_weight)
    outs = [outs[0]] + [swap(outs[k], FS, k) for k in range(1, groups)]

    row_spec = lambda cols_, col=0: pl.BlockSpec((span, cols_), lambda r: (r, col))
    gz, ds, mixed, gate_sum = call(
        partial(gatebwd_kernel, groups, float(full)),
        (
            jax.ShapeDtypeStruct((whole, inner), BF),
            jax.ShapeDtypeStruct((whole, inner), F32),
            jax.ShapeDtypeStruct((whole, inner), BF),
            jax.ShapeDtypeStruct((8, inner), F32),
        ),
        20 * whole * inner,
        20 * whole * inner,
        mib=16,
        grid=(groups,),
        in_specs=[
            pl.BlockSpec((8, span), (lambda k: lambda r: (jnp.bitwise_xor(r, k), 0))(k)) for k in range(groups)
        ]
        + [row_spec(inner), row_spec(inner), row_spec(inner), pl.BlockSpec((8, inner), lambda r: (0, 0))],
        out_specs=(
            row_spec(inner),
            row_spec(inner),
            row_spec(inner),
            pl.BlockSpec((8, inner), lambda r: (0, 0)),
        ),
    )(*sums_all, projected, scanned, dm, jnp.broadcast_to(gate_gain.astype(F32).reshape(1, inner), (8, inner)))

    z_sum = core_sum(weightgrad(place, [gz], [normed], (inner // 2,)))
    o_sum = core_sum(weightgrad(place, [mixed], cots, (inner // 2,)))
    out_part = line_sum(o_sum)
    z_part = line_sum(jnp.concatenate(to_owners(z_sum, groups), axis=0))

    third = pairs // 3
    cuts = (0, third, 2 * third, pairs)
    split = cuts[2]
    carry_shapes = (side(span), side(LANES), side(LANES))
    carry_specs = (per_row(span, 0), per_row(LANES, 0), per_row(LANES, 0))

    def backward(n, carry):
        first, count, last = cuts[n], cuts[n + 1] - cuts[n], n == 2
        cols_ = count * LANES
        outs_ = (jax.ShapeDtypeStruct((whole, cols_), BF), jax.ShapeDtypeStruct((8, cols_), F32))
        specs_ = (tile(0), fixed((8, cols_)))
        scratch, more, more_specs = [], [], []
        if last:
            outs_ += (jax.ShapeDtypeStruct((whole, padded), BF), jax.ShapeDtypeStruct((8, padded), F32))
            specs_ += (per_row(padded, 0), fixed((8, padded)))
            scratch = [
                pltpu.VMEM((span, span), F32),
                pltpu.VMEM((span, LANES), F32),
                pltpu.VMEM((span, LANES), F32),
            ]
            more = [projected, kept[5], kept[6], kept[7], segs, taps_s, heads, place]
            more_specs = [shared_spec, kept_specs[5], kept_specs[6], kept_specs[7], seg_spec]
            more_specs += [fixed((8, conv - full)), fixed((8, LANES)), smem]
        else:
            outs_ += carry_shapes
            specs_ += carry_specs
        return call(
            partial(backward_kernel, per, first, last, len(carry) > 0),
            outs_,
            16 * scan_flops * count // pairs,
            24 * whole * cols_,
            mib=48 if last else 12,
            grid=(groups, count),
            in_specs=[tile(first), tile(pairs + first), tile(first), tile(first)]
            + list(kept_specs[:5])
            + [pl.BlockSpec((8, LANES), lambda r, p: (0, first + p))]
            + (list(carry_specs) if carry else [])
            + more_specs,
            out_specs=specs_,
            scratch_shapes=scratch,
        )(ds, projected, totals, scanned, *kept[:5], taps_v, *carry, *more)

    gva, vsum1, *handed = backward(0, ())
    gvb, vsum2, *handed = backward(1, handed)
    v1_sum = core_sum(weightgrad(place, [gva, gvb], [normed], (third * HEADDIM, third * HEADDIM)))
    gv2, vsum3, gs, ssum = backward(2, handed)
    vsum = jnp.concatenate([vsum1, vsum2, vsum3], axis=1)

    backs = call(
        partial(normgrad_kernel, groups),
        tuple(jax.ShapeDtypeStruct((span, model), BF if k else F32) for k in range(groups)),
        2 * whole * width * model,
        2 * whole * model + 2 * whole * width + 2 * width * model,
        in_specs=[VM] * 6,
        out_specs=(VM,) * groups,
    )(gz, gva, gvb, gv2, gs, weight)
    backs = [backs[0]] + [swap(backs[k], FS, k) for k in range(1, groups)]

    v1_part = line_sum(jnp.concatenate(to_owners(v1_sum, groups), axis=0))
    deep = (pairs - split) * HEADDIM
    s_sum = core_sum(weightgrad(place, [gv2, gs], [normed], (deep, padded // 2)))
    terms = to_owners(s_sum, groups)
    shared_sum = terms[0][deep:].astype(F32)
    for term in terms[1:]:
        shared_sum = shared_sum + term[deep:].astype(F32)
    s_part = line_sum(jnp.concatenate([t[:deep] for t in terms] + [shared_sum.astype(BF)], axis=0))

    whole_spec = lambda shape: pl.BlockSpec(shape, lambda i: (0,) * len(shape))
    output, tokens_grad, norm_sum = call(
        partial(final_kernel, groups, aligned, float(full)),
        (
            jax.ShapeDtypeStruct((span, model), BF),
            jax.ShapeDtypeStruct((span, model), BF),
            jax.ShapeDtypeStruct((8, model), F32),
        ),
        30 * span * model,
        24 * span * model,
        grid=(1,),
        in_specs=[whole_spec((span, model))] * (2 * groups)
        + [pl.BlockSpec((8, span), (lambda k: lambda i: (k, 0))(k)) for k in range(groups)]
        + [smem]
        + [whole_spec((span, model))] * 3
        + [whole_spec((1, model))],
        out_specs=(whole_spec((span, model)), whole_spec((span, model)), whole_spec((8, model))),
    )(*outs, *backs, *sums_all, place, tokens, in_peer_order(tokens), in_peer_order(cotangent), gain_x)
    tokens_grad = in_peer_order(tokens_grad)
    norm_sum = jnp.take(norm_sum[0].reshape(groups, rows), order, axis=0).reshape(1, model)

    def returned(part):
        return [part, swap(part, REP, 1)]

    grad_outproj = place_rows(place, 1, out_weight.shape, ((((inner // 2, 0),), 0, None),), returned(out_part))
    early = returned(z_part) + returned(v1_part)
    gin = place_rows(
        place,
        groups,
        weight_t.shape,
        (
            (((inner // 2, 0),), inner, None),
            (((third * HEADDIM, full), (third * HEADDIM, full + third * 2 * HEADDIM)), inner, None),
        ),
        early,
    )
    grad_inproj = place_rows(
        place,
        groups,
        weight_t.shape,
        ((((deep, full + split * 2 * HEADDIM),), inner, (2 * full, tail)),),
        returned(s_part),
        gin,
    ).T

    own_cols = lambda v: lax.dynamic_update_slice_in_dim(
        jnp.zeros((v.shape[0], full), F32), v, member * inner, 1
    )
    own_spot = lambda v: lax.dynamic_update_slice_in_dim(jnp.zeros((HEADS,), F32), v, member * per, 0)
    taps_grad = jnp.concatenate([own_cols(vsum[: KERNEL + 1]), ssum[: KERNEL + 1, : conv - full]], axis=1)
    head_grads = [
        own_spot(ssum[0, 2 * LANES : 2 * LANES + per]),
        own_spot(ssum[1, 2 * LANES : 2 * LANES + per]),
        own_spot(vsum[KERNEL + 1].reshape(per, HEADDIM).sum(axis=1)),
    ]
    flat = jnp.concatenate(
        [norm_sum[0], taps_grad.reshape(-1), own_cols(gate_sum[:1]).reshape(-1)] + head_grads
    )
    length = flat.shape[0]
    flat = jnp.pad(flat, (0, -length % 1024)).reshape(-1, LANES)
    flat = all_sum(flat).reshape(-1)
    at = 0
    grad_norm = lax.dynamic_slice_in_dim(flat, member * rows, rows, 0)
    at += model
    taps_all = flat[at : at + (KERNEL + 1) * conv].reshape(KERNEL + 1, conv)
    taps_own = lax.dynamic_slice_in_dim(taps_all, member * cols, cols, 1)
    at += (KERNEL + 1) * conv
    grad_gate = lax.dynamic_slice_in_dim(flat, at + member * inner, inner, 0)
    at += full
    return (
        output,
        tokens_grad,
        grad_norm,
        grad_inproj,
        taps_own[:KERNEL],
        taps_own[KERNEL],
        flat[at : at + HEADS],
        flat[at + HEADS : at + 2 * HEADS],
        flat[at + 2 * HEADS : at + 3 * HEADS],
        grad_gate,
        grad_outproj,
    )


def solution(mesh):
    rows = P((REP, FS), None)
    in_specs = (
        rows,
        rows,
        rows,
        P(FS),
        P(FS, None),
        P(None, FS),
        P(FS),
        P(),
        P(),
        P(),
        P(FS),
        P(FS, None),
    )
    out_specs = (
        rows,
        rows,
        P(FS),
        P(FS, None),
        P(None, FS),
        P(FS),
        P(),
        P(),
        P(),
        P(FS),
        P(FS, None),
    )

    return jax.shard_map(body, mesh=mesh, in_specs=in_specs, out_specs=out_specs, check_vma=False)
```
